128 devices in a mesh: pipe: 2 (over x_hi), tensor: 4 (over z), dp: 16 (over x_lo, y, core).
Axes of the slice: x: 4 (x_hi: 2, x_lo: 2; x = x_hi * 2 + x_lo), y: 4, z: 4, core: 2. Of those that a mesh axis runs over, the one named last changes fastest.
Arguments:
- tokens: bfloat16 [8192, 1024], P('dp', 'tensor'), may hold values from -6 to 6
- lengths: int32 [64, 4], P('dp'), may hold values from 1 to 85, 128 in all within a row
- ln_gain: bfloat16 [2, 2, 1024], P('pipe'), may hold values from 0.099609375 to 1.8984375
- ln_bias: bfloat16 [2, 2, 1024], P('pipe'), may hold values from -3 to 3
- joined_weight: bfloat16 [2, 1024, 3, 1024], P('pipe', None, None, 'tensor'), may hold values from -0.1875 to 0.1875
- joined_bias: bfloat16 [2, 3, 1024], P('pipe', None, 'tensor'), may hold values from -3 to 3
- dense_weight: bfloat16 [2, 1024, 1024], P('pipe', 'tensor'), may hold values from -0.5 to 0.5
- up_weight: bfloat16 [2, 1024, 4096], P('pipe', None, 'tensor'), may hold values from -0.1875 to 0.1875
- up_bias: bfloat16 [2, 4096], P('pipe', 'tensor'), may hold values from -3 to 3
- down_weight: bfloat16 [2, 4096, 1024], P('pipe', 'tensor'), may hold values from -0.09375 to 0.09375
- output_bias: bfloat16 [2, 2, 1024], P('pipe'), may hold values from -3 to 3
- cotangent: bfloat16 [8192, 1024], P('dp', 'tensor'), may hold values from -6 to 6
Outputs:
- section_out: bfloat16 [2, 8192, 1024], P('pipe', 'dp', 'tensor')
- input_grad: bfloat16 [2, 8192, 1024], P('pipe', 'dp', 'tensor')
- grad_ln_gain: float32 [2, 2, 1024], P('pipe')
- grad_ln_bias: float32 [2, 2, 1024], P('pipe')
- grad_joined: float32 [2, 1024, 3, 1024], P('pipe', None, None, 'tensor')
- grad_joined_bias: float32 [2, 3, 1024], P('pipe', None, 'tensor')
- grad_dense: float32 [2, 1024, 1024], P('pipe', 'tensor')
- grad_up: float32 [2, 1024, 4096], P('pipe', None, 'tensor')
- grad_up_bias: float32 [2, 4096], P('pipe', 'tensor')
- grad_down: float32 [2, 4096, 1024], P('pipe', 'tensor')
- grad_output_bias: float32 [2, 2, 1024], P('pipe')
The draws below stay inside these ranges and needn't reach their ends.
Inputs may be any that keep to these rules, and one draw needn't show every extreme that they name: Row b gives, in order, the lengths of the 4 sequences that fill block b (tokens b * 128 to (b + 1) * 128 - 1); every row sums to 128.
All inputs are finite; a program needn't handle non-finite values.
Results may differ from the reference program's by a relative error of at most 0.035.
Values may be sent and summed in bfloat16 or wider, within the bound.
No kernel may reach another device: no remote copies, remote signals or barrier semaphores. Data moves between devices by JAX's collectives and lax.ppermute only.
A program may use at most 192 MiB of HBM per device.

```python
import math
import jax
import jax.numpy as jnp
import numpy as np
from jax import lax

D = 1024
HEADS = 16
HD = 64
ROT = 16
FF = 4096
MB = 128
NSEQ = 4
LONGEST = 85
TOKENS = 8192
BLOCKS = 64


def levels(key, shape, cuts, least, largest):
    loudness, own = 1.0, jax.random.fold_in(key, 6)
    for dim, blocks in cuts:
        heights = jnp.exp(jax.random.uniform(jax.random.fold_in(own, dim), (blocks,), jnp.float32, least / len(cuts), largest / len(cuts)))
        loudness = loudness * jnp.repeat(heights, shape[dim] // blocks).reshape([-1 if axis == dim else 1 for axis in range(len(shape))])
    return loudness


def split_up(amount, total, bound, slope):
    loads = [(1 << 20) // math.isqrt(rank ** slope) + 1 for rank in range(2, amount + 1)]
    surplus, counts = total - bound - (amount - 1), [1] * (amount - 1)
    while surplus > 0:
        candidates = [i for i in range(amount - 1) if counts[i] < bound]
        whole, remaining = sum([loads[i] for i in candidates]), surplus
        for i in candidates:
            addition = min(bound - counts[i], max(1, remaining * loads[i] // whole), surplus)
            counts[i] = counts[i] + addition
            surplus = surplus - addition
    return np.array([bound] + counts)


def uneven_parts(stream_key, number_of, total, limit, lean):
    if number_of == 2:
        one = jax.random.randint(stream_key, (), max(1, total - limit), min(limit, total - 1) + 1)
        return jnp.stack([one, total - one])
    tallies = jnp.asarray(split_up(number_of, total, limit, lean), jnp.int32)
    twos = (number_of - 1) // 2
    donor, taker = tallies[1:1 + 2 * twos:2], tallies[2:2 + 2 * twos:2]
    room = jnp.minimum(donor - 1, limit - taker)
    moved = jax.random.randint(jax.random.fold_in(stream_key, 1), (twos,), 0, 1 << 20) % (room + 1)
    tallies = tallies.at[1:1 + 2 * twos:2].set(donor - moved).at[2:2 + 2 * twos:2].set(taker + moved)
    return tallies[jax.random.permutation(jax.random.fold_in(stream_key, 2), number_of)]


def normal_values(own_key, dims, width, reach, cuts=(), held_as=jnp.bfloat16):
    entries = width * jax.random.normal(own_key, dims, jnp.float32)
    if cuts:
        entries = entries * levels(own_key, dims, cuts, -0.22, 0.18)
    return jnp.clip(entries, -reach, reach).astype(held_as)


def setup_inputs(seed: int = 0) -> dict:
    keys = jax.random.split(jax.random.key(seed), 13)
    return {
        "tokens": normal_values(keys[0], (TOKENS, D), 1.0, 6.0, ((0, 16), (1, 4))),
        "lengths": jax.vmap(lambda own: uneven_parts(own, NSEQ, MB, LONGEST, 2))(jax.random.split(keys[1], BLOCKS)).reshape((BLOCKS, NSEQ)).astype(jnp.int32),
        "ln_gain": jnp.clip(1.0 + 0.18 * jax.random.normal(keys[2], (2, 2, D), jnp.float32), 0.099609375, 1.8984375).astype(jnp.bfloat16),
        "ln_bias": normal_values(keys[3], (2, 2, D), 0.5, 3.0, ((0, 2),)),
        "joined_weight": normal_values(keys[4], (2, D, 3, D), D ** -0.5, 0.1875, ((0, 2), (3, 4))),
        "joined_bias": normal_values(keys[5], (2, 3, D), 0.5, 3.0, ((0, 2), (2, 4))),
        "dense_weight": normal_values(keys[6], (2, D, D), (D // 8) ** -0.5, 0.5, ((0, 2), (1, 4))),
        "up_weight": normal_values(keys[7], (2, D, FF), D ** -0.5, 0.1875, ((0, 2), (2, 4))),
        "up_bias": normal_values(keys[8], (2, FF), 0.5, 3.0, ((0, 2), (1, 4))),
        "down_weight": normal_values(keys[9], (2, FF, D), FF ** -0.5, 0.09375, ((0, 2), (1, 4))),
        "output_bias": normal_values(keys[10], (2, 2, D), 0.5, 3.0, ((0, 2),)),
        "cotangent": normal_values(keys[11], (TOKENS, D), 1.0, 6.0, ((0, 16), (1, 4))),
    }


PRECISE = lax.Precision.HIGHEST
EPSILON = 1e-05
MASKED = -1e+30

@jax.custom_vjp
def low(v):
    return lax.optimization_barrier(v.astype(jnp.bfloat16)).astype(jnp.float32)

@jax.custom_vjp
def low_back(v):
    return v

def low_keep(v):
    return (low(v), None)

def low_pass(kept, grad):
    return (grad,)

def back_keep(v):
    return (v, None)

def back_low(kept, grad):
    return (low(grad),)
low.defvjp(low_keep, low_pass)
low_back.defvjp(back_keep, back_low)

def positions(lengths, block_rows):
    seq_count = lengths.shape[1]
    counter = jnp.arange(seq_count, dtype=jnp.int32)
    lower_tri = (counter[:, None] >= counter[None, :]).astype(jnp.int32)
    seg_ends = lax.optimization_barrier(jnp.sum(lengths[:, None, :] * lower_tri[None, :, :], axis=2)).astype(jnp.int32)
    starts = seg_ends - lengths
    row_index = jnp.arange(block_rows, dtype=jnp.int32)
    segment = lax.optimization_barrier(jnp.sum((row_index[None, :, None] >= seg_ends[:, None, :]).astype(jnp.int32), axis=2)).astype(jnp.int32)
    member = (segment[:, :, None] == counter[None, None, :]).astype(jnp.int32)
    place = row_index[None, :] - lax.optimization_barrier(jnp.sum(member * starts[:, None, :], axis=2)).astype(jnp.int32)
    return (segment, place)

def rotary(place):
    half_rot = ROT // 2
    inv_freq = jnp.power(10000.0, -2.0 * jnp.arange(half_rot, dtype=jnp.float32) / ROT)
    angles = place.astype(jnp.float32)[..., None] * inv_freq
    return (jnp.cos(angles), jnp.sin(angles))

def rotate(heads_in, cosv, sinv):
    half_rot = ROT // 2
    first_half = heads_in[..., :half_rot]
    second_half = heads_in[..., half_rot:ROT]
    cos_rows = cosv[:, None, :]
    sin_rows = sinv[:, None, :]
    return jnp.concatenate([first_half * cos_rows - second_half * sin_rows, second_half * cos_rows + first_half * sin_rows, heads_in[..., ROT:]], axis=-1)

def attend(blocks_in):
    queries, keys_rot, values, segment = blocks_in
    row_index = jnp.arange(MB, dtype=jnp.int32)
    allowed = (segment[:, None] == segment[None, :]) & (row_index[None, :] <= row_index[:, None])
    scores = jnp.einsum('qhd,khd->hqk', queries, keys_rot, precision=PRECISE) * HD ** (-0.5)
    scores = low_back(scores)
    scores = jnp.where(allowed[None], scores, MASKED)
    row_top = lax.optimization_barrier(jnp.max(scores, axis=2, keepdims=True))
    exponent = jnp.exp(scores - row_top)
    weights_soft = low(exponent / lax.optimization_barrier(jnp.sum(exponent, axis=2, keepdims=True)))
    return jnp.einsum('hqk,khd->qhd', weights_soft, values, precision=PRECISE)

def residual_block(inputs, ln_gains, ln_shifts, joined_weight, joined_bias, dense_weight, up_weight, up_bias, down_weight, output_bias, segment, cosv, sinv):
    row_mean = lax.optimization_barrier(jnp.mean(inputs, axis=1, keepdims=True))
    centred = inputs - row_mean
    inv_scale = lax.rsqrt(lax.optimization_barrier(jnp.mean(centred * centred, axis=1, keepdims=True)) + EPSILON)
    normed = centred * inv_scale
    h_attn = low(normed * ln_gains[0] + ln_shifts[0])
    h_mlp = low(normed * ln_gains[1] + ln_shifts[1])
    joined_proj = jnp.dot(h_attn, joined_weight.reshape(D, 3 * D), precision=PRECISE) + joined_bias.reshape(3 * D)
    queries = low(rotate(low_back(joined_proj[:, :D]).reshape(TOKENS, HEADS, HD), cosv, sinv))
    keys_rot = low(rotate(low_back(joined_proj[:, D:2 * D]).reshape(TOKENS, HEADS, HD), cosv, sinv))
    values = low(low_back(joined_proj[:, 2 * D:])).reshape(TOKENS, HEADS, HD)
    blocks_in = (queries.reshape(BLOCKS, MB, HEADS, HD), keys_rot.reshape(BLOCKS, MB, HEADS, HD), values.reshape(BLOCKS, MB, HEADS, HD), segment)
    context = lax.map(jax.checkpoint(attend), blocks_in).reshape(TOKENS, D)
    context = low(low_back(context))
    up_proj = low_back(jnp.dot(h_mlp, up_weight, precision=PRECISE) + up_bias)
    activated = low(jax.nn.gelu(up_proj, approximate=False))
    attn_branch = jnp.dot(context, dense_weight, precision=PRECISE) + output_bias[0]
    mlp_branch = jnp.dot(activated, down_weight, precision=PRECISE) + output_bias[1]
    return inputs + attn_branch + mlp_branch

def reference(tokens, lengths, ln_gain, ln_bias, joined_weight, joined_bias, dense_weight, up_weight, up_bias, down_weight, output_bias, cotangent):
    segment, place = positions(lengths, MB)
    cosv, sinv = rotary(place.reshape(TOKENS))
    params = (ln_gain.astype(jnp.float32), ln_bias.astype(jnp.float32), joined_weight.astype(jnp.float32), joined_bias.astype(jnp.float32), dense_weight.astype(jnp.float32), up_weight.astype(jnp.float32), up_bias.astype(jnp.float32), down_weight.astype(jnp.float32), output_bias.astype(jnp.float32))

    def forward(inputs, probe_zero, gains, shifts, joined_w, joined_b, dense_w, up_w, up_b, down_w, out_b):
        first_out = residual_block(inputs, gains[0], shifts[0], joined_w[0], joined_b[0], dense_w[0], up_w[0], up_b[0], down_w[0], out_b[0], segment, cosv, sinv)
        second_in = low(low_back(first_out)) + probe_zero
        second_out = residual_block(second_in, gains[1], shifts[1], joined_w[1], joined_b[1], dense_w[1], up_w[1], up_b[1], down_w[1], out_b[1], segment, cosv, sinv)
        return (first_out, second_out)
    inputs = tokens.astype(jnp.float32)
    probe_zero = jnp.zeros((TOKENS, D), jnp.float32)
    (first_out, second_out), pullback = jax.vjp(forward, inputs, probe_zero, *params)
    gradients = pullback((jnp.zeros_like(first_out), cotangent.astype(jnp.float32)))
    section_out = jnp.stack([first_out.astype(jnp.bfloat16), second_out.astype(jnp.bfloat16)])
    input_grad = jnp.stack([gradients[0].astype(jnp.bfloat16), gradients[1].astype(jnp.bfloat16)])
    return (section_out, input_grad, gradients[2], gradients[3], gradients[4], gradients[5], gradients[6], gradients[7], gradients[8], gradients[9], gradients[10])
```

```python
import jax
import jax.numpy as jnp
from jax import lax
from jax.sharding import PartitionSpec as P

HD = 64
ROT = 16
MB = 128
NMB = 4


EPSILON = 1e-05
MASKED = -1e30


def passed_along(x, axis, by):
    peers = lax.axis_size(axis)
    pairs = [(i, i + by) for i in range(peers) if 0 <= i + by < peers]
    return lax.ppermute(x, axis, pairs)


def as_sent(x):
    return jax.tree.map(lambda a: a.astype(jnp.bfloat16) if a.dtype == jnp.float32 else a, x)


def positions(lengths, block_rows):
    seq_count = lengths.shape[1]
    counter = jnp.arange(seq_count, dtype=jnp.int32)
    lower_tri = (counter[:, None] >= counter[None, :]).astype(jnp.int32)
    seg_ends = jnp.sum(lengths[:, None, :] * lower_tri[None, :, :], axis=2)
    starts = seg_ends - lengths
    row_index = jnp.arange(block_rows, dtype=jnp.int32)
    segment = jnp.sum((row_index[None, :, None] >= seg_ends[:, None, :]).astype(jnp.int32), axis=2)
    member = (segment[:, :, None] == counter[None, None, :]).astype(jnp.int32)
    place = row_index[None, :] - jnp.sum(member * starts[:, None, :], axis=2)
    return (segment, place)


def rotary(place):
    half_rot = ROT // 2
    inv_freq = jnp.power(10000.0, -2.0 * jnp.arange(half_rot, dtype=jnp.float32) / ROT)
    angles = place.astype(jnp.float32)[..., None] * inv_freq
    return (jnp.cos(angles), jnp.sin(angles))


def rotate(heads_in, cosv, sinv):
    half_rot = ROT // 2
    first_half = heads_in[..., :half_rot]
    second_half = heads_in[..., half_rot:ROT]
    cos_rows = cosv[:, None, :]
    sin_rows = sinv[:, None, :]
    return jnp.concatenate(
        [
            first_half * cos_rows - second_half * sin_rows,
            second_half * cos_rows + first_half * sin_rows,
            heads_in[..., ROT:],
        ],
        axis=-1,
    )


def rotate_back(heads_in, cosv, sinv):
    half_rot = ROT // 2
    first_half = heads_in[..., :half_rot]
    second_half = heads_in[..., half_rot:ROT]
    cos_rows = cosv[:, None, :]
    sin_rows = sinv[:, None, :]
    return jnp.concatenate(
        [
            first_half * cos_rows + second_half * sin_rows,
            second_half * cos_rows - first_half * sin_rows,
            heads_in[..., ROT:],
        ],
        axis=-1,
    )


def exact_gelu(values):
    return jax.nn.gelu(values, approximate=False)


def allowed_keys(segment):
    row_index = jnp.arange(segment.shape[0], dtype=jnp.int32)
    return (segment[:, None] == segment[None, :]) & (row_index[None, :] <= row_index[:, None])


def contract_rows(left, right):
    return lax.dot_general(
        left, right, (((0,), (0,)), ((), ())), preferred_element_type=jnp.float32
    )


def contract_cols(left, right):
    return lax.dot_general(
        left, right, (((1,), (1,)), ((), ())), preferred_element_type=jnp.float32
    )


def per_device(
    tokens,
    lengths,
    ln_gain,
    ln_bias,
    joined_weight,
    joined_bias,
    dense_weight,
    up_weight,
    up_bias,
    down_weight,
    output_bias,
    cotangent,
):
    leading = lax.axis_index("pipe") == 0
    model_width = joined_weight.shape[1]
    local_width = joined_weight.shape[3]
    local_heads = local_width // HD
    hidden_local = up_weight.shape[2]
    quarter = tokens.shape[1]
    score_scale = HD ** (-0.5)
    ln_gains = ln_gain[0].astype(jnp.float32)
    ln_shifts = ln_bias[0].astype(jnp.float32)
    joined_mat = joined_weight[0].reshape(model_width, 3 * local_width)
    joined_add = joined_bias[0].astype(jnp.float32).reshape(3 * local_width)
    dense_mat = dense_weight[0]
    up_mat = up_weight[0]
    up_add = up_bias[0].astype(jnp.float32)
    down_mat = down_weight[0]
    bias_sum = output_bias[0, 0].astype(jnp.float32) + output_bias[0, 1].astype(jnp.float32)
    gathered_rows = lax.all_gather(
        jnp.concatenate([tokens, cotangent], axis=0), "tensor", axis=1, tiled=True
    )
    input_rows = gathered_rows[: tokens.shape[0]]
    output_grads = gathered_rows[tokens.shape[0] :]
    segment_all, place_all = positions(lengths, MB)
    cos_all, sin_all = rotary(place_all)

    def pick(early_val, late_val):
        return jax.tree.map(
            lambda upper_val, lower_val: jnp.where(leading, upper_val, lower_val),
            early_val,
            late_val,
        )

    received = jnp.zeros((MB, model_width), jnp.bfloat16)
    tick_outputs = []
    tick_stored = []
    for section_tick in range(NMB + 1):
        early_block = min(section_tick, NMB - 1)
        late_block = max(section_tick - 1, 0)
        block_rows = jnp.where(
            leading, input_rows[early_block * MB : (early_block + 1) * MB], received
        )
        segment, cosv, sinv = pick(
            (segment_all[early_block], cos_all[early_block], sin_all[early_block]),
            (segment_all[late_block], cos_all[late_block], sin_all[late_block]),
        )
        inputs = block_rows.astype(jnp.float32)
        row_mean = jnp.mean(inputs, axis=1, keepdims=True)
        centred = inputs - row_mean
        forward_inv_scale = lax.rsqrt(jnp.mean(centred * centred, axis=1, keepdims=True) + EPSILON)
        forward_normed = centred * forward_inv_scale
        forward_h_attn = (forward_normed * ln_gains[0] + ln_shifts[0]).astype(jnp.bfloat16)
        forward_h_mlp = (forward_normed * ln_gains[1] + ln_shifts[1]).astype(jnp.bfloat16)
        joined_proj = (
            jnp.dot(forward_h_attn, joined_mat, preferred_element_type=jnp.float32) + joined_add
        )
        forward_block_len = block_rows.shape[0]
        forward_queries = rotate(
            joined_proj[:, :local_width].reshape(forward_block_len, local_heads, HD), cosv, sinv
        ).astype(jnp.bfloat16)
        forward_keys_rot = rotate(
            joined_proj[:, local_width : 2 * local_width].reshape(
                forward_block_len, local_heads, HD
            ),
            cosv,
            sinv,
        ).astype(jnp.bfloat16)
        forward_values = (
            joined_proj[:, 2 * local_width :]
            .reshape(forward_block_len, local_heads, HD)
            .astype(jnp.bfloat16)
        )
        forward_scores = (
            jnp.einsum(
                "qhd,khd->hqk",
                forward_queries,
                forward_keys_rot,
                preferred_element_type=jnp.float32,
            )
            * score_scale
        )
        forward_scores = jnp.where(allowed_keys(segment)[None], forward_scores, MASKED)
        row_top = jnp.max(forward_scores, axis=2, keepdims=True)
        exponent = jnp.exp(forward_scores - row_top)
        row_total = jnp.sum(exponent, axis=2, keepdims=True)
        forward_log_total = row_top + jnp.log(row_total)
        weights_low = (exponent / row_total).astype(jnp.bfloat16)
        forward_context = jnp.einsum(
            "hqk,khd->qhd", weights_low, forward_values, preferred_element_type=jnp.float32
        )
        forward_context = forward_context.reshape(forward_block_len, local_width).astype(
            jnp.bfloat16
        )
        forward_up_proj = (
            jnp.dot(forward_h_mlp, up_mat, preferred_element_type=jnp.float32) + up_add
        )
        forward_activated = exact_gelu(forward_up_proj).astype(jnp.bfloat16)
        partial_value = jnp.dot(forward_context, dense_mat, preferred_element_type=jnp.float32)
        partial_value = partial_value + jnp.dot(
            forward_activated, down_mat, preferred_element_type=jnp.float32
        )
        branches = lax.psum(partial_value.astype(jnp.bfloat16), "tensor").astype(jnp.float32)
        result = inputs + branches + bias_sum
        forward_stored = (
            forward_normed,
            forward_inv_scale,
            forward_h_attn,
            forward_h_mlp,
            forward_queries,
            forward_keys_rot,
            forward_values,
            forward_log_total,
            forward_context,
            forward_up_proj,
            forward_activated,
        )
        result, stored = (result, forward_stored)
        result_low = result.astype(jnp.bfloat16)
        tick_outputs.append(result_low)
        tick_stored.append((stored, segment, cosv, sinv))
        if section_tick < NMB:
            received = passed_along(result_low, "pipe", 1)
    column_start = lax.axis_index("tensor") * quarter
    section_rows = jnp.concatenate(
        [jnp.where(leading, tick_outputs[block], tick_outputs[block + 1]) for block in range(NMB)],
        axis=0,
    )
    section_out = lax.dynamic_slice_in_dim(section_rows, column_start, quarter, 1)[None]
    returned = jnp.zeros((MB, model_width), jnp.bfloat16)
    tick_grads = []
    totals = None
    for section_tick in range(NMB + 1):
        own_block = min(section_tick, NMB - 1)
        late_tick = max(section_tick - 1, 0)
        upper_tick = min(section_tick + 1, NMB)
        from_output = output_grads[own_block * MB : (own_block + 1) * MB]
        if section_tick == NMB:
            from_output = jnp.zeros_like(from_output)
        grad_rows = jnp.where(leading, returned, from_output)
        stored, segment, cosv, sinv = pick(tick_stored[late_tick], tick_stored[upper_tick])
        (
            normed,
            inv_scale,
            h_attn,
            h_mlp,
            queries,
            keys_rot,
            values,
            log_total,
            context,
            up_proj,
            activated,
        ) = stored
        block_len = grad_rows.shape[0]
        grad_wide = grad_rows.astype(jnp.float32)
        column_sum = jnp.sum(grad_wide, axis=0)
        backward_grad_dense = contract_rows(context, grad_rows)
        backward_grad_down = contract_rows(activated, grad_rows)
        d_context = contract_cols(grad_rows, dense_mat).astype(jnp.bfloat16)
        d_act = contract_cols(grad_rows, down_mat)
        unused, slope_back = jax.vjp(exact_gelu, up_proj)
        d_up = slope_back(d_act)[0].astype(jnp.bfloat16)
        grad_up_add = jnp.sum(d_up.astype(jnp.float32), axis=0)
        backward_grad_up = contract_rows(h_mlp, d_up)
        d_hmlp = contract_cols(d_up, up_mat)
        scores = (
            jnp.einsum("qhd,khd->hqk", queries, keys_rot, preferred_element_type=jnp.float32)
            * score_scale
        )
        scores = jnp.where(allowed_keys(segment)[None], scores, MASKED)
        weights_soft = jnp.exp(scores - log_total)
        d_context3 = d_context.reshape(block_len, local_heads, HD)
        d_values = jnp.einsum(
            "hqk,qhd->khd",
            weights_soft.astype(jnp.bfloat16),
            d_context3,
            preferred_element_type=jnp.float32,
        ).astype(jnp.bfloat16)
        d_weights = jnp.einsum(
            "qhd,khd->hqk", d_context3, values, preferred_element_type=jnp.float32
        )
        row_delta = jnp.sum(weights_soft * d_weights, axis=2, keepdims=True)
        d_scores = (weights_soft * (d_weights - row_delta)).astype(jnp.bfloat16)
        d_queries = (
            jnp.einsum("hqk,khd->qhd", d_scores, keys_rot, preferred_element_type=jnp.float32)
            * score_scale
        )
        d_keys = (
            jnp.einsum("hqk,qhd->khd", d_scores, queries, preferred_element_type=jnp.float32)
            * score_scale
        )
        d_queries = (
            rotate_back(d_queries, cosv, sinv).reshape(block_len, local_width).astype(jnp.bfloat16)
        )
        d_keys = (
            rotate_back(d_keys, cosv, sinv).reshape(block_len, local_width).astype(jnp.bfloat16)
        )
        d_joined = jnp.concatenate(
            [d_queries, d_keys, d_values.reshape(block_len, local_width)], axis=1
        )
        grad_joined_add = jnp.sum(d_joined.astype(jnp.float32), axis=0)
        backward_grad_joined = contract_rows(d_joined, h_attn)
        d_hattn = contract_cols(d_joined, joined_mat)
        d_hattn, d_hmlp = (
            lax.psum(d_hattn.astype(jnp.bfloat16), "tensor").astype(jnp.float32),
            lax.psum(d_hmlp.astype(jnp.bfloat16), "tensor").astype(jnp.float32),
        )
        grad_gains = jnp.concatenate(
            [jnp.sum(d_hattn * normed, axis=0), jnp.sum(d_hmlp * normed, axis=0)]
        )
        grad_shifts = jnp.concatenate([jnp.sum(d_hattn, axis=0), jnp.sum(d_hmlp, axis=0)])
        d_norm = d_hattn * ln_gains[0] + d_hmlp * ln_gains[1]
        grad_input = grad_wide + inv_scale * (
            d_norm
            - jnp.mean(d_norm, axis=1, keepdims=True)
            - normed * jnp.mean(d_norm * normed, axis=1, keepdims=True)
        )
        small_terms = jnp.concatenate(
            [grad_gains, grad_shifts, column_sum, column_sum, grad_joined_add, grad_up_add]
        )
        terms = (
            backward_grad_joined[None],
            backward_grad_dense[None],
            backward_grad_up[None],
            backward_grad_down[None],
            small_terms[None],
        )
        grad_input, terms = (grad_input, terms)
        grad_low = grad_input.astype(jnp.bfloat16)
        tick_grads.append(grad_low)
        if totals is None:
            totals = terms
        else:
            totals = jax.tree.map(lambda older, newer: older + newer, totals, terms)
        if section_tick < NMB:
            returned = passed_along(grad_low, "pipe", -1)
    small_rows = totals[4][0]
    small_pad = (-small_rows.shape[0]) % model_width
    small_rows = jnp.pad(small_rows, (0, small_pad)).reshape(-1, model_width)
    pieces = (totals[0][0], totals[1][0], totals[2][0], totals[3][0], small_rows)
    slab = jnp.concatenate([piece.astype(jnp.bfloat16) for piece in pieces], axis=0)
    slab = lax.psum(slab, "dp").astype(jnp.float32)
    summed = []
    offset = 0
    for piece in pieces:
        summed.append(slab[offset : offset + piece.shape[0]])
        offset = offset + piece.shape[0]
    grad_rows_all = jnp.concatenate(
        [jnp.where(leading, tick_grads[block + 1], tick_grads[block]) for block in range(NMB)],
        axis=0,
    )
    input_grad = lax.dynamic_slice_in_dim(grad_rows_all, column_start, quarter, 1)[None]
    grad_joined = summed[0].T.reshape(1, model_width, 3, local_width)
    grad_dense = summed[1][None]
    grad_up = summed[2][None]
    grad_down = summed[3][None]
    small_sum = summed[4].reshape(-1)
    offset = 0
    grad_ln_gain = small_sum[offset : offset + 2 * model_width].reshape(1, 2, model_width)
    offset = offset + 2 * model_width
    grad_ln_bias = small_sum[offset : offset + 2 * model_width].reshape(1, 2, model_width)
    offset = offset + 2 * model_width
    grad_output_bias = small_sum[offset : offset + 2 * model_width].reshape(1, 2, model_width)
    offset = offset + 2 * model_width
    grad_joined_bias = small_sum[offset : offset + 3 * local_width].reshape(1, 3, local_width)
    offset = offset + 3 * local_width
    grad_up_bias = small_sum[offset : offset + hidden_local].reshape(1, hidden_local)
    return (
        section_out,
        input_grad,
        grad_ln_gain,
        grad_ln_bias,
        grad_joined,
        grad_joined_bias,
        grad_dense,
        grad_up,
        grad_up_bias,
        grad_down,
        grad_output_bias,
    )


def solution(mesh):
    placed = (
        P("dp", "tensor"),
        P("dp", None),
        P("pipe", None, None),
        P("pipe", None, None),
        P("pipe", None, None, "tensor"),
        P("pipe", None, "tensor"),
        P("pipe", "tensor", None),
        P("pipe", None, "tensor"),
        P("pipe", "tensor"),
        P("pipe", "tensor", None),
        P("pipe", None, None),
        P("dp", "tensor"),
    )
    return jax.shard_map(
        per_device,
        mesh=mesh,
        in_specs=placed,
        out_specs=(
            P("pipe", "dp", "tensor"),
            P("pipe", "dp", "tensor"),
            P("pipe", None, None),
            P("pipe", None, None),
            P("pipe", None, None, "tensor"),
            P("pipe", None, "tensor"),
            P("pipe", "tensor", None),
            P("pipe", None, "tensor"),
            P("pipe", "tensor"),
            P("pipe", "tensor", None),
            P("pipe", None, None),
        ),
        check_vma=False,
    )
```

```python
import jax
import jax.numpy as jnp
from jax import lax
from jax.sharding import PartitionSpec as P

HD = 64
ROT = 16
MB = 128
NMB = 4


EPSILON = 1e-05
MASKED = -1e30


def passed_along(x, axis, by):
    peers = lax.axis_size(axis)
    pairs = [(i, i + by) for i in range(peers) if 0 <= i + by < peers]
    return lax.ppermute(x, axis, pairs)


def tensor_pieces(x):
    peers = lax.axis_size("tensor")
    me = lax.axis_index("tensor")
    parts = [x]
    for shift in range(1, peers):
        pairs = [(i, (i + shift) % peers) for i in range(peers)]
        parts.append(lax.ppermute(x, "tensor", pairs))
    reverse = [parts[(-m) % peers] for m in range(peers)]
    doubled = jnp.stack(reverse + reverse)
    return lax.dynamic_slice_in_dim(doubled, peers - me, peers, 0)


def tensor_sum(x):
    pieces = tensor_pieces(x)
    total = pieces[0].astype(jnp.float32)
    for j in range(1, pieces.shape[0]):
        total = total + pieces[j].astype(jnp.float32)
    return total


def as_sent(x):
    return jax.tree.map(lambda a: a.astype(jnp.bfloat16) if a.dtype == jnp.float32 else a, x)


def positions(lengths, block_rows):
    seq_count = lengths.shape[1]
    counter = jnp.arange(seq_count, dtype=jnp.int32)
    lower_tri = (counter[:, None] >= counter[None, :]).astype(jnp.int32)
    seg_ends = jnp.sum(lengths[:, None, :] * lower_tri[None, :, :], axis=2)
    starts = seg_ends - lengths
    row_index = jnp.arange(block_rows, dtype=jnp.int32)
    segment = jnp.sum((row_index[None, :, None] >= seg_ends[:, None, :]).astype(jnp.int32), axis=2)
    member = (segment[:, :, None] == counter[None, None, :]).astype(jnp.int32)
    place = row_index[None, :] - jnp.sum(member * starts[:, None, :], axis=2)
    return (segment, place)


def rotary(place):
    half_rot = ROT // 2
    inv_freq = jnp.power(10000.0, -2.0 * jnp.arange(half_rot, dtype=jnp.float32) / ROT)
    angles = place.astype(jnp.float32)[..., None] * inv_freq
    return (jnp.cos(angles), jnp.sin(angles))


def rotate(heads_in, cosv, sinv):
    half_rot = ROT // 2
    first_half = heads_in[..., :half_rot]
    second_half = heads_in[..., half_rot:ROT]
    cos_rows = cosv[:, None, :]
    sin_rows = sinv[:, None, :]
    return jnp.concatenate(
        [
            first_half * cos_rows - second_half * sin_rows,
            second_half * cos_rows + first_half * sin_rows,
            heads_in[..., ROT:],
        ],
        axis=-1,
    )


def rotate_back(heads_in, cosv, sinv):
    half_rot = ROT // 2
    first_half = heads_in[..., :half_rot]
    second_half = heads_in[..., half_rot:ROT]
    cos_rows = cosv[:, None, :]
    sin_rows = sinv[:, None, :]
    return jnp.concatenate(
        [
            first_half * cos_rows + second_half * sin_rows,
            second_half * cos_rows - first_half * sin_rows,
            heads_in[..., ROT:],
        ],
        axis=-1,
    )


def exact_gelu(values):
    return jax.nn.gelu(values, approximate=False)


def allowed_keys(segment):
    row_index = jnp.arange(segment.shape[0], dtype=jnp.int32)
    return (segment[:, None] == segment[None, :]) & (row_index[None, :] <= row_index[:, None])


def contract_rows(left, right):
    return lax.dot_general(
        left, right, (((0,), (0,)), ((), ())), preferred_element_type=jnp.float32
    )


def contract_cols(left, right):
    return lax.dot_general(
        left, right, (((1,), (1,)), ((), ())), preferred_element_type=jnp.float32
    )


def per_device(
    tokens,
    lengths,
    ln_gain,
    ln_bias,
    joined_weight,
    joined_bias,
    dense_weight,
    up_weight,
    up_bias,
    down_weight,
    output_bias,
    cotangent,
):
    leading = lax.axis_index("pipe") == 0
    model_width = joined_weight.shape[1]
    local_width = joined_weight.shape[3]
    local_heads = local_width // HD
    hidden_local = up_weight.shape[2]
    quarter = tokens.shape[1]
    score_scale = HD ** (-0.5)
    ln_gains = ln_gain[0].astype(jnp.float32)
    ln_shifts = ln_bias[0].astype(jnp.float32)
    joined_mat = joined_weight[0].reshape(model_width, 3 * local_width)
    joined_add = joined_bias[0].astype(jnp.float32).reshape(3 * local_width)
    dense_mat = dense_weight[0]
    up_mat = up_weight[0]
    up_add = up_bias[0].astype(jnp.float32)
    down_mat = down_weight[0]
    bias_sum = output_bias[0, 0].astype(jnp.float32) + output_bias[0, 1].astype(jnp.float32)
    gathered_pieces = tensor_pieces(jnp.concatenate([tokens, cotangent], axis=0))
    gathered_rows = jnp.concatenate(
        [gathered_pieces[j] for j in range(gathered_pieces.shape[0])], axis=1
    )
    input_rows = gathered_rows[: tokens.shape[0]]
    output_grads = gathered_rows[tokens.shape[0] :]
    segment_all, place_all = positions(lengths, MB)
    cos_all, sin_all = rotary(place_all)

    def pick(early_val, late_val):
        return jax.tree.map(
            lambda upper_val, lower_val: jnp.where(leading, upper_val, lower_val),
            early_val,
            late_val,
        )

    received = jnp.zeros((MB, model_width), jnp.bfloat16)
    tick_outputs = []
    tick_stored = []
    for section_tick in range(NMB + 1):
        early_block = min(section_tick, NMB - 1)
        late_block = max(section_tick - 1, 0)
        block_rows = jnp.where(
            leading, input_rows[early_block * MB : (early_block + 1) * MB], received
        )
        segment, cosv, sinv = pick(
            (segment_all[early_block], cos_all[early_block], sin_all[early_block]),
            (segment_all[late_block], cos_all[late_block], sin_all[late_block]),
        )
        inputs = block_rows.astype(jnp.float32)
        row_mean = jnp.mean(inputs, axis=1, keepdims=True)
        centred = inputs - row_mean
        forward_inv_scale = lax.rsqrt(jnp.mean(centred * centred, axis=1, keepdims=True) + EPSILON)
        forward_normed = centred * forward_inv_scale
        forward_h_attn = (forward_normed * ln_gains[0] + ln_shifts[0]).astype(jnp.bfloat16)
        forward_h_mlp = (forward_normed * ln_gains[1] + ln_shifts[1]).astype(jnp.bfloat16)
        joined_proj = (
            jnp.dot(forward_h_attn, joined_mat, preferred_element_type=jnp.float32) + joined_add
        )
        forward_block_len = block_rows.shape[0]
        forward_queries = rotate(
            joined_proj[:, :local_width].reshape(forward_block_len, local_heads, HD), cosv, sinv
        ).astype(jnp.bfloat16)
        forward_keys_rot = rotate(
            joined_proj[:, local_width : 2 * local_width].reshape(
                forward_block_len, local_heads, HD
            ),
            cosv,
            sinv,
        ).astype(jnp.bfloat16)
        forward_values = (
            joined_proj[:, 2 * local_width :]
            .reshape(forward_block_len, local_heads, HD)
            .astype(jnp.bfloat16)
        )
        forward_scores = (
            jnp.einsum(
                "qhd,khd->hqk",
                forward_queries,
                forward_keys_rot,
                preferred_element_type=jnp.float32,
            )
            * score_scale
        )
        forward_scores = jnp.where(allowed_keys(segment)[None], forward_scores, MASKED)
        row_top = jnp.max(forward_scores, axis=2, keepdims=True)
        exponent = jnp.exp(forward_scores - row_top)
        row_total = jnp.sum(exponent, axis=2, keepdims=True)
        forward_log_total = row_top + jnp.log(row_total)
        weights_low = (exponent / row_total).astype(jnp.bfloat16)
        forward_context = jnp.einsum(
            "hqk,khd->qhd", weights_low, forward_values, preferred_element_type=jnp.float32
        )
        forward_context = forward_context.reshape(forward_block_len, local_width).astype(
            jnp.bfloat16
        )
        forward_up_proj = (
            jnp.dot(forward_h_mlp, up_mat, preferred_element_type=jnp.float32) + up_add
        )
        forward_activated = exact_gelu(forward_up_proj).astype(jnp.bfloat16)
        partial_value = jnp.dot(forward_context, dense_mat, preferred_element_type=jnp.float32)
        partial_value = partial_value + jnp.dot(
            forward_activated, down_mat, preferred_element_type=jnp.float32
        )
        branches = tensor_sum(partial_value.astype(jnp.bfloat16))
        result = inputs + branches + bias_sum
        forward_stored = (
            forward_normed,
            forward_inv_scale,
            forward_h_attn,
            forward_h_mlp,
            forward_queries,
            forward_keys_rot,
            forward_values,
            forward_log_total,
            forward_context,
            forward_up_proj,
            forward_activated,
        )
        result, stored = (result, forward_stored)
        result_low = result.astype(jnp.bfloat16)
        tick_outputs.append(result_low)
        tick_stored.append((stored, segment, cosv, sinv))
        if section_tick < NMB:
            received = passed_along(result_low, "pipe", 1)
    column_start = lax.axis_index("tensor") * quarter
    section_rows = jnp.concatenate(
        [jnp.where(leading, tick_outputs[block], tick_outputs[block + 1]) for block in range(NMB)],
        axis=0,
    )
    section_out = lax.dynamic_slice_in_dim(section_rows, column_start, quarter, 1)[None]
    returned = jnp.zeros((MB, model_width), jnp.bfloat16)
    tick_grads = []
    totals = None
    for section_tick in range(NMB + 1):
        own_block = min(section_tick, NMB - 1)
        late_tick = max(section_tick - 1, 0)
        upper_tick = min(section_tick + 1, NMB)
        from_output = output_grads[own_block * MB : (own_block + 1) * MB]
        if section_tick == NMB:
            from_output = jnp.zeros_like(from_output)
        grad_rows = jnp.where(leading, returned, from_output)
        stored, segment, cosv, sinv = pick(tick_stored[late_tick], tick_stored[upper_tick])
        (
            normed,
            inv_scale,
            h_attn,
            h_mlp,
            queries,
            keys_rot,
            values,
            log_total,
            context,
            up_proj,
            activated,
        ) = stored
        block_len = grad_rows.shape[0]
        grad_wide = grad_rows.astype(jnp.float32)
        column_sum = jnp.sum(grad_wide, axis=0)
        backward_grad_dense = contract_rows(context, grad_rows)
        backward_grad_down = contract_rows(activated, grad_rows)
        d_context = contract_cols(grad_rows, dense_mat).astype(jnp.bfloat16)
        d_act = contract_cols(grad_rows, down_mat)
        unused, slope_back = jax.vjp(exact_gelu, up_proj)
        d_up = slope_back(d_act)[0].astype(jnp.bfloat16)
        grad_up_add = jnp.sum(d_up.astype(jnp.float32), axis=0)
        backward_grad_up = contract_rows(h_mlp, d_up)
        d_hmlp = contract_cols(d_up, up_mat)
        scores = (
            jnp.einsum("qhd,khd->hqk", queries, keys_rot, preferred_element_type=jnp.float32)
            * score_scale
        )
        scores = jnp.where(allowed_keys(segment)[None], scores, MASKED)
        weights_soft = jnp.exp(scores - log_total)
        d_context3 = d_context.reshape(block_len, local_heads, HD)
        d_values = jnp.einsum(
            "hqk,qhd->khd",
            weights_soft.astype(jnp.bfloat16),
            d_context3,
            preferred_element_type=jnp.float32,
        ).astype(jnp.bfloat16)
        d_weights = jnp.einsum(
            "qhd,khd->hqk", d_context3, values, preferred_element_type=jnp.float32
        )
        row_delta = jnp.sum(weights_soft * d_weights, axis=2, keepdims=True)
        d_scores = (weights_soft * (d_weights - row_delta)).astype(jnp.bfloat16)
        d_queries = (
            jnp.einsum("hqk,khd->qhd", d_scores, keys_rot, preferred_element_type=jnp.float32)
            * score_scale
        )
        d_keys = (
            jnp.einsum("hqk,qhd->khd", d_scores, queries, preferred_element_type=jnp.float32)
            * score_scale
        )
        d_queries = (
            rotate_back(d_queries, cosv, sinv).reshape(block_len, local_width).astype(jnp.bfloat16)
        )
        d_keys = (
            rotate_back(d_keys, cosv, sinv).reshape(block_len, local_width).astype(jnp.bfloat16)
        )
        d_joined = jnp.concatenate(
            [d_queries, d_keys, d_values.reshape(block_len, local_width)], axis=1
        )
        grad_joined_add = jnp.sum(d_joined.astype(jnp.float32), axis=0)
        backward_grad_joined = contract_rows(d_joined, h_attn)
        d_hattn = contract_cols(d_joined, joined_mat)
        d_both = tensor_sum(
            jnp.concatenate([d_hattn, d_hmlp], axis=1).astype(jnp.bfloat16)
        )
        d_hattn, d_hmlp = d_both[:, :model_width], d_both[:, model_width:]
        grad_gains = jnp.concatenate(
            [jnp.sum(d_hattn * normed, axis=0), jnp.sum(d_hmlp * normed, axis=0)]
        )
        grad_shifts = jnp.concatenate([jnp.sum(d_hattn, axis=0), jnp.sum(d_hmlp, axis=0)])
        d_norm = d_hattn * ln_gains[0] + d_hmlp * ln_gains[1]
        grad_input = grad_wide + inv_scale * (
            d_norm
            - jnp.mean(d_norm, axis=1, keepdims=True)
            - normed * jnp.mean(d_norm * normed, axis=1, keepdims=True)
        )
        small_terms = jnp.concatenate(
            [grad_gains, grad_shifts, column_sum, column_sum, grad_joined_add, grad_up_add]
        )
        terms = (
            backward_grad_joined[None],
            backward_grad_dense[None],
            backward_grad_up[None],
            backward_grad_down[None],
            small_terms[None],
        )
        grad_input, terms = (grad_input, terms)
        grad_low = grad_input.astype(jnp.bfloat16)
        tick_grads.append(grad_low)
        if totals is None:
            totals = terms
        else:
            totals = jax.tree.map(lambda older, newer: older + newer, totals, terms)
        if section_tick < NMB:
            returned = passed_along(grad_low, "pipe", -1)
    small_rows = totals[4][0]
    small_pad = (-small_rows.shape[0]) % model_width
    small_rows = jnp.pad(small_rows, (0, small_pad)).reshape(-1, model_width)
    pieces = (totals[0][0], totals[1][0], totals[2][0], totals[3][0], small_rows)
    slab = jnp.concatenate([piece.astype(jnp.bfloat16) for piece in pieces], axis=0)
    slab = lax.psum(slab, "dp").astype(jnp.float32)
    summed = []
    offset = 0
    for piece in pieces:
        summed.append(slab[offset : offset + piece.shape[0]])
        offset = offset + piece.shape[0]
    grad_rows_all = jnp.concatenate(
        [jnp.where(leading, tick_grads[block + 1], tick_grads[block]) for block in range(NMB)],
        axis=0,
    )
    input_grad = lax.dynamic_slice_in_dim(grad_rows_all, column_start, quarter, 1)[None]
    grad_joined = summed[0].T.reshape(1, model_width, 3, local_width)
    grad_dense = summed[1][None]
    grad_up = summed[2][None]
    grad_down = summed[3][None]
    small_sum = summed[4].reshape(-1)
    offset = 0
    grad_ln_gain = small_sum[offset : offset + 2 * model_width].reshape(1, 2, model_width)
    offset = offset + 2 * model_width
    grad_ln_bias = small_sum[offset : offset + 2 * model_width].reshape(1, 2, model_width)
    offset = offset + 2 * model_width
    grad_output_bias = small_sum[offset : offset + 2 * model_width].reshape(1, 2, model_width)
    offset = offset + 2 * model_width
    grad_joined_bias = small_sum[offset : offset + 3 * local_width].reshape(1, 3, local_width)
    offset = offset + 3 * local_width
    grad_up_bias = small_sum[offset : offset + hidden_local].reshape(1, hidden_local)
    return (
        section_out,
        input_grad,
        grad_ln_gain,
        grad_ln_bias,
        grad_joined,
        grad_joined_bias,
        grad_dense,
        grad_up,
        grad_up_bias,
        grad_down,
        grad_output_bias,
    )


def solution(mesh):
    placed = (
        P("dp", "tensor"),
        P("dp", None),
        P("pipe", None, None),
        P("pipe", None, None),
        P("pipe", None, None, "tensor"),
        P("pipe", None, "tensor"),
        P("pipe", "tensor", None),
        P("pipe", None, "tensor"),
        P("pipe", "tensor"),
        P("pipe", "tensor", None),
        P("pipe", None, None),
        P("dp", "tensor"),
    )
    return jax.shard_map(
        per_device,
        mesh=mesh,
        in_specs=placed,
        out_specs=(
            P("pipe", "dp", "tensor"),
            P("pipe", "dp", "tensor"),
            P("pipe", None, None),
            P("pipe", None, None),
            P("pipe", None, None, "tensor"),
            P("pipe", None, "tensor"),
            P("pipe", "tensor", None),
            P("pipe", None, "tensor"),
            P("pipe", "tensor"),
            P("pipe", "tensor", None),
            P("pipe", None, None),
        ),
        check_vma=False,
    )
```

```python
import jax
import jax.numpy as jnp
from jax import lax
from jax.sharding import PartitionSpec as P

HD = 64
ROT = 16
MB = 128
NMB = 4


EPSILON = 1e-05
MASKED = -1e30


def passed_along(x, axis, by):
    peers = lax.axis_size(axis)
    pairs = [(i, i + by) for i in range(peers) if 0 <= i + by < peers]
    return lax.ppermute(x, axis, pairs)


def tensor_pieces(x):
    peers = lax.axis_size("tensor")
    me = lax.axis_index("tensor")
    parts = [x]
    for shift in range(1, peers):
        pairs = [(i, (i + shift) % peers) for i in range(peers)]
        parts.append(lax.ppermute(x, "tensor", pairs))
    ordered = []
    for owner in range(peers):
        slot = (me - owner) % peers
        chosen = parts[peers - 1]
        for k in range(peers - 2, -1, -1):
            chosen = jnp.where(slot == k, parts[k], chosen)
        ordered.append(chosen)
    return ordered


def tensor_sum(x):
    pieces = tensor_pieces(x)
    total = pieces[0].astype(jnp.float32)
    for piece in pieces[1:]:
        total = total + piece.astype(jnp.float32)
    return total

def as_sent(x):
    return jax.tree.map(lambda a: a.astype(jnp.bfloat16) if a.dtype == jnp.float32 else a, x)


def positions(lengths, block_rows):
    seq_count = lengths.shape[1]
    counter = jnp.arange(seq_count, dtype=jnp.int32)
    lower_tri = (counter[:, None] >= counter[None, :]).astype(jnp.int32)
    seg_ends = jnp.sum(lengths[:, None, :] * lower_tri[None, :, :], axis=2)
    starts = seg_ends - lengths
    row_index = jnp.arange(block_rows, dtype=jnp.int32)
    segment = jnp.sum((row_index[None, :, None] >= seg_ends[:, None, :]).astype(jnp.int32), axis=2)
    member = (segment[:, :, None] == counter[None, None, :]).astype(jnp.int32)
    place = row_index[None, :] - jnp.sum(member * starts[:, None, :], axis=2)
    return (segment, place)


def rotary(place):
    half_rot = ROT // 2
    inv_freq = jnp.power(10000.0, -2.0 * jnp.arange(half_rot, dtype=jnp.float32) / ROT)
    angles = place.astype(jnp.float32)[..., None] * inv_freq
    return (jnp.cos(angles), jnp.sin(angles))


def rotate(heads_in, cosv, sinv):
    half_rot = ROT // 2
    first_half = heads_in[..., :half_rot]
    second_half = heads_in[..., half_rot:ROT]
    cos_rows = cosv[:, None, :]
    sin_rows = sinv[:, None, :]
    return jnp.concatenate(
        [
            first_half * cos_rows - second_half * sin_rows,
            second_half * cos_rows + first_half * sin_rows,
            heads_in[..., ROT:],
        ],
        axis=-1,
    )


def rotate_back(heads_in, cosv, sinv):
    half_rot = ROT // 2
    first_half = heads_in[..., :half_rot]
    second_half = heads_in[..., half_rot:ROT]
    cos_rows = cosv[:, None, :]
    sin_rows = sinv[:, None, :]
    return jnp.concatenate(
        [
            first_half * cos_rows + second_half * sin_rows,
            second_half * cos_rows - first_half * sin_rows,
            heads_in[..., ROT:],
        ],
        axis=-1,
    )


def exact_gelu(values):
    return jax.nn.gelu(values, approximate=False)


def allowed_keys(segment):
    row_index = jnp.arange(segment.shape[0], dtype=jnp.int32)
    return (segment[:, None] == segment[None, :]) & (row_index[None, :] <= row_index[:, None])


def contract_rows(left, right):
    return lax.dot_general(
        left, right, (((0,), (0,)), ((), ())), preferred_element_type=jnp.float32
    )


def contract_cols(left, right):
    return lax.dot_general(
        left, right, (((1,), (1,)), ((), ())), preferred_element_type=jnp.float32
    )


def per_device(
    tokens,
    lengths,
    ln_gain,
    ln_bias,
    joined_weight,
    joined_bias,
    dense_weight,
    up_weight,
    up_bias,
    down_weight,
    output_bias,
    cotangent,
):
    leading = lax.axis_index("pipe") == 0
    model_width = joined_weight.shape[1]
    local_width = joined_weight.shape[3]
    local_heads = local_width // HD
    hidden_local = up_weight.shape[2]
    quarter = tokens.shape[1]
    score_scale = HD ** (-0.5)
    ln_gains = ln_gain[0].astype(jnp.float32)
    ln_shifts = ln_bias[0].astype(jnp.float32)
    joined_mat = joined_weight[0].reshape(model_width, 3 * local_width)
    joined_add = joined_bias[0].astype(jnp.float32).reshape(3 * local_width)
    dense_mat = dense_weight[0]
    up_mat = up_weight[0]
    up_add = up_bias[0].astype(jnp.float32)
    down_mat = down_weight[0]
    bias_sum = output_bias[0, 0].astype(jnp.float32) + output_bias[0, 1].astype(jnp.float32)
    gathered_pieces = tensor_pieces(jnp.concatenate([tokens, cotangent], axis=0))
    gathered_rows = jnp.concatenate(gathered_pieces, axis=1)
    input_rows = gathered_rows[: tokens.shape[0]]
    output_grads = gathered_rows[tokens.shape[0] :]
    segment_all, place_all = positions(lengths, MB)
    cos_all, sin_all = rotary(place_all)

    def pick(early_val, late_val):
        return jax.tree.map(
            lambda upper_val, lower_val: jnp.where(leading, upper_val, lower_val),
            early_val,
            late_val,
        )

    received = jnp.zeros((MB, model_width), jnp.bfloat16)
    tick_outputs = []
    tick_stored = []
    for section_tick in range(NMB + 1):
        early_block = min(section_tick, NMB - 1)
        late_block = max(section_tick - 1, 0)
        block_rows = jnp.where(
            leading, input_rows[early_block * MB : (early_block + 1) * MB], received
        )
        segment, cosv, sinv = pick(
            (segment_all[early_block], cos_all[early_block], sin_all[early_block]),
            (segment_all[late_block], cos_all[late_block], sin_all[late_block]),
        )
        inputs = block_rows.astype(jnp.float32)
        row_mean = jnp.mean(inputs, axis=1, keepdims=True)
        centred = inputs - row_mean
        forward_inv_scale = lax.rsqrt(jnp.mean(centred * centred, axis=1, keepdims=True) + EPSILON)
        forward_normed = centred * forward_inv_scale
        forward_h_attn = (forward_normed * ln_gains[0] + ln_shifts[0]).astype(jnp.bfloat16)
        forward_h_mlp = (forward_normed * ln_gains[1] + ln_shifts[1]).astype(jnp.bfloat16)
        joined_proj = (
            jnp.dot(forward_h_attn, joined_mat, preferred_element_type=jnp.float32) + joined_add
        )
        forward_block_len = block_rows.shape[0]
        forward_queries = rotate(
            joined_proj[:, :local_width].reshape(forward_block_len, local_heads, HD), cosv, sinv
        ).astype(jnp.bfloat16)
        forward_keys_rot = rotate(
            joined_proj[:, local_width : 2 * local_width].reshape(
                forward_block_len, local_heads, HD
            ),
            cosv,
            sinv,
        ).astype(jnp.bfloat16)
        forward_values = (
            joined_proj[:, 2 * local_width :]
            .reshape(forward_block_len, local_heads, HD)
            .astype(jnp.bfloat16)
        )
        forward_scores = (
            jnp.einsum(
                "qhd,khd->hqk",
                forward_queries,
                forward_keys_rot,
                preferred_element_type=jnp.float32,
            )
            * score_scale
        )
        forward_scores = jnp.where(allowed_keys(segment)[None], forward_scores, MASKED)
        row_top = jnp.max(forward_scores, axis=2, keepdims=True)
        exponent = jnp.exp(forward_scores - row_top)
        row_total = jnp.sum(exponent, axis=2, keepdims=True)
        forward_log_total = row_top + jnp.log(row_total)
        weights_low = (exponent / row_total).astype(jnp.bfloat16)
        forward_context = jnp.einsum(
            "hqk,khd->qhd", weights_low, forward_values, preferred_element_type=jnp.float32
        )
        forward_context = forward_context.reshape(forward_block_len, local_width).astype(
            jnp.bfloat16
        )
        forward_up_proj = (
            jnp.dot(forward_h_mlp, up_mat, preferred_element_type=jnp.float32) + up_add
        )
        forward_activated = exact_gelu(forward_up_proj).astype(jnp.bfloat16)
        partial_value = jnp.dot(forward_context, dense_mat, preferred_element_type=jnp.float32)
        partial_value = partial_value + jnp.dot(
            forward_activated, down_mat, preferred_element_type=jnp.float32
        )
        branches = tensor_sum(partial_value.astype(jnp.bfloat16))
        result = inputs + branches + bias_sum
        forward_stored = (
            forward_normed,
            forward_inv_scale,
            forward_h_attn,
            forward_h_mlp,
            forward_queries,
            forward_keys_rot,
            forward_values,
            forward_log_total,
            forward_context,
            forward_up_proj,
            forward_activated,
        )
        result, stored = (result, forward_stored)
        result_low = result.astype(jnp.bfloat16)
        tick_outputs.append(result_low)
        tick_stored.append((stored, segment, cosv, sinv))
        if section_tick < NMB:
            received = passed_along(result_low, "pipe", 1)
    column_start = lax.axis_index("tensor") * quarter
    section_rows = jnp.concatenate(
        [jnp.where(leading, tick_outputs[block], tick_outputs[block + 1]) for block in range(NMB)],
        axis=0,
    )
    section_out = lax.dynamic_slice_in_dim(section_rows, column_start, quarter, 1)[None]
    returned = jnp.zeros((MB, model_width), jnp.bfloat16)
    tick_grads = []
    totals = None
    for section_tick in range(NMB + 1):
        own_block = min(section_tick, NMB - 1)
        late_tick = max(section_tick - 1, 0)
        upper_tick = min(section_tick + 1, NMB)
        from_output = output_grads[own_block * MB : (own_block + 1) * MB]
        if section_tick == NMB:
            from_output = jnp.zeros_like(from_output)
        grad_rows = jnp.where(leading, returned, from_output)
        stored, segment, cosv, sinv = pick(tick_stored[late_tick], tick_stored[upper_tick])
        (
            normed,
            inv_scale,
            h_attn,
            h_mlp,
            queries,
            keys_rot,
            values,
            log_total,
            context,
            up_proj,
            activated,
        ) = stored
        block_len = grad_rows.shape[0]
        grad_wide = grad_rows.astype(jnp.float32)
        column_sum = jnp.sum(grad_wide, axis=0)
        backward_grad_dense = contract_rows(context, grad_rows)
        backward_grad_down = contract_rows(activated, grad_rows)
        d_context = contract_cols(grad_rows, dense_mat).astype(jnp.bfloat16)
        d_act = contract_cols(grad_rows, down_mat)
        unused, slope_back = jax.vjp(exact_gelu, up_proj)
        d_up = slope_back(d_act)[0].astype(jnp.bfloat16)
        grad_up_add = jnp.sum(d_up.astype(jnp.float32), axis=0)
        backward_grad_up = contract_rows(h_mlp, d_up)
        d_hmlp = contract_cols(d_up, up_mat)
        scores = (
            jnp.einsum("qhd,khd->hqk", queries, keys_rot, preferred_element_type=jnp.float32)
            * score_scale
        )
        scores = jnp.where(allowed_keys(segment)[None], scores, MASKED)
        weights_soft = jnp.exp(scores - log_total)
        d_context3 = d_context.reshape(block_len, local_heads, HD)
        d_values = jnp.einsum(
            "hqk,qhd->khd",
            weights_soft.astype(jnp.bfloat16),
            d_context3,
            preferred_element_type=jnp.float32,
        ).astype(jnp.bfloat16)
        d_weights = jnp.einsum(
            "qhd,khd->hqk", d_context3, values, preferred_element_type=jnp.float32
        )
        row_delta = jnp.sum(weights_soft * d_weights, axis=2, keepdims=True)
        d_scores = (weights_soft * (d_weights - row_delta)).astype(jnp.bfloat16)
        d_queries = (
            jnp.einsum("hqk,khd->qhd", d_scores, keys_rot, preferred_element_type=jnp.float32)
            * score_scale
        )
        d_keys = (
            jnp.einsum("hqk,qhd->khd", d_scores, queries, preferred_element_type=jnp.float32)
            * score_scale
        )
        d_queries = (
            rotate_back(d_queries, cosv, sinv).reshape(block_len, local_width).astype(jnp.bfloat16)
        )
        d_keys = (
            rotate_back(d_keys, cosv, sinv).reshape(block_len, local_width).astype(jnp.bfloat16)
        )
        d_joined = jnp.concatenate(
            [d_queries, d_keys, d_values.reshape(block_len, local_width)], axis=1
        )
        grad_joined_add = jnp.sum(d_joined.astype(jnp.float32), axis=0)
        backward_grad_joined = contract_rows(d_joined, h_attn)
        d_hattn = contract_cols(d_joined, joined_mat)
        d_both = tensor_sum(
            jnp.concatenate([d_hattn, d_hmlp], axis=1).astype(jnp.bfloat16)
        )
        d_hattn, d_hmlp = d_both[:, :model_width], d_both[:, model_width:]
        grad_gains = jnp.concatenate(
            [jnp.sum(d_hattn * normed, axis=0), jnp.sum(d_hmlp * normed, axis=0)]
        )
        grad_shifts = jnp.concatenate([jnp.sum(d_hattn, axis=0), jnp.sum(d_hmlp, axis=0)])
        d_norm = d_hattn * ln_gains[0] + d_hmlp * ln_gains[1]
        grad_input = grad_wide + inv_scale * (
            d_norm
            - jnp.mean(d_norm, axis=1, keepdims=True)
            - normed * jnp.mean(d_norm * normed, axis=1, keepdims=True)
        )
        small_terms = jnp.concatenate(
            [grad_gains, grad_shifts, column_sum, column_sum, grad_joined_add, grad_up_add]
        )
        terms = (
            backward_grad_joined[None],
            backward_grad_dense[None],
            backward_grad_up[None],
            backward_grad_down[None],
            small_terms[None],
        )
        grad_input, terms = (grad_input, terms)
        grad_low = grad_input.astype(jnp.bfloat16)
        tick_grads.append(grad_low)
        if totals is None:
            totals = terms
        else:
            totals = jax.tree.map(lambda older, newer: older + newer, totals, terms)
        if section_tick < NMB:
            returned = passed_along(grad_low, "pipe", -1)
    small_rows = totals[4][0]
    small_pad = (-small_rows.shape[0]) % model_width
    small_rows = jnp.pad(small_rows, (0, small_pad)).reshape(-1, model_width)
    pieces = (totals[0][0], totals[1][0], totals[2][0], totals[3][0], small_rows)
    slab = jnp.concatenate([piece.astype(jnp.bfloat16) for piece in pieces], axis=0)
    slab = lax.psum(slab, "dp").astype(jnp.float32)
    summed = []
    offset = 0
    for piece in pieces:
        summed.append(slab[offset : offset + piece.shape[0]])
        offset = offset + piece.shape[0]
    grad_rows_all = jnp.concatenate(
        [jnp.where(leading, tick_grads[block + 1], tick_grads[block]) for block in range(NMB)],
        axis=0,
    )
    input_grad = lax.dynamic_slice_in_dim(grad_rows_all, column_start, quarter, 1)[None]
    grad_joined = summed[0].T.reshape(1, model_width, 3, local_width)
    grad_dense = summed[1][None]
    grad_up = summed[2][None]
    grad_down = summed[3][None]
    small_sum = summed[4].reshape(-1)
    offset = 0
    grad_ln_gain = small_sum[offset : offset + 2 * model_width].reshape(1, 2, model_width)
    offset = offset + 2 * model_width
    grad_ln_bias = small_sum[offset : offset + 2 * model_width].reshape(1, 2, model_width)
    offset = offset + 2 * model_width
    grad_output_bias = small_sum[offset : offset + 2 * model_width].reshape(1, 2, model_width)
    offset = offset + 2 * model_width
    grad_joined_bias = small_sum[offset : offset + 3 * local_width].reshape(1, 3, local_width)
    offset = offset + 3 * local_width
    grad_up_bias = small_sum[offset : offset + hidden_local].reshape(1, hidden_local)
    return (
        section_out,
        input_grad,
        grad_ln_gain,
        grad_ln_bias,
        grad_joined,
        grad_joined_bias,
        grad_dense,
        grad_up,
        grad_up_bias,
        grad_down,
        grad_output_bias,
    )


def solution(mesh):
    placed = (
        P("dp", "tensor"),
        P("dp", None),
        P("pipe", None, None),
        P("pipe", None, None),
        P("pipe", None, None, "tensor"),
        P("pipe", None, "tensor"),
        P("pipe", "tensor", None),
        P("pipe", None, "tensor"),
        P("pipe", "tensor"),
        P("pipe", "tensor", None),
        P("pipe", None, None),
        P("dp", "tensor"),
    )
    return jax.shard_map(
        per_device,
        mesh=mesh,
        in_specs=placed,
        out_specs=(
            P("pipe", "dp", "tensor"),
            P("pipe", "dp", "tensor"),
            P("pipe", None, None),
            P("pipe", None, None),
            P("pipe", None, None, "tensor"),
            P("pipe", None, "tensor"),
            P("pipe", "tensor", None),
            P("pipe", None, "tensor"),
            P("pipe", "tensor"),
            P("pipe", "tensor", None),
            P("pipe", None, None),
        ),
        check_vma=False,
    )
```

```python
import jax
import jax.numpy as jnp
from jax import lax
from jax.sharding import PartitionSpec as P
from jax.experimental import pallas as pl
from jax.experimental.pallas import tpu as pltpu

HD = 64
ROT = 16
MB = 128
NMB = 4


EPSILON = 1e-05
MASKED = -1e30


def passed_along(x, axis, by):
    peers = lax.axis_size(axis)
    pairs = [(i, i + by) for i in range(peers) if 0 <= i + by < peers]
    return lax.ppermute(x, axis, pairs)


def tensor_pieces(x):
    peers = lax.axis_size("tensor")
    me = lax.axis_index("tensor")
    parts = [x]
    for shift in range(1, peers):
        pairs = [(i, (i + shift) % peers) for i in range(peers)]
        parts.append(lax.ppermute(x, "tensor", pairs))
    ordered = []
    for owner in range(peers):
        slot = (me - owner) % peers
        chosen = parts[peers - 1]
        for k in range(peers - 2, -1, -1):
            chosen = jnp.where(slot == k, parts[k], chosen)
        ordered.append(chosen)
    return ordered


def tensor_sum(x):
    pieces = tensor_pieces(x)
    total = pieces[0].astype(jnp.float32)
    for piece in pieces[1:]:
        total = total + piece.astype(jnp.float32)
    return total

def as_sent(x):
    return jax.tree.map(lambda a: a.astype(jnp.bfloat16) if a.dtype == jnp.float32 else a, x)


def positions(lengths, block_rows):
    seq_count = lengths.shape[1]
    counter = jnp.arange(seq_count, dtype=jnp.int32)
    lower_tri = (counter[:, None] >= counter[None, :]).astype(jnp.int32)
    seg_ends = jnp.sum(lengths[:, None, :] * lower_tri[None, :, :], axis=2)
    starts = seg_ends - lengths
    row_index = jnp.arange(block_rows, dtype=jnp.int32)
    segment = jnp.sum((row_index[None, :, None] >= seg_ends[:, None, :]).astype(jnp.int32), axis=2)
    member = (segment[:, :, None] == counter[None, None, :]).astype(jnp.int32)
    place = row_index[None, :] - jnp.sum(member * starts[:, None, :], axis=2)
    return (segment, place)


def rotary(place):
    half_rot = ROT // 2
    inv_freq = jnp.power(10000.0, -2.0 * jnp.arange(half_rot, dtype=jnp.float32) / ROT)
    angles = place.astype(jnp.float32)[..., None] * inv_freq
    return (jnp.cos(angles), jnp.sin(angles))


def rotate(heads_in, cosv, sinv):
    half_rot = ROT // 2
    first_half = heads_in[..., :half_rot]
    second_half = heads_in[..., half_rot:ROT]
    cos_rows = cosv[:, None, :]
    sin_rows = sinv[:, None, :]
    return jnp.concatenate(
        [
            first_half * cos_rows - second_half * sin_rows,
            second_half * cos_rows + first_half * sin_rows,
            heads_in[..., ROT:],
        ],
        axis=-1,
    )


def rotate_back(heads_in, cosv, sinv):
    half_rot = ROT // 2
    first_half = heads_in[..., :half_rot]
    second_half = heads_in[..., half_rot:ROT]
    cos_rows = cosv[:, None, :]
    sin_rows = sinv[:, None, :]
    return jnp.concatenate(
        [
            first_half * cos_rows + second_half * sin_rows,
            second_half * cos_rows - first_half * sin_rows,
            heads_in[..., ROT:],
        ],
        axis=-1,
    )


def exact_gelu(values):
    return jax.nn.gelu(values, approximate=False)


def allowed_keys(segment):
    row_index = jnp.arange(segment.shape[0], dtype=jnp.int32)
    return (segment[:, None] == segment[None, :]) & (row_index[None, :] <= row_index[:, None])


def contract_rows(left, right):
    return lax.dot_general(
        left, right, (((0,), (0,)), ((), ())), preferred_element_type=jnp.float32
    )


def contract_cols(left, right):
    return lax.dot_general(
        left, right, (((1,), (1,)), ((), ())), preferred_element_type=jnp.float32
    )


def _allowed_in_kernel(seg_col_ref, seg_row_ref, rows):
    row_id = lax.broadcasted_iota(jnp.int32, (rows, rows), 0)
    col_id = lax.broadcasted_iota(jnp.int32, (rows, rows), 1)
    return (seg_col_ref[...] == seg_row_ref[...]) & (col_id <= row_id)


def _masked_scores(q, k, allowed):
    scores = lax.dot_general(
        q, k, (((1,), (1,)), ((), ())), preferred_element_type=jnp.float32
    ) * (HD ** (-0.5))
    return jnp.where(allowed, scores, MASKED)


def _attention_forward_kernel(seg_col_ref, seg_row_ref, q_ref, k_ref, v_ref, ctx_ref, lt_ref):
    rows = q_ref.shape[0]
    allowed = _allowed_in_kernel(seg_col_ref, seg_row_ref, rows)
    for head in range(q_ref.shape[1] // HD):
        cols = slice(head * HD, (head + 1) * HD)
        scores = _masked_scores(q_ref[:, cols], k_ref[:, cols], allowed)
        row_top = jnp.max(scores, axis=1, keepdims=True)
        exponent = jnp.exp(scores - row_top)
        row_total = jnp.sum(exponent, axis=1, keepdims=True)
        lt_ref[:, head : head + 1] = row_top + jnp.log(row_total)
        weights = (exponent / row_total).astype(jnp.bfloat16)
        ctx_ref[:, cols] = jnp.dot(
            weights, v_ref[:, cols], preferred_element_type=jnp.float32
        ).astype(ctx_ref.dtype)


def _attention_backward_kernel(
    seg_col_ref, seg_row_ref, q_ref, k_ref, v_ref, dctx_ref, lt_ref, dq_ref, dk_ref, dv_ref
):
    rows = q_ref.shape[0]
    allowed = _allowed_in_kernel(seg_col_ref, seg_row_ref, rows)
    scale = HD ** (-0.5)
    for head in range(q_ref.shape[1] // HD):
        cols = slice(head * HD, (head + 1) * HD)
        q = q_ref[:, cols]
        k = k_ref[:, cols]
        dctx = dctx_ref[:, cols]
        scores = _masked_scores(q, k, allowed)
        weights = jnp.exp(scores - lt_ref[:, head : head + 1])
        dv_ref[:, cols] = lax.dot_general(
            weights.astype(jnp.bfloat16),
            dctx,
            (((0,), (0,)), ((), ())),
            preferred_element_type=jnp.float32,
        ).astype(dv_ref.dtype)
        d_weights = lax.dot_general(
            dctx, v_ref[:, cols], (((1,), (1,)), ((), ())), preferred_element_type=jnp.float32
        )
        row_delta = jnp.sum(weights * d_weights, axis=1, keepdims=True)
        d_scores = (weights * (d_weights - row_delta)).astype(jnp.bfloat16)
        dq_ref[:, cols] = jnp.dot(d_scores, k, preferred_element_type=jnp.float32) * scale
        dk_ref[:, cols] = (
            lax.dot_general(
                d_scores, q, (((0,), (0,)), ((), ())), preferred_element_type=jnp.float32
            )
            * scale
        )


def _vmem_specs(count):
    return [pl.BlockSpec(memory_space=pltpu.VMEM)] * count


def attention_forward(q, k, v, segment):
    rows, width = q.shape
    heads = width // HD
    return pl.pallas_call(
        _attention_forward_kernel,
        out_shape=(
            jax.ShapeDtypeStruct((rows, width), jnp.bfloat16),
            jax.ShapeDtypeStruct((rows, heads), jnp.float32),
        ),
        in_specs=_vmem_specs(5),
        out_specs=tuple(_vmem_specs(2)),
        cost_estimate=pl.CostEstimate(
            flops=4 * rows * rows * width, transcendentals=rows * rows * heads,
            bytes_accessed=4 * rows * width * 2,
        ),
    )(segment[:, None], segment[None, :], q, k, v)


def attention_backward(q, k, v, d_context, log_total, segment):
    rows, width = q.shape
    heads = width // HD
    return pl.pallas_call(
        _attention_backward_kernel,
        out_shape=(
            jax.ShapeDtypeStruct((rows, width), jnp.float32),
            jax.ShapeDtypeStruct((rows, width), jnp.float32),
            jax.ShapeDtypeStruct((rows, width), jnp.bfloat16),
        ),
        in_specs=_vmem_specs(7),
        out_specs=tuple(_vmem_specs(3)),
        cost_estimate=pl.CostEstimate(
            flops=10 * rows * rows * width, transcendentals=rows * rows * heads,
            bytes_accessed=4 * rows * width * 2 + 2 * rows * width * 4,
        ),
    )(segment[:, None], segment[None, :], q, k, v, d_context, log_total)


def per_device(
    tokens,
    lengths,
    ln_gain,
    ln_bias,
    joined_weight,
    joined_bias,
    dense_weight,
    up_weight,
    up_bias,
    down_weight,
    output_bias,
    cotangent,
):
    leading = lax.axis_index("pipe") == 0
    model_width = joined_weight.shape[1]
    local_width = joined_weight.shape[3]
    local_heads = local_width // HD
    hidden_local = up_weight.shape[2]
    quarter = tokens.shape[1]
    score_scale = HD ** (-0.5)
    ln_gains = ln_gain[0].astype(jnp.float32)
    ln_shifts = ln_bias[0].astype(jnp.float32)
    joined_mat = joined_weight[0].reshape(model_width, 3 * local_width)
    joined_add = joined_bias[0].astype(jnp.float32).reshape(3 * local_width)
    dense_mat = dense_weight[0]
    up_mat = up_weight[0]
    up_add = up_bias[0].astype(jnp.float32)
    down_mat = down_weight[0]
    bias_sum = output_bias[0, 0].astype(jnp.float32) + output_bias[0, 1].astype(jnp.float32)
    gathered_pieces = tensor_pieces(jnp.concatenate([tokens, cotangent], axis=0))
    gathered_rows = jnp.concatenate(gathered_pieces, axis=1)
    input_rows = gathered_rows[: tokens.shape[0]]
    output_grads = gathered_rows[tokens.shape[0] :]
    segment_all, place_all = positions(lengths, MB)
    cos_all, sin_all = rotary(place_all)

    def pick(early_val, late_val):
        return jax.tree.map(
            lambda upper_val, lower_val: jnp.where(leading, upper_val, lower_val),
            early_val,
            late_val,
        )

    received = jnp.zeros((MB, model_width), jnp.bfloat16)
    tick_outputs = []
    tick_stored = []
    for section_tick in range(NMB + 1):
        early_block = min(section_tick, NMB - 1)
        late_block = max(section_tick - 1, 0)
        block_rows = jnp.where(
            leading, input_rows[early_block * MB : (early_block + 1) * MB], received
        )
        segment, cosv, sinv = pick(
            (segment_all[early_block], cos_all[early_block], sin_all[early_block]),
            (segment_all[late_block], cos_all[late_block], sin_all[late_block]),
        )
        inputs = block_rows.astype(jnp.float32)
        row_mean = jnp.mean(inputs, axis=1, keepdims=True)
        centred = inputs - row_mean
        forward_inv_scale = lax.rsqrt(jnp.mean(centred * centred, axis=1, keepdims=True) + EPSILON)
        forward_normed = centred * forward_inv_scale
        forward_h_attn = (forward_normed * ln_gains[0] + ln_shifts[0]).astype(jnp.bfloat16)
        forward_h_mlp = (forward_normed * ln_gains[1] + ln_shifts[1]).astype(jnp.bfloat16)
        joined_proj = (
            jnp.dot(forward_h_attn, joined_mat, preferred_element_type=jnp.float32) + joined_add
        )
        forward_block_len = block_rows.shape[0]
        forward_queries = rotate(
            joined_proj[:, :local_width].reshape(forward_block_len, local_heads, HD), cosv, sinv
        ).astype(jnp.bfloat16)
        forward_keys_rot = rotate(
            joined_proj[:, local_width : 2 * local_width].reshape(
                forward_block_len, local_heads, HD
            ),
            cosv,
            sinv,
        ).astype(jnp.bfloat16)
        forward_values = (
            joined_proj[:, 2 * local_width :]
            .reshape(forward_block_len, local_heads, HD)
            .astype(jnp.bfloat16)
        )
        local_rows = (forward_block_len, local_width)
        forward_context, forward_log_total = attention_forward(
            forward_queries.reshape(local_rows),
            forward_keys_rot.reshape(local_rows),
            forward_values.reshape(local_rows),
            segment,
        )
        forward_up_proj = (
            jnp.dot(forward_h_mlp, up_mat, preferred_element_type=jnp.float32) + up_add
        )
        forward_activated = exact_gelu(forward_up_proj).astype(jnp.bfloat16)
        partial_value = jnp.dot(forward_context, dense_mat, preferred_element_type=jnp.float32)
        partial_value = partial_value + jnp.dot(
            forward_activated, down_mat, preferred_element_type=jnp.float32
        )
        branches = tensor_sum(partial_value.astype(jnp.bfloat16))
        result = inputs + branches + bias_sum
        forward_stored = (
            forward_normed,
            forward_inv_scale,
            forward_h_attn,
            forward_h_mlp,
            forward_queries,
            forward_keys_rot,
            forward_values,
            forward_log_total,
            forward_context,
            forward_up_proj,
            forward_activated,
        )
        result, stored = (result, forward_stored)
        result_low = result.astype(jnp.bfloat16)
        tick_outputs.append(result_low)
        tick_stored.append((stored, segment, cosv, sinv))
        if section_tick < NMB:
            received = passed_along(result_low, "pipe", 1)
    column_start = lax.axis_index("tensor") * quarter
    section_rows = jnp.concatenate(
        [jnp.where(leading, tick_outputs[block], tick_outputs[block + 1]) for block in range(NMB)],
        axis=0,
    )
    section_out = lax.dynamic_slice_in_dim(section_rows, column_start, quarter, 1)[None]
    returned = jnp.zeros((MB, model_width), jnp.bfloat16)
    tick_grads = []
    totals = None
    for section_tick in range(NMB + 1):
        own_block = min(section_tick, NMB - 1)
        late_tick = max(section_tick - 1, 0)
        upper_tick = min(section_tick + 1, NMB)
        from_output = output_grads[own_block * MB : (own_block + 1) * MB]
        if section_tick == NMB:
            from_output = jnp.zeros_like(from_output)
        grad_rows = jnp.where(leading, returned, from_output)
        stored, segment, cosv, sinv = pick(tick_stored[late_tick], tick_stored[upper_tick])
        (
            normed,
            inv_scale,
            h_attn,
            h_mlp,
            queries,
            keys_rot,
            values,
            log_total,
            context,
            up_proj,
            activated,
        ) = stored
        block_len = grad_rows.shape[0]
        grad_wide = grad_rows.astype(jnp.float32)
        column_sum = jnp.sum(grad_wide, axis=0)
        backward_grad_dense = contract_rows(context, grad_rows)
        backward_grad_down = contract_rows(activated, grad_rows)
        d_context = contract_cols(grad_rows, dense_mat).astype(jnp.bfloat16)
        d_act = contract_cols(grad_rows, down_mat)
        unused, slope_back = jax.vjp(exact_gelu, up_proj)
        d_up = slope_back(d_act)[0].astype(jnp.bfloat16)
        grad_up_add = jnp.sum(d_up.astype(jnp.float32), axis=0)
        backward_grad_up = contract_rows(h_mlp, d_up)
        d_hmlp = contract_cols(d_up, up_mat)
        flat = (block_len, local_width)
        d_queries, d_keys, d_values = attention_backward(
            queries.reshape(flat),
            keys_rot.reshape(flat),
            values.reshape(flat),
            d_context,
            log_total,
            segment,
        )
        heads_shape = (block_len, local_heads, HD)
        d_queries = (
            rotate_back(d_queries.reshape(heads_shape), cosv, sinv).reshape(flat).astype(jnp.bfloat16)
        )
        d_keys = (
            rotate_back(d_keys.reshape(heads_shape), cosv, sinv).reshape(flat).astype(jnp.bfloat16)
        )
        d_joined = jnp.concatenate([d_queries, d_keys, d_values], axis=1)
        grad_joined_add = jnp.sum(d_joined.astype(jnp.float32), axis=0)
        backward_grad_joined = contract_rows(d_joined, h_attn)
        d_hattn = contract_cols(d_joined, joined_mat)
        d_both = tensor_sum(
            jnp.concatenate([d_hattn, d_hmlp], axis=1).astype(jnp.bfloat16)
        )
        d_hattn, d_hmlp = d_both[:, :model_width], d_both[:, model_width:]
        grad_gains = jnp.concatenate(
            [jnp.sum(d_hattn * normed, axis=0), jnp.sum(d_hmlp * normed, axis=0)]
        )
        grad_shifts = jnp.concatenate([jnp.sum(d_hattn, axis=0), jnp.sum(d_hmlp, axis=0)])
        d_norm = d_hattn * ln_gains[0] + d_hmlp * ln_gains[1]
        grad_input = grad_wide + inv_scale * (
            d_norm
            - jnp.mean(d_norm, axis=1, keepdims=True)
            - normed * jnp.mean(d_norm * normed, axis=1, keepdims=True)
        )
        small_terms = jnp.concatenate(
            [grad_gains, grad_shifts, column_sum, column_sum, grad_joined_add, grad_up_add]
        )
        terms = (
            backward_grad_joined[None],
            backward_grad_dense[None],
            backward_grad_up[None],
            backward_grad_down[None],
            small_terms[None],
        )
        grad_input, terms = (grad_input, terms)
        grad_low = grad_input.astype(jnp.bfloat16)
        tick_grads.append(grad_low)
        if totals is None:
            totals = terms
        else:
            totals = jax.tree.map(lambda older, newer: older + newer, totals, terms)
        if section_tick < NMB:
            returned = passed_along(grad_low, "pipe", -1)
    small_rows = totals[4][0]
    small_pad = (-small_rows.shape[0]) % model_width
    small_rows = jnp.pad(small_rows, (0, small_pad)).reshape(-1, model_width)
    pieces = (totals[0][0], totals[1][0], totals[2][0], totals[3][0], small_rows)
    slab = jnp.concatenate([piece.astype(jnp.bfloat16) for piece in pieces], axis=0)
    slab = lax.psum(slab, "dp").astype(jnp.float32)
    summed = []
    offset = 0
    for piece in pieces:
        summed.append(slab[offset : offset + piece.shape[0]])
        offset = offset + piece.shape[0]
    grad_rows_all = jnp.concatenate(
        [jnp.where(leading, tick_grads[block + 1], tick_grads[block]) for block in range(NMB)],
        axis=0,
    )
    input_grad = lax.dynamic_slice_in_dim(grad_rows_all, column_start, quarter, 1)[None]
    grad_joined = summed[0].T.reshape(1, model_width, 3, local_width)
    grad_dense = summed[1][None]
    grad_up = summed[2][None]
    grad_down = summed[3][None]
    small_sum = summed[4].reshape(-1)
    offset = 0
    grad_ln_gain = small_sum[offset : offset + 2 * model_width].reshape(1, 2, model_width)
    offset = offset + 2 * model_width
    grad_ln_bias = small_sum[offset : offset + 2 * model_width].reshape(1, 2, model_width)
    offset = offset + 2 * model_width
    grad_output_bias = small_sum[offset : offset + 2 * model_width].reshape(1, 2, model_width)
    offset = offset + 2 * model_width
    grad_joined_bias = small_sum[offset : offset + 3 * local_width].reshape(1, 3, local_width)
    offset = offset + 3 * local_width
    grad_up_bias = small_sum[offset : offset + hidden_local].reshape(1, hidden_local)
    return (
        section_out,
        input_grad,
        grad_ln_gain,
        grad_ln_bias,
        grad_joined,
        grad_joined_bias,
        grad_dense,
        grad_up,
        grad_up_bias,
        grad_down,
        grad_output_bias,
    )


def solution(mesh):
    placed = (
        P("dp", "tensor"),
        P("dp", None),
        P("pipe", None, None),
        P("pipe", None, None),
        P("pipe", None, None, "tensor"),
        P("pipe", None, "tensor"),
        P("pipe", "tensor", None),
        P("pipe", None, "tensor"),
        P("pipe", "tensor"),
        P("pipe", "tensor", None),
        P("pipe", None, None),
        P("dp", "tensor"),
    )
    return jax.shard_map(
        per_device,
        mesh=mesh,
        in_specs=placed,
        out_specs=(
            P("pipe", "dp", "tensor"),
            P("pipe", "dp", "tensor"),
            P("pipe", None, None),
            P("pipe", None, None),
            P("pipe", None, None, "tensor"),
            P("pipe", None, "tensor"),
            P("pipe", "tensor", None),
            P("pipe", None, "tensor"),
            P("pipe", "tensor"),
            P("pipe", "tensor", None),
            P("pipe", None, None),
        ),
        check_vma=False,
    )
```

```python
import jax
import jax.numpy as jnp
from jax import lax
from jax.sharding import PartitionSpec as P

HD = 64
ROT = 16
MB = 128
NMB = 2


EPSILON = 1e-05
MASKED = -1e30


def passed_along(x, axis, by):
    peers = lax.axis_size(axis)
    pairs = [(i, i + by) for i in range(peers) if 0 <= i + by < peers]
    return lax.ppermute(x, axis, pairs)


def tensor_pieces(x):
    peers = lax.axis_size("tensor")
    me = lax.axis_index("tensor")
    parts = [x]
    for shift in range(1, peers):
        pairs = [(i, (i + shift) % peers) for i in range(peers)]
        parts.append(lax.ppermute(x, "tensor", pairs))
    ordered = []
    for owner in range(peers):
        slot = (me - owner) % peers
        chosen = parts[peers - 1]
        for k in range(peers - 2, -1, -1):
            chosen = jnp.where(slot == k, parts[k], chosen)
        ordered.append(chosen)
    return ordered


def tensor_sum(x):
    pieces = tensor_pieces(x)
    total = pieces[0].astype(jnp.float32)
    for piece in pieces[1:]:
        total = total + piece.astype(jnp.float32)
    return total

def as_sent(x):
    return jax.tree.map(lambda a: a.astype(jnp.bfloat16) if a.dtype == jnp.float32 else a, x)


def positions(lengths, block_rows):
    seq_count = lengths.shape[1]
    counter = jnp.arange(seq_count, dtype=jnp.int32)
    lower_tri = (counter[:, None] >= counter[None, :]).astype(jnp.int32)
    seg_ends = jnp.sum(lengths[:, None, :] * lower_tri[None, :, :], axis=2)
    starts = seg_ends - lengths
    row_index = jnp.arange(block_rows, dtype=jnp.int32)
    segment = jnp.sum((row_index[None, :, None] >= seg_ends[:, None, :]).astype(jnp.int32), axis=2)
    member = (segment[:, :, None] == counter[None, None, :]).astype(jnp.int32)
    place = row_index[None, :] - jnp.sum(member * starts[:, None, :], axis=2)
    return (segment, place)


def rotary(place):
    half_rot = ROT // 2
    inv_freq = jnp.power(10000.0, -2.0 * jnp.arange(half_rot, dtype=jnp.float32) / ROT)
    angles = place.astype(jnp.float32)[..., None] * inv_freq
    return (jnp.cos(angles), jnp.sin(angles))


def rotate(heads_in, cosv, sinv):
    half_rot = ROT // 2
    first_half = heads_in[..., :half_rot]
    second_half = heads_in[..., half_rot:ROT]
    cos_rows = cosv[:, None, :]
    sin_rows = sinv[:, None, :]
    return jnp.concatenate(
        [
            first_half * cos_rows - second_half * sin_rows,
            second_half * cos_rows + first_half * sin_rows,
            heads_in[..., ROT:],
        ],
        axis=-1,
    )


def rotate_back(heads_in, cosv, sinv):
    half_rot = ROT // 2
    first_half = heads_in[..., :half_rot]
    second_half = heads_in[..., half_rot:ROT]
    cos_rows = cosv[:, None, :]
    sin_rows = sinv[:, None, :]
    return jnp.concatenate(
        [
            first_half * cos_rows + second_half * sin_rows,
            second_half * cos_rows - first_half * sin_rows,
            heads_in[..., ROT:],
        ],
        axis=-1,
    )


def exact_gelu(values):
    return jax.nn.gelu(values, approximate=False)


def allowed_keys(segment):
    row_index = jnp.arange(segment.shape[-1], dtype=jnp.int32)
    same = segment[..., :, None] == segment[..., None, :]
    return same & (row_index[None, :] <= row_index[:, None])


def contract_rows(left, right):
    return lax.dot_general(
        left, right, (((0,), (0,)), ((), ())), preferred_element_type=jnp.float32
    )


def contract_cols(left, right):
    return lax.dot_general(
        left, right, (((1,), (1,)), ((), ())), preferred_element_type=jnp.float32
    )


def per_device(
    tokens,
    lengths,
    ln_gain,
    ln_bias,
    joined_weight,
    joined_bias,
    dense_weight,
    up_weight,
    up_bias,
    down_weight,
    output_bias,
    cotangent,
):
    leading = lax.axis_index("pipe") == 0
    model_width = joined_weight.shape[1]
    local_width = joined_weight.shape[3]
    local_heads = local_width // HD
    hidden_local = up_weight.shape[2]
    quarter = tokens.shape[1]
    score_scale = HD ** (-0.5)
    ln_gains = ln_gain[0].astype(jnp.float32)
    ln_shifts = ln_bias[0].astype(jnp.float32)
    joined_mat = joined_weight[0].reshape(model_width, 3 * local_width)
    joined_add = joined_bias[0].astype(jnp.float32).reshape(3 * local_width)
    dense_mat = dense_weight[0]
    up_mat = up_weight[0]
    up_add = up_bias[0].astype(jnp.float32)
    down_mat = down_weight[0]
    bias_sum = output_bias[0, 0].astype(jnp.float32) + output_bias[0, 1].astype(jnp.float32)
    gathered_pieces = tensor_pieces(jnp.concatenate([tokens, cotangent], axis=0))
    gathered_rows = jnp.concatenate(gathered_pieces, axis=1)
    input_rows = gathered_rows[: tokens.shape[0]]
    output_grads = gathered_rows[tokens.shape[0] :]
    tick_rows = tokens.shape[0] // NMB
    sub_blocks = tick_rows // MB
    segment_all, place_all = positions(lengths, MB)
    cos_all, sin_all = rotary(place_all)
    segment_all = segment_all.reshape(NMB, sub_blocks, MB)
    cos_all = cos_all.reshape(NMB, tick_rows, cos_all.shape[-1])
    sin_all = sin_all.reshape(NMB, tick_rows, sin_all.shape[-1])

    def pick(early_val, late_val):
        return jax.tree.map(
            lambda upper_val, lower_val: jnp.where(leading, upper_val, lower_val),
            early_val,
            late_val,
        )

    received = jnp.zeros((tick_rows, model_width), jnp.bfloat16)
    tick_outputs = []
    tick_stored = []
    for section_tick in range(NMB + 1):
        early_block = min(section_tick, NMB - 1)
        late_block = max(section_tick - 1, 0)
        block_rows = jnp.where(
            leading, input_rows[early_block * tick_rows : (early_block + 1) * tick_rows], received
        )
        segment, cosv, sinv = pick(
            (segment_all[early_block], cos_all[early_block], sin_all[early_block]),
            (segment_all[late_block], cos_all[late_block], sin_all[late_block]),
        )
        inputs = block_rows.astype(jnp.float32)
        row_mean = jnp.mean(inputs, axis=1, keepdims=True)
        centred = inputs - row_mean
        forward_inv_scale = lax.rsqrt(jnp.mean(centred * centred, axis=1, keepdims=True) + EPSILON)
        forward_normed = centred * forward_inv_scale
        forward_h_attn = (forward_normed * ln_gains[0] + ln_shifts[0]).astype(jnp.bfloat16)
        forward_h_mlp = (forward_normed * ln_gains[1] + ln_shifts[1]).astype(jnp.bfloat16)
        joined_proj = (
            jnp.dot(forward_h_attn, joined_mat, preferred_element_type=jnp.float32) + joined_add
        )
        forward_block_len = block_rows.shape[0]
        forward_queries = rotate(
            joined_proj[:, :local_width].reshape(forward_block_len, local_heads, HD), cosv, sinv
        ).astype(jnp.bfloat16)
        forward_keys_rot = rotate(
            joined_proj[:, local_width : 2 * local_width].reshape(
                forward_block_len, local_heads, HD
            ),
            cosv,
            sinv,
        ).astype(jnp.bfloat16)
        forward_values = (
            joined_proj[:, 2 * local_width :]
            .reshape(forward_block_len, local_heads, HD)
            .astype(jnp.bfloat16)
        )
        blocked = (sub_blocks, MB, local_heads, HD)
        forward_scores = (
            jnp.einsum(
                "bqhd,bkhd->bhqk",
                forward_queries.reshape(blocked),
                forward_keys_rot.reshape(blocked),
                preferred_element_type=jnp.float32,
            )
            * score_scale
        )
        forward_scores = jnp.where(allowed_keys(segment)[:, None], forward_scores, MASKED)
        row_top = jnp.max(forward_scores, axis=3, keepdims=True)
        exponent = jnp.exp(forward_scores - row_top)
        row_total = jnp.sum(exponent, axis=3, keepdims=True)
        forward_log_total = row_top + jnp.log(row_total)
        weights_low = (exponent / row_total).astype(jnp.bfloat16)
        forward_context = jnp.einsum(
            "bhqk,bkhd->bqhd",
            weights_low,
            forward_values.reshape(blocked),
            preferred_element_type=jnp.float32,
        )
        forward_context = forward_context.reshape(forward_block_len, local_width).astype(
            jnp.bfloat16
        )
        forward_up_proj = (
            jnp.dot(forward_h_mlp, up_mat, preferred_element_type=jnp.float32) + up_add
        )
        forward_activated = exact_gelu(forward_up_proj).astype(jnp.bfloat16)
        partial_value = jnp.dot(forward_context, dense_mat, preferred_element_type=jnp.float32)
        partial_value = partial_value + jnp.dot(
            forward_activated, down_mat, preferred_element_type=jnp.float32
        )
        branches = tensor_sum(partial_value.astype(jnp.bfloat16))
        result = inputs + branches + bias_sum
        forward_stored = (
            forward_normed,
            forward_inv_scale,
            forward_h_attn,
            forward_h_mlp,
            forward_queries,
            forward_keys_rot,
            forward_values,
            forward_log_total,
            forward_context,
            forward_up_proj,
            forward_activated,
        )
        result, stored = (result, forward_stored)
        result_low = result.astype(jnp.bfloat16)
        tick_outputs.append(result_low)
        tick_stored.append((stored, segment, cosv, sinv))
        if section_tick < NMB:
            received = passed_along(result_low, "pipe", 1)
    column_start = lax.axis_index("tensor") * quarter
    section_rows = jnp.concatenate(
        [jnp.where(leading, tick_outputs[block], tick_outputs[block + 1]) for block in range(NMB)],
        axis=0,
    )
    section_out = lax.dynamic_slice_in_dim(section_rows, column_start, quarter, 1)[None]
    returned = jnp.zeros((tick_rows, model_width), jnp.bfloat16)
    tick_grads = []
    totals = None
    for section_tick in range(NMB + 1):
        own_block = min(section_tick, NMB - 1)
        late_tick = max(section_tick - 1, 0)
        upper_tick = min(section_tick + 1, NMB)
        from_output = output_grads[own_block * tick_rows : (own_block + 1) * tick_rows]
        if section_tick == NMB:
            from_output = jnp.zeros_like(from_output)
        grad_rows = jnp.where(leading, returned, from_output)
        stored, segment, cosv, sinv = pick(tick_stored[late_tick], tick_stored[upper_tick])
        (
            normed,
            inv_scale,
            h_attn,
            h_mlp,
            queries,
            keys_rot,
            values,
            log_total,
            context,
            up_proj,
            activated,
        ) = stored
        block_len = grad_rows.shape[0]
        grad_wide = grad_rows.astype(jnp.float32)
        column_sum = jnp.sum(grad_wide, axis=0)
        backward_grad_dense = contract_rows(context, grad_rows)
        backward_grad_down = contract_rows(activated, grad_rows)
        d_context = contract_cols(grad_rows, dense_mat).astype(jnp.bfloat16)
        d_act = contract_cols(grad_rows, down_mat)
        unused, slope_back = jax.vjp(exact_gelu, up_proj)
        d_up = slope_back(d_act)[0].astype(jnp.bfloat16)
        grad_up_add = jnp.sum(d_up.astype(jnp.float32), axis=0)
        backward_grad_up = contract_rows(h_mlp, d_up)
        d_hmlp = contract_cols(d_up, up_mat)
        blocked = (sub_blocks, MB, local_heads, HD)
        queries_b = queries.reshape(blocked)
        keys_b = keys_rot.reshape(blocked)
        scores = (
            jnp.einsum("bqhd,bkhd->bhqk", queries_b, keys_b, preferred_element_type=jnp.float32)
            * score_scale
        )
        scores = jnp.where(allowed_keys(segment)[:, None], scores, MASKED)
        weights_soft = jnp.exp(scores - log_total)
        d_context3 = d_context.reshape(blocked)
        d_values = jnp.einsum(
            "bhqk,bqhd->bkhd",
            weights_soft.astype(jnp.bfloat16),
            d_context3,
            preferred_element_type=jnp.float32,
        ).astype(jnp.bfloat16)
        d_weights = jnp.einsum(
            "bqhd,bkhd->bhqk", d_context3, values.reshape(blocked), preferred_element_type=jnp.float32
        )
        row_delta = jnp.sum(weights_soft * d_weights, axis=3, keepdims=True)
        d_scores = (weights_soft * (d_weights - row_delta)).astype(jnp.bfloat16)
        heads_shape = (block_len, local_heads, HD)
        d_queries = (
            jnp.einsum("bhqk,bkhd->bqhd", d_scores, keys_b, preferred_element_type=jnp.float32)
            * score_scale
        ).reshape(heads_shape)
        d_keys = (
            jnp.einsum("bhqk,bqhd->bkhd", d_scores, queries_b, preferred_element_type=jnp.float32)
            * score_scale
        ).reshape(heads_shape)
        d_queries = (
            rotate_back(d_queries, cosv, sinv).reshape(block_len, local_width).astype(jnp.bfloat16)
        )
        d_keys = (
            rotate_back(d_keys, cosv, sinv).reshape(block_len, local_width).astype(jnp.bfloat16)
        )
        d_joined = jnp.concatenate(
            [d_queries, d_keys, d_values.reshape(block_len, local_width)], axis=1
        )
        grad_joined_add = jnp.sum(d_joined.astype(jnp.float32), axis=0)
        backward_grad_joined = contract_rows(d_joined, h_attn)
        d_hattn = contract_cols(d_joined, joined_mat)
        d_both = tensor_sum(
            jnp.concatenate([d_hattn, d_hmlp], axis=1).astype(jnp.bfloat16)
        )
        d_hattn, d_hmlp = d_both[:, :model_width], d_both[:, model_width:]
        grad_gains = jnp.concatenate(
            [jnp.sum(d_hattn * normed, axis=0), jnp.sum(d_hmlp * normed, axis=0)]
        )
        grad_shifts = jnp.concatenate([jnp.sum(d_hattn, axis=0), jnp.sum(d_hmlp, axis=0)])
        d_norm = d_hattn * ln_gains[0] + d_hmlp * ln_gains[1]
        grad_input = grad_wide + inv_scale * (
            d_norm
            - jnp.mean(d_norm, axis=1, keepdims=True)
            - normed * jnp.mean(d_norm * normed, axis=1, keepdims=True)
        )
        small_terms = jnp.concatenate(
            [grad_gains, grad_shifts, column_sum, column_sum, grad_joined_add, grad_up_add]
        )
        terms = (
            backward_grad_joined[None],
            backward_grad_dense[None],
            backward_grad_up[None],
            backward_grad_down[None],
            small_terms[None],
        )
        grad_input, terms = (grad_input, terms)
        grad_low = grad_input.astype(jnp.bfloat16)
        tick_grads.append(grad_low)
        if totals is None:
            totals = terms
        else:
            totals = jax.tree.map(lambda older, newer: older + newer, totals, terms)
        if section_tick < NMB:
            returned = passed_along(grad_low, "pipe", -1)
    small_rows = totals[4][0]
    small_pad = (-small_rows.shape[0]) % model_width
    small_rows = jnp.pad(small_rows, (0, small_pad)).reshape(-1, model_width)
    pieces = (totals[0][0], totals[1][0], totals[2][0], totals[3][0], small_rows)
    slab = jnp.concatenate([piece.astype(jnp.bfloat16) for piece in pieces], axis=0)
    slab = lax.psum(slab, "dp").astype(jnp.float32)
    summed = []
    offset = 0
    for piece in pieces:
        summed.append(slab[offset : offset + piece.shape[0]])
        offset = offset + piece.shape[0]
    grad_rows_all = jnp.concatenate(
        [jnp.where(leading, tick_grads[block + 1], tick_grads[block]) for block in range(NMB)],
        axis=0,
    )
    input_grad = lax.dynamic_slice_in_dim(grad_rows_all, column_start, quarter, 1)[None]
    grad_joined = summed[0].T.reshape(1, model_width, 3, local_width)
    grad_dense = summed[1][None]
    grad_up = summed[2][None]
    grad_down = summed[3][None]
    small_sum = summed[4].reshape(-1)
    offset = 0
    grad_ln_gain = small_sum[offset : offset + 2 * model_width].reshape(1, 2, model_width)
    offset = offset + 2 * model_width
    grad_ln_bias = small_sum[offset : offset + 2 * model_width].reshape(1, 2, model_width)
    offset = offset + 2 * model_width
    grad_output_bias = small_sum[offset : offset + 2 * model_width].reshape(1, 2, model_width)
    offset = offset + 2 * model_width
    grad_joined_bias = small_sum[offset : offset + 3 * local_width].reshape(1, 3, local_width)
    offset = offset + 3 * local_width
    grad_up_bias = small_sum[offset : offset + hidden_local].reshape(1, hidden_local)
    return (
        section_out,
        input_grad,
        grad_ln_gain,
        grad_ln_bias,
        grad_joined,
        grad_joined_bias,
        grad_dense,
        grad_up,
        grad_up_bias,
        grad_down,
        grad_output_bias,
    )


def solution(mesh):
    placed = (
        P("dp", "tensor"),
        P("dp", None),
        P("pipe", None, None),
        P("pipe", None, None),
        P("pipe", None, None, "tensor"),
        P("pipe", None, "tensor"),
        P("pipe", "tensor", None),
        P("pipe", None, "tensor"),
        P("pipe", "tensor"),
        P("pipe", "tensor", None),
        P("pipe", None, None),
        P("dp", "tensor"),
    )
    return jax.shard_map(
        per_device,
        mesh=mesh,
        in_specs=placed,
        out_specs=(
            P("pipe", "dp", "tensor"),
            P("pipe", "dp", "tensor"),
            P("pipe", None, None),
            P("pipe", None, None),
            P("pipe", None, None, "tensor"),
            P("pipe", None, "tensor"),
            P("pipe", "tensor", None),
            P("pipe", None, "tensor"),
            P("pipe", "tensor"),
            P("pipe", "tensor", None),
            P("pipe", None, None),
        ),
        check_vma=False,
    )
```

```python
import jax
import jax.numpy as jnp
from jax import lax
from jax.sharding import PartitionSpec as P

HD = 64
ROT = 16
MB = 128
NMB = 1


EPSILON = 1e-05
MASKED = -1e30


def passed_along(x, axis, by):
    peers = lax.axis_size(axis)
    pairs = [(i, i + by) for i in range(peers) if 0 <= i + by < peers]
    return lax.ppermute(x, axis, pairs)


def tensor_pieces(x):
    peers = lax.axis_size("tensor")
    me = lax.axis_index("tensor")
    parts = [x]
    for shift in range(1, peers):
        pairs = [(i, (i + shift) % peers) for i in range(peers)]
        parts.append(lax.ppermute(x, "tensor", pairs))
    ordered = []
    for owner in range(peers):
        slot = (me - owner) % peers
        chosen = parts[peers - 1]
        for k in range(peers - 2, -1, -1):
            chosen = jnp.where(slot == k, parts[k], chosen)
        ordered.append(chosen)
    return ordered


def tensor_sum(x):
    pieces = tensor_pieces(x)
    total = pieces[0].astype(jnp.float32)
    for piece in pieces[1:]:
        total = total + piece.astype(jnp.float32)
    return total

def as_sent(x):
    return jax.tree.map(lambda a: a.astype(jnp.bfloat16) if a.dtype == jnp.float32 else a, x)


def positions(lengths, block_rows):
    seq_count = lengths.shape[1]
    counter = jnp.arange(seq_count, dtype=jnp.int32)
    lower_tri = (counter[:, None] >= counter[None, :]).astype(jnp.int32)
    seg_ends = jnp.sum(lengths[:, None, :] * lower_tri[None, :, :], axis=2)
    starts = seg_ends - lengths
    row_index = jnp.arange(block_rows, dtype=jnp.int32)
    segment = jnp.sum((row_index[None, :, None] >= seg_ends[:, None, :]).astype(jnp.int32), axis=2)
    member = (segment[:, :, None] == counter[None, None, :]).astype(jnp.int32)
    place = row_index[None, :] - jnp.sum(member * starts[:, None, :], axis=2)
    return (segment, place)


def rotary(place):
    half_rot = ROT // 2
    inv_freq = jnp.power(10000.0, -2.0 * jnp.arange(half_rot, dtype=jnp.float32) / ROT)
    angles = place.astype(jnp.float32)[..., None] * inv_freq
    return (jnp.cos(angles), jnp.sin(angles))


def rotate(heads_in, cosv, sinv):
    half_rot = ROT // 2
    first_half = heads_in[..., :half_rot]
    second_half = heads_in[..., half_rot:ROT]
    cos_rows = cosv[:, None, :]
    sin_rows = sinv[:, None, :]
    return jnp.concatenate(
        [
            first_half * cos_rows - second_half * sin_rows,
            second_half * cos_rows + first_half * sin_rows,
            heads_in[..., ROT:],
        ],
        axis=-1,
    )


def rotate_back(heads_in, cosv, sinv):
    half_rot = ROT // 2
    first_half = heads_in[..., :half_rot]
    second_half = heads_in[..., half_rot:ROT]
    cos_rows = cosv[:, None, :]
    sin_rows = sinv[:, None, :]
    return jnp.concatenate(
        [
            first_half * cos_rows + second_half * sin_rows,
            second_half * cos_rows - first_half * sin_rows,
            heads_in[..., ROT:],
        ],
        axis=-1,
    )


def exact_gelu(values):
    return jax.nn.gelu(values, approximate=False)


def allowed_keys(segment):
    row_index = jnp.arange(segment.shape[-1], dtype=jnp.int32)
    same = segment[..., :, None] == segment[..., None, :]
    return same & (row_index[None, :] <= row_index[:, None])


def contract_rows(left, right):
    return lax.dot_general(
        left, right, (((0,), (0,)), ((), ())), preferred_element_type=jnp.float32
    )


def contract_cols(left, right):
    return lax.dot_general(
        left, right, (((1,), (1,)), ((), ())), preferred_element_type=jnp.float32
    )


def per_device(
    tokens,
    lengths,
    ln_gain,
    ln_bias,
    joined_weight,
    joined_bias,
    dense_weight,
    up_weight,
    up_bias,
    down_weight,
    output_bias,
    cotangent,
):
    leading = lax.axis_index("pipe") == 0
    model_width = joined_weight.shape[1]
    local_width = joined_weight.shape[3]
    local_heads = local_width // HD
    hidden_local = up_weight.shape[2]
    quarter = tokens.shape[1]
    score_scale = HD ** (-0.5)
    ln_gains = ln_gain[0].astype(jnp.float32)
    ln_shifts = ln_bias[0].astype(jnp.float32)
    joined_mat = joined_weight[0].reshape(model_width, 3 * local_width)
    joined_add = joined_bias[0].astype(jnp.float32).reshape(3 * local_width)
    dense_mat = dense_weight[0]
    up_mat = up_weight[0]
    up_add = up_bias[0].astype(jnp.float32)
    down_mat = down_weight[0]
    bias_sum = output_bias[0, 0].astype(jnp.float32) + output_bias[0, 1].astype(jnp.float32)
    gathered_pieces = tensor_pieces(jnp.concatenate([tokens, cotangent], axis=0))
    gathered_rows = jnp.concatenate(gathered_pieces, axis=1)
    input_rows = gathered_rows[: tokens.shape[0]]
    output_grads = gathered_rows[tokens.shape[0] :]
    tick_rows = tokens.shape[0] // NMB
    sub_blocks = tick_rows // MB
    segment_all, place_all = positions(lengths, MB)
    cos_all, sin_all = rotary(place_all)
    segment_all = segment_all.reshape(NMB, sub_blocks, MB)
    cos_all = cos_all.reshape(NMB, tick_rows, cos_all.shape[-1])
    sin_all = sin_all.reshape(NMB, tick_rows, sin_all.shape[-1])

    def pick(early_val, late_val):
        return jax.tree.map(
            lambda upper_val, lower_val: jnp.where(leading, upper_val, lower_val),
            early_val,
            late_val,
        )

    received = jnp.zeros((tick_rows, model_width), jnp.bfloat16)
    tick_outputs = []
    tick_stored = []
    for section_tick in range(NMB + 1):
        early_block = min(section_tick, NMB - 1)
        late_block = max(section_tick - 1, 0)
        block_rows = jnp.where(
            leading, input_rows[early_block * tick_rows : (early_block + 1) * tick_rows], received
        )
        segment, cosv, sinv = pick(
            (segment_all[early_block], cos_all[early_block], sin_all[early_block]),
            (segment_all[late_block], cos_all[late_block], sin_all[late_block]),
        )
        inputs = block_rows.astype(jnp.float32)
        row_mean = jnp.mean(inputs, axis=1, keepdims=True)
        centred = inputs - row_mean
        forward_inv_scale = lax.rsqrt(jnp.mean(centred * centred, axis=1, keepdims=True) + EPSILON)
        forward_normed = centred * forward_inv_scale
        forward_h_attn = (forward_normed * ln_gains[0] + ln_shifts[0]).astype(jnp.bfloat16)
        forward_h_mlp = (forward_normed * ln_gains[1] + ln_shifts[1]).astype(jnp.bfloat16)
        joined_proj = (
            jnp.dot(forward_h_attn, joined_mat, preferred_element_type=jnp.float32) + joined_add
        )
        forward_block_len = block_rows.shape[0]
        forward_queries = rotate(
            joined_proj[:, :local_width].reshape(forward_block_len, local_heads, HD), cosv, sinv
        ).astype(jnp.bfloat16)
        forward_keys_rot = rotate(
            joined_proj[:, local_width : 2 * local_width].reshape(
                forward_block_len, local_heads, HD
            ),
            cosv,
            sinv,
        ).astype(jnp.bfloat16)
        forward_values = (
            joined_proj[:, 2 * local_width :]
            .reshape(forward_block_len, local_heads, HD)
            .astype(jnp.bfloat16)
        )
        blocked = (sub_blocks, MB, local_heads, HD)
        forward_scores = (
            jnp.einsum(
                "bqhd,bkhd->bhqk",
                forward_queries.reshape(blocked),
                forward_keys_rot.reshape(blocked),
                preferred_element_type=jnp.float32,
            )
            * score_scale
        )
        forward_scores = jnp.where(allowed_keys(segment)[:, None], forward_scores, MASKED)
        row_top = jnp.max(forward_scores, axis=3, keepdims=True)
        exponent = jnp.exp(forward_scores - row_top)
        row_total = jnp.sum(exponent, axis=3, keepdims=True)
        forward_log_total = row_top + jnp.log(row_total)
        weights_low = (exponent / row_total).astype(jnp.bfloat16)
        forward_context = jnp.einsum(
            "bhqk,bkhd->bqhd",
            weights_low,
            forward_values.reshape(blocked),
            preferred_element_type=jnp.float32,
        )
        forward_context = forward_context.reshape(forward_block_len, local_width).astype(
            jnp.bfloat16
        )
        forward_up_proj = (
            jnp.dot(forward_h_mlp, up_mat, preferred_element_type=jnp.float32) + up_add
        )
        forward_activated = exact_gelu(forward_up_proj).astype(jnp.bfloat16)
        partial_value = jnp.dot(forward_context, dense_mat, preferred_element_type=jnp.float32)
        partial_value = partial_value + jnp.dot(
            forward_activated, down_mat, preferred_element_type=jnp.float32
        )
        branches = tensor_sum(partial_value.astype(jnp.bfloat16))
        result = inputs + branches + bias_sum
        forward_stored = (
            forward_normed,
            forward_inv_scale,
            forward_h_attn,
            forward_h_mlp,
            forward_queries,
            forward_keys_rot,
            forward_values,
            forward_log_total,
            forward_context,
            forward_up_proj,
            forward_activated,
        )
        result, stored = (result, forward_stored)
        result_low = result.astype(jnp.bfloat16)
        tick_outputs.append(result_low)
        tick_stored.append((stored, segment, cosv, sinv))
        if section_tick < NMB:
            received = passed_along(result_low, "pipe", 1)
    column_start = lax.axis_index("tensor") * quarter
    section_rows = jnp.concatenate(
        [jnp.where(leading, tick_outputs[block], tick_outputs[block + 1]) for block in range(NMB)],
        axis=0,
    )
    section_out = lax.dynamic_slice_in_dim(section_rows, column_start, quarter, 1)[None]
    returned = jnp.zeros((tick_rows, model_width), jnp.bfloat16)
    tick_grads = []
    totals = None
    for section_tick in range(NMB + 1):
        own_block = min(section_tick, NMB - 1)
        late_tick = max(section_tick - 1, 0)
        upper_tick = min(section_tick + 1, NMB)
        from_output = output_grads[own_block * tick_rows : (own_block + 1) * tick_rows]
        if section_tick == NMB:
            from_output = jnp.zeros_like(from_output)
        grad_rows = jnp.where(leading, returned, from_output)
        stored, segment, cosv, sinv = pick(tick_stored[late_tick], tick_stored[upper_tick])
        (
            normed,
            inv_scale,
            h_attn,
            h_mlp,
            queries,
            keys_rot,
            values,
            log_total,
            context,
            up_proj,
            activated,
        ) = stored
        block_len = grad_rows.shape[0]
        grad_wide = grad_rows.astype(jnp.float32)
        column_sum = jnp.sum(grad_wide, axis=0)
        backward_grad_dense = contract_rows(context, grad_rows)
        backward_grad_down = contract_rows(activated, grad_rows)
        d_context = contract_cols(grad_rows, dense_mat).astype(jnp.bfloat16)
        d_act = contract_cols(grad_rows, down_mat)
        unused, slope_back = jax.vjp(exact_gelu, up_proj)
        d_up = slope_back(d_act)[0].astype(jnp.bfloat16)
        grad_up_add = jnp.sum(d_up.astype(jnp.float32), axis=0)
        backward_grad_up = contract_rows(h_mlp, d_up)
        d_hmlp = contract_cols(d_up, up_mat)
        blocked = (sub_blocks, MB, local_heads, HD)
        queries_b = queries.reshape(blocked)
        keys_b = keys_rot.reshape(blocked)
        scores = (
            jnp.einsum("bqhd,bkhd->bhqk", queries_b, keys_b, preferred_element_type=jnp.float32)
            * score_scale
        )
        scores = jnp.where(allowed_keys(segment)[:, None], scores, MASKED)
        weights_soft = jnp.exp(scores - log_total)
        d_context3 = d_context.reshape(blocked)
        d_values = jnp.einsum(
            "bhqk,bqhd->bkhd",
            weights_soft.astype(jnp.bfloat16),
            d_context3,
            preferred_element_type=jnp.float32,
        ).astype(jnp.bfloat16)
        d_weights = jnp.einsum(
            "bqhd,bkhd->bhqk", d_context3, values.reshape(blocked), preferred_element_type=jnp.float32
        )
        row_delta = jnp.sum(weights_soft * d_weights, axis=3, keepdims=True)
        d_scores = (weights_soft * (d_weights - row_delta)).astype(jnp.bfloat16)
        heads_shape = (block_len, local_heads, HD)
        d_queries = (
            jnp.einsum("bhqk,bkhd->bqhd", d_scores, keys_b, preferred_element_type=jnp.float32)
            * score_scale
        ).reshape(heads_shape)
        d_keys = (
            jnp.einsum("bhqk,bqhd->bkhd", d_scores, queries_b, preferred_element_type=jnp.float32)
            * score_scale
        ).reshape(heads_shape)
        d_queries = (
            rotate_back(d_queries, cosv, sinv).reshape(block_len, local_width).astype(jnp.bfloat16)
        )
        d_keys = (
            rotate_back(d_keys, cosv, sinv).reshape(block_len, local_width).astype(jnp.bfloat16)
        )
        d_joined = jnp.concatenate(
            [d_queries, d_keys, d_values.reshape(block_len, local_width)], axis=1
        )
        grad_joined_add = jnp.sum(d_joined.astype(jnp.float32), axis=0)
        backward_grad_joined = contract_rows(d_joined, h_attn)
        d_hattn = contract_cols(d_joined, joined_mat)
        d_both = tensor_sum(
            jnp.concatenate([d_hattn, d_hmlp], axis=1).astype(jnp.bfloat16)
        )
        d_hattn, d_hmlp = d_both[:, :model_width], d_both[:, model_width:]
        grad_gains = jnp.concatenate(
            [jnp.sum(d_hattn * normed, axis=0), jnp.sum(d_hmlp * normed, axis=0)]
        )
        grad_shifts = jnp.concatenate([jnp.sum(d_hattn, axis=0), jnp.sum(d_hmlp, axis=0)])
        d_norm = d_hattn * ln_gains[0] + d_hmlp * ln_gains[1]
        grad_input = grad_wide + inv_scale * (
            d_norm
            - jnp.mean(d_norm, axis=1, keepdims=True)
            - normed * jnp.mean(d_norm * normed, axis=1, keepdims=True)
        )
        small_terms = jnp.concatenate(
            [grad_gains, grad_shifts, column_sum, column_sum, grad_joined_add, grad_up_add]
        )
        terms = (
            backward_grad_joined[None],
            backward_grad_dense[None],
            backward_grad_up[None],
            backward_grad_down[None],
            small_terms[None],
        )
        grad_input, terms = (grad_input, terms)
        grad_low = grad_input.astype(jnp.bfloat16)
        tick_grads.append(grad_low)
        if totals is None:
            totals = terms
        else:
            totals = jax.tree.map(lambda older, newer: older + newer, totals, terms)
        if section_tick < NMB:
            returned = passed_along(grad_low, "pipe", -1)
    small_rows = totals[4][0]
    small_pad = (-small_rows.shape[0]) % model_width
    small_rows = jnp.pad(small_rows, (0, small_pad)).reshape(-1, model_width)
    pieces = (totals[0][0], totals[1][0], totals[2][0], totals[3][0], small_rows)
    slab = jnp.concatenate([piece.astype(jnp.bfloat16) for piece in pieces], axis=0)
    slab = lax.psum(slab, "dp").astype(jnp.float32)
    summed = []
    offset = 0
    for piece in pieces:
        summed.append(slab[offset : offset + piece.shape[0]])
        offset = offset + piece.shape[0]
    grad_rows_all = jnp.concatenate(
        [jnp.where(leading, tick_grads[block + 1], tick_grads[block]) for block in range(NMB)],
        axis=0,
    )
    input_grad = lax.dynamic_slice_in_dim(grad_rows_all, column_start, quarter, 1)[None]
    grad_joined = summed[0].T.reshape(1, model_width, 3, local_width)
    grad_dense = summed[1][None]
    grad_up = summed[2][None]
    grad_down = summed[3][None]
    small_sum = summed[4].reshape(-1)
    offset = 0
    grad_ln_gain = small_sum[offset : offset + 2 * model_width].reshape(1, 2, model_width)
    offset = offset + 2 * model_width
    grad_ln_bias = small_sum[offset : offset + 2 * model_width].reshape(1, 2, model_width)
    offset = offset + 2 * model_width
    grad_output_bias = small_sum[offset : offset + 2 * model_width].reshape(1, 2, model_width)
    offset = offset + 2 * model_width
    grad_joined_bias = small_sum[offset : offset + 3 * local_width].reshape(1, 3, local_width)
    offset = offset + 3 * local_width
    grad_up_bias = small_sum[offset : offset + hidden_local].reshape(1, hidden_local)
    return (
        section_out,
        input_grad,
        grad_ln_gain,
        grad_ln_bias,
        grad_joined,
        grad_joined_bias,
        grad_dense,
        grad_up,
        grad_up_bias,
        grad_down,
        grad_output_bias,
    )


def solution(mesh):
    placed = (
        P("dp", "tensor"),
        P("dp", None),
        P("pipe", None, None),
        P("pipe", None, None),
        P("pipe", None, None, "tensor"),
        P("pipe", None, "tensor"),
        P("pipe", "tensor", None),
        P("pipe", None, "tensor"),
        P("pipe", "tensor"),
        P("pipe", "tensor", None),
        P("pipe", None, None),
        P("dp", "tensor"),
    )
    return jax.shard_map(
        per_device,
        mesh=mesh,
        in_specs=placed,
        out_specs=(
            P("pipe", "dp", "tensor"),
            P("pipe", "dp", "tensor"),
            P("pipe", None, None),
            P("pipe", None, None),
            P("pipe", None, None, "tensor"),
            P("pipe", None, "tensor"),
            P("pipe", "tensor", None),
            P("pipe", None, "tensor"),
            P("pipe", "tensor"),
            P("pipe", "tensor", None),
            P("pipe", None, None),
        ),
        check_vma=False,
    )
```

```python
import jax
import jax.numpy as jnp
from jax import lax
from jax.sharding import PartitionSpec as P

HD = 64
ROT = 16
MB = 128
NMB = 2


EPSILON = 1e-05
MASKED = -1e30


def passed_along(x, axis, by):
    peers = lax.axis_size(axis)
    pairs = [(i, i + by) for i in range(peers) if 0 <= i + by < peers]
    return lax.ppermute(x, axis, pairs)


def tensor_pieces(x):
    peers = lax.axis_size("tensor")
    me = lax.axis_index("tensor")
    parts = [x]
    for shift in range(1, peers):
        pairs = [(i, (i + shift) % peers) for i in range(peers)]
        parts.append(lax.ppermute(x, "tensor", pairs))
    ordered = []
    for owner in range(peers):
        slot = (me - owner) % peers
        chosen = parts[peers - 1]
        for k in range(peers - 2, -1, -1):
            chosen = jnp.where(slot == k, parts[k], chosen)
        ordered.append(chosen)
    return ordered


def tensor_sum(x):
    pieces = tensor_pieces(x)
    total = pieces[0].astype(jnp.float32)
    for piece in pieces[1:]:
        total = total + piece.astype(jnp.float32)
    return total

def as_sent(x):
    return jax.tree.map(lambda a: a.astype(jnp.bfloat16) if a.dtype == jnp.float32 else a, x)


def positions(lengths, block_rows):
    seq_count = lengths.shape[1]
    counter = jnp.arange(seq_count, dtype=jnp.int32)
    lower_tri = (counter[:, None] >= counter[None, :]).astype(jnp.int32)
    seg_ends = jnp.sum(lengths[:, None, :] * lower_tri[None, :, :], axis=2)
    starts = seg_ends - lengths
    row_index = jnp.arange(block_rows, dtype=jnp.int32)
    segment = jnp.sum((row_index[None, :, None] >= seg_ends[:, None, :]).astype(jnp.int32), axis=2)
    member = (segment[:, :, None] == counter[None, None, :]).astype(jnp.int32)
    place = row_index[None, :] - jnp.sum(member * starts[:, None, :], axis=2)
    return (segment, place)


def rotary(place):
    half_rot = ROT // 2
    inv_freq = jnp.power(10000.0, -2.0 * jnp.arange(half_rot, dtype=jnp.float32) / ROT)
    angles = place.astype(jnp.float32)[..., None] * inv_freq
    return (jnp.cos(angles), jnp.sin(angles))


def rotate(heads_in, cosv, sinv):
    half_rot = ROT // 2
    first_half = heads_in[..., :half_rot]
    second_half = heads_in[..., half_rot:ROT]
    cos_rows = cosv[:, None, :]
    sin_rows = sinv[:, None, :]
    return jnp.concatenate(
        [
            first_half * cos_rows - second_half * sin_rows,
            second_half * cos_rows + first_half * sin_rows,
            heads_in[..., ROT:],
        ],
        axis=-1,
    )


def rotate_back(heads_in, cosv, sinv):
    half_rot = ROT // 2
    first_half = heads_in[..., :half_rot]
    second_half = heads_in[..., half_rot:ROT]
    cos_rows = cosv[:, None, :]
    sin_rows = sinv[:, None, :]
    return jnp.concatenate(
        [
            first_half * cos_rows + second_half * sin_rows,
            second_half * cos_rows - first_half * sin_rows,
            heads_in[..., ROT:],
        ],
        axis=-1,
    )


def exact_gelu(values):
    return jax.nn.gelu(values, approximate=False)


def allowed_keys(segment):
    row_index = jnp.arange(segment.shape[-1], dtype=jnp.int32)
    same = segment[..., :, None] == segment[..., None, :]
    return same & (row_index[None, :] <= row_index[:, None])


def contract_rows(left, right):
    return lax.dot_general(
        left, right, (((0,), (0,)), ((), ())), preferred_element_type=jnp.float32
    )


def contract_cols(left, right):
    return lax.dot_general(
        left, right, (((1,), (1,)), ((), ())), preferred_element_type=jnp.float32
    )


def per_device(
    tokens,
    lengths,
    ln_gain,
    ln_bias,
    joined_weight,
    joined_bias,
    dense_weight,
    up_weight,
    up_bias,
    down_weight,
    output_bias,
    cotangent,
):
    leading = lax.axis_index("pipe") == 0
    model_width = joined_weight.shape[1]
    local_width = joined_weight.shape[3]
    local_heads = local_width // HD
    hidden_local = up_weight.shape[2]
    quarter = tokens.shape[1]
    score_scale = HD ** (-0.5)
    ln_gains = ln_gain[0].astype(jnp.float32)
    ln_shifts = ln_bias[0].astype(jnp.float32)
    joined_mat = joined_weight[0].reshape(model_width, 3 * local_width)
    joined_add = joined_bias[0].astype(jnp.float32).reshape(3 * local_width)
    dense_mat = dense_weight[0]
    up_mat = up_weight[0]
    up_add = up_bias[0].astype(jnp.float32)
    down_mat = down_weight[0]
    bias_sum = output_bias[0, 0].astype(jnp.float32) + output_bias[0, 1].astype(jnp.float32)
    gathered_pieces = tensor_pieces(jnp.concatenate([tokens, cotangent], axis=0))
    gathered_rows = jnp.concatenate(gathered_pieces, axis=1)
    input_rows = gathered_rows[: tokens.shape[0]]
    output_grads = gathered_rows[tokens.shape[0] :]
    tick_rows = tokens.shape[0] // NMB
    sub_blocks = tick_rows // MB
    segment_all, place_all = positions(lengths, MB)
    cos_all, sin_all = rotary(place_all)
    segment_all = segment_all.reshape(NMB, sub_blocks, MB)
    cos_all = cos_all.reshape(NMB, tick_rows, cos_all.shape[-1])
    sin_all = sin_all.reshape(NMB, tick_rows, sin_all.shape[-1])

    def pick(early_val, late_val):
        return jax.tree.map(
            lambda upper_val, lower_val: jnp.where(leading, upper_val, lower_val),
            early_val,
            late_val,
        )

    received = jnp.zeros((tick_rows, model_width), jnp.bfloat16)
    tick_outputs = []
    tick_stored = []
    for section_tick in range(NMB + 1):
        early_block = min(section_tick, NMB - 1)
        late_block = max(section_tick - 1, 0)
        block_rows = jnp.where(
            leading, input_rows[early_block * tick_rows : (early_block + 1) * tick_rows], received
        )
        segment, cosv, sinv = pick(
            (segment_all[early_block], cos_all[early_block], sin_all[early_block]),
            (segment_all[late_block], cos_all[late_block], sin_all[late_block]),
        )
        inputs = block_rows.astype(jnp.float32)
        row_mean = jnp.mean(inputs, axis=1, keepdims=True)
        centred = inputs - row_mean
        forward_inv_scale = lax.rsqrt(jnp.mean(centred * centred, axis=1, keepdims=True) + EPSILON)
        forward_normed = centred * forward_inv_scale
        forward_h_attn = (forward_normed * ln_gains[0] + ln_shifts[0]).astype(jnp.bfloat16)
        forward_h_mlp = (forward_normed * ln_gains[1] + ln_shifts[1]).astype(jnp.bfloat16)
        joined_proj = (
            jnp.dot(forward_h_attn, joined_mat, preferred_element_type=jnp.float32) + joined_add
        )
        forward_block_len = block_rows.shape[0]
        forward_queries = rotate(
            joined_proj[:, :local_width].reshape(forward_block_len, local_heads, HD), cosv, sinv
        ).astype(jnp.bfloat16)
        forward_keys_rot = rotate(
            joined_proj[:, local_width : 2 * local_width].reshape(
                forward_block_len, local_heads, HD
            ),
            cosv,
            sinv,
        ).astype(jnp.bfloat16)
        forward_values = (
            joined_proj[:, 2 * local_width :]
            .reshape(forward_block_len, local_heads, HD)
            .astype(jnp.bfloat16)
        )
        blocked = (sub_blocks, MB, local_heads, HD)
        forward_scores = (
            jnp.einsum(
                "bqhd,bkhd->bhqk",
                forward_queries.reshape(blocked),
                forward_keys_rot.reshape(blocked),
                preferred_element_type=jnp.float32,
            )
            * score_scale
        )
        forward_scores = jnp.where(allowed_keys(segment)[:, None], forward_scores, MASKED)
        row_top = jnp.max(forward_scores, axis=3, keepdims=True)
        exponent = jnp.exp(forward_scores - row_top)
        row_total = jnp.sum(exponent, axis=3, keepdims=True)
        forward_log_total = row_top + jnp.log(row_total)
        weights_low = (exponent / row_total).astype(jnp.bfloat16)
        forward_context = jnp.einsum(
            "bhqk,bkhd->bqhd",
            weights_low,
            forward_values.reshape(blocked),
            preferred_element_type=jnp.float32,
        )
        forward_context = forward_context.reshape(forward_block_len, local_width).astype(
            jnp.bfloat16
        )
        forward_up_proj = (
            jnp.dot(forward_h_mlp, up_mat, preferred_element_type=jnp.float32) + up_add
        )
        forward_activated = exact_gelu(forward_up_proj).astype(jnp.bfloat16)
        partial_value = jnp.dot(forward_context, dense_mat, preferred_element_type=jnp.float32)
        partial_value = partial_value + jnp.dot(
            forward_activated, down_mat, preferred_element_type=jnp.float32
        )
        branches = tensor_sum(partial_value.astype(jnp.bfloat16))
        result = inputs + branches + bias_sum
        forward_stored = (
            forward_normed,
            forward_inv_scale,
            forward_h_attn,
            forward_h_mlp,
            forward_queries,
            forward_keys_rot,
            forward_values,
            forward_log_total,
            forward_context,
            forward_up_proj,
            forward_activated,
        )
        result, stored = (result, forward_stored)
        result_low = result.astype(jnp.bfloat16)
        tick_outputs.append(result_low)
        tick_stored.append((stored, segment, cosv, sinv))
        if section_tick < NMB:
            received = passed_along(result_low, "pipe", 1)
    column_start = lax.axis_index("tensor") * quarter
    section_rows = jnp.concatenate(
        [jnp.where(leading, tick_outputs[block], tick_outputs[block + 1]) for block in range(NMB)],
        axis=0,
    )
    section_out = lax.dynamic_slice_in_dim(section_rows, column_start, quarter, 1)[None]
    returned = jnp.zeros((tick_rows, model_width), jnp.bfloat16)
    tick_grads = []
    totals = None
    for section_tick in range(NMB + 1):
        own_block = min(section_tick, NMB - 1)
        late_tick = max(section_tick - 1, 0)
        upper_tick = min(section_tick + 1, NMB)
        from_output = output_grads[own_block * tick_rows : (own_block + 1) * tick_rows]
        if section_tick == NMB:
            from_output = jnp.zeros_like(from_output)
        grad_rows = jnp.where(leading, returned, from_output)
        stored, segment, cosv, sinv = pick(tick_stored[late_tick], tick_stored[upper_tick])
        (
            normed,
            inv_scale,
            h_attn,
            h_mlp,
            queries,
            keys_rot,
            values,
            log_total,
            context,
            up_proj,
            activated,
        ) = stored
        block_len = grad_rows.shape[0]
        grad_wide = grad_rows.astype(jnp.float32)
        column_sum = jnp.sum(grad_wide, axis=0)
        backward_grad_dense = contract_rows(context, grad_rows)
        backward_grad_down = contract_rows(activated, grad_rows)
        d_context = contract_cols(grad_rows, dense_mat).astype(jnp.bfloat16)
        d_act = contract_cols(grad_rows, down_mat)
        unused, slope_back = jax.vjp(exact_gelu, up_proj)
        d_up = slope_back(d_act)[0].astype(jnp.bfloat16)
        grad_up_add = jnp.sum(d_up.astype(jnp.float32), axis=0)
        backward_grad_up = contract_rows(h_mlp, d_up)
        d_hmlp = contract_cols(d_up, up_mat)
        blocked = (sub_blocks, MB, local_heads, HD)
        queries_b = queries.reshape(blocked)
        keys_b = keys_rot.reshape(blocked)
        scores = (
            jnp.einsum("bqhd,bkhd->bhqk", queries_b, keys_b, preferred_element_type=jnp.float32)
            * score_scale
        )
        scores = jnp.where(allowed_keys(segment)[:, None], scores, MASKED)
        weights_soft = jnp.exp(scores - log_total)
        d_context3 = d_context.reshape(blocked)
        d_values = jnp.einsum(
            "bhqk,bqhd->bkhd",
            weights_soft.astype(jnp.bfloat16),
            d_context3,
            preferred_element_type=jnp.float32,
        ).astype(jnp.bfloat16)
        d_weights = jnp.einsum(
            "bqhd,bkhd->bhqk", d_context3, values.reshape(blocked), preferred_element_type=jnp.float32
        )
        row_delta = jnp.sum(weights_soft * d_weights, axis=3, keepdims=True)
        d_scores = (weights_soft * (d_weights - row_delta)).astype(jnp.bfloat16)
        heads_shape = (block_len, local_heads, HD)
        d_queries = (
            jnp.einsum("bhqk,bkhd->bqhd", d_scores, keys_b, preferred_element_type=jnp.float32)
            * score_scale
        ).reshape(heads_shape)
        d_keys = (
            jnp.einsum("bhqk,bqhd->bkhd", d_scores, queries_b, preferred_element_type=jnp.float32)
            * score_scale
        ).reshape(heads_shape)
        d_queries = (
            rotate_back(d_queries, cosv, sinv).reshape(block_len, local_width).astype(jnp.bfloat16)
        )
        d_keys = (
            rotate_back(d_keys, cosv, sinv).reshape(block_len, local_width).astype(jnp.bfloat16)
        )
        d_joined = jnp.concatenate(
            [d_queries, d_keys, d_values.reshape(block_len, local_width)], axis=1
        )
        grad_joined_add = jnp.sum(d_joined.astype(jnp.float32), axis=0)
        backward_grad_joined = contract_rows(d_joined, h_attn)
        d_hattn = contract_cols(d_joined, joined_mat)
        grad_gains = jnp.concatenate(
            [jnp.sum(d_hattn * normed, axis=0), jnp.sum(d_hmlp * normed, axis=0)]
        )
        grad_shifts = jnp.concatenate([jnp.sum(d_hattn, axis=0), jnp.sum(d_hmlp, axis=0)])
        d_norm = tensor_sum((d_hattn * ln_gains[0] + d_hmlp * ln_gains[1]).astype(jnp.bfloat16))
        grad_input = grad_wide + inv_scale * (
            d_norm
            - jnp.mean(d_norm, axis=1, keepdims=True)
            - normed * jnp.mean(d_norm * normed, axis=1, keepdims=True)
        )
        small_terms = jnp.concatenate(
            [grad_gains, grad_shifts, column_sum, column_sum, grad_joined_add, grad_up_add]
        )
        terms = (
            backward_grad_joined[None],
            backward_grad_dense[None],
            backward_grad_up[None],
            backward_grad_down[None],
            small_terms[None],
        )
        grad_input, terms = (grad_input, terms)
        grad_low = grad_input.astype(jnp.bfloat16)
        tick_grads.append(grad_low)
        if totals is None:
            totals = terms
        else:
            totals = jax.tree.map(lambda older, newer: older + newer, totals, terms)
        if section_tick < NMB:
            returned = passed_along(grad_low, "pipe", -1)
    small_rows = totals[4][0]
    small_pad = (-small_rows.shape[0]) % model_width
    small_rows = jnp.pad(small_rows, (0, small_pad)).reshape(-1, model_width)
    pieces = (totals[0][0], totals[1][0], totals[2][0], totals[3][0], small_rows)
    slab = jnp.concatenate([piece.astype(jnp.bfloat16) for piece in pieces], axis=0)
    slab = lax.psum(slab, "dp").astype(jnp.float32)
    summed = []
    offset = 0
    for piece in pieces:
        summed.append(slab[offset : offset + piece.shape[0]])
        offset = offset + piece.shape[0]
    grad_rows_all = jnp.concatenate(
        [jnp.where(leading, tick_grads[block + 1], tick_grads[block]) for block in range(NMB)],
        axis=0,
    )
    input_grad = lax.dynamic_slice_in_dim(grad_rows_all, column_start, quarter, 1)[None]
    grad_joined = summed[0].T.reshape(1, model_width, 3, local_width)
    grad_dense = summed[1][None]
    grad_up = summed[2][None]
    grad_down = summed[3][None]
    small_sum = summed[4].reshape(-1)
    ln_sum = tensor_sum(small_sum[: 4 * model_width])
    grad_ln_gain = ln_sum[: 2 * model_width].reshape(1, 2, model_width)
    grad_ln_bias = ln_sum[2 * model_width :].reshape(1, 2, model_width)
    offset = 4 * model_width
    grad_output_bias = small_sum[offset : offset + 2 * model_width].reshape(1, 2, model_width)
    offset = offset + 2 * model_width
    grad_joined_bias = small_sum[offset : offset + 3 * local_width].reshape(1, 3, local_width)
    offset = offset + 3 * local_width
    grad_up_bias = small_sum[offset : offset + hidden_local].reshape(1, hidden_local)
    return (
        section_out,
        input_grad,
        grad_ln_gain,
        grad_ln_bias,
        grad_joined,
        grad_joined_bias,
        grad_dense,
        grad_up,
        grad_up_bias,
        grad_down,
        grad_output_bias,
    )


def solution(mesh):
    placed = (
        P("dp", "tensor"),
        P("dp", None),
        P("pipe", None, None),
        P("pipe", None, None),
        P("pipe", None, None, "tensor"),
        P("pipe", None, "tensor"),
        P("pipe", "tensor", None),
        P("pipe", None, "tensor"),
        P("pipe", "tensor"),
        P("pipe", "tensor", None),
        P("pipe", None, None),
        P("dp", "tensor"),
    )
    return jax.shard_map(
        per_device,
        mesh=mesh,
        in_specs=placed,
        out_specs=(
            P("pipe", "dp", "tensor"),
            P("pipe", "dp", "tensor"),
            P("pipe", None, None),
            P("pipe", None, None),
            P("pipe", None, None, "tensor"),
            P("pipe", None, "tensor"),
            P("pipe", "tensor", None),
            P("pipe", None, "tensor"),
            P("pipe", "tensor"),
            P("pipe", "tensor", None),
            P("pipe", None, None),
        ),
        check_vma=False,
    )
```

```python
import jax
import jax.numpy as jnp
from jax import lax
from jax.sharding import PartitionSpec as P

HD = 64
ROT = 16
MB = 128
NMB = 2


EPSILON = 1e-05
MASKED = -1e30


def passed_along(x, axis, by):
    peers = lax.axis_size(axis)
    pairs = [(i, i + by) for i in range(peers) if 0 <= i + by < peers]
    return lax.ppermute(x, axis, pairs)


def tensor_pieces(x):
    peers = lax.axis_size("tensor")
    me = lax.axis_index("tensor")
    parts = [x]
    for shift in range(1, peers):
        pairs = [(i, (i + shift) % peers) for i in range(peers)]
        parts.append(lax.ppermute(x, "tensor", pairs))
    ordered = []
    for owner in range(peers):
        slot = (me - owner) % peers
        chosen = parts[peers - 1]
        for k in range(peers - 2, -1, -1):
            chosen = jnp.where(slot == k, parts[k], chosen)
        ordered.append(chosen)
    return ordered


def tensor_sum(x):
    pieces = tensor_pieces(x)
    total = pieces[0].astype(jnp.float32)
    for piece in pieces[1:]:
        total = total + piece.astype(jnp.float32)
    return total

def ordered_by_owner(parts, me, peers):
    ordered = []
    for owner in range(peers):
        slot = (me - owner) % peers
        chosen = parts[peers - 1]
        for k in range(peers - 2, -1, -1):
            chosen = jnp.where(slot == k, parts[k], chosen)
        ordered.append(chosen)
    return ordered


def tensor_scatter_sum(x):
    peers = lax.axis_size("tensor")
    me = lax.axis_index("tensor")
    width = x.shape[1] // peers

    def piece_for(owner):
        return lax.dynamic_slice_in_dim(x, owner * width, width, 1)

    parts = [piece_for(me)]
    for shift in range(1, peers):
        pairs = [(i, (i + shift) % peers) for i in range(peers)]
        parts.append(lax.ppermute(piece_for((me + shift) % peers), "tensor", pairs))
    ordered = ordered_by_owner(parts, me, peers)
    total = ordered[0].astype(jnp.float32)
    for piece in ordered[1:]:
        total = total + piece.astype(jnp.float32)
    return total


def cross_gather(x, source_stage):
    peers = lax.axis_size("tensor")
    me = lax.axis_index("tensor")
    target_stage = 1 - source_stage
    parts = []
    for shift in range(peers):
        pairs = [
            (source_stage * peers + i, target_stage * peers + (i + shift) % peers)
            for i in range(peers)
        ]
        parts.append(lax.ppermute(x, ("pipe", "tensor"), pairs))
    return jnp.concatenate(ordered_by_owner(parts, me, peers), axis=1)


def as_sent(x):
    return jax.tree.map(lambda a: a.astype(jnp.bfloat16) if a.dtype == jnp.float32 else a, x)


def positions(lengths, block_rows):
    seq_count = lengths.shape[1]
    counter = jnp.arange(seq_count, dtype=jnp.int32)
    lower_tri = (counter[:, None] >= counter[None, :]).astype(jnp.int32)
    seg_ends = jnp.sum(lengths[:, None, :] * lower_tri[None, :, :], axis=2)
    starts = seg_ends - lengths
    row_index = jnp.arange(block_rows, dtype=jnp.int32)
    segment = jnp.sum((row_index[None, :, None] >= seg_ends[:, None, :]).astype(jnp.int32), axis=2)
    member = (segment[:, :, None] == counter[None, None, :]).astype(jnp.int32)
    place = row_index[None, :] - jnp.sum(member * starts[:, None, :], axis=2)
    return (segment, place)


def rotary(place):
    half_rot = ROT // 2
    inv_freq = jnp.power(10000.0, -2.0 * jnp.arange(half_rot, dtype=jnp.float32) / ROT)
    angles = place.astype(jnp.float32)[..., None] * inv_freq
    return (jnp.cos(angles), jnp.sin(angles))


def rotate(heads_in, cosv, sinv):
    half_rot = ROT // 2
    first_half = heads_in[..., :half_rot]
    second_half = heads_in[..., half_rot:ROT]
    cos_rows = cosv[:, None, :]
    sin_rows = sinv[:, None, :]
    return jnp.concatenate(
        [
            first_half * cos_rows - second_half * sin_rows,
            second_half * cos_rows + first_half * sin_rows,
            heads_in[..., ROT:],
        ],
        axis=-1,
    )


def rotate_back(heads_in, cosv, sinv):
    half_rot = ROT // 2
    first_half = heads_in[..., :half_rot]
    second_half = heads_in[..., half_rot:ROT]
    cos_rows = cosv[:, None, :]
    sin_rows = sinv[:, None, :]
    return jnp.concatenate(
        [
            first_half * cos_rows + second_half * sin_rows,
            second_half * cos_rows - first_half * sin_rows,
            heads_in[..., ROT:],
        ],
        axis=-1,
    )


def exact_gelu(values):
    return jax.nn.gelu(values, approximate=False)


def allowed_keys(segment):
    row_index = jnp.arange(segment.shape[-1], dtype=jnp.int32)
    same = segment[..., :, None] == segment[..., None, :]
    return same & (row_index[None, :] <= row_index[:, None])


def contract_rows(left, right):
    return lax.dot_general(
        left, right, (((0,), (0,)), ((), ())), preferred_element_type=jnp.float32
    )


def contract_cols(left, right):
    return lax.dot_general(
        left, right, (((1,), (1,)), ((), ())), preferred_element_type=jnp.float32
    )


def per_device(
    tokens,
    lengths,
    ln_gain,
    ln_bias,
    joined_weight,
    joined_bias,
    dense_weight,
    up_weight,
    up_bias,
    down_weight,
    output_bias,
    cotangent,
):
    leading = lax.axis_index("pipe") == 0
    model_width = joined_weight.shape[1]
    local_width = joined_weight.shape[3]
    local_heads = local_width // HD
    hidden_local = up_weight.shape[2]
    quarter = tokens.shape[1]
    score_scale = HD ** (-0.5)
    ln_gains = ln_gain[0].astype(jnp.float32)
    ln_shifts = ln_bias[0].astype(jnp.float32)
    joined_mat = joined_weight[0].reshape(model_width, 3 * local_width)
    joined_add = joined_bias[0].astype(jnp.float32).reshape(3 * local_width)
    dense_mat = dense_weight[0]
    up_mat = up_weight[0]
    up_add = up_bias[0].astype(jnp.float32)
    down_mat = down_weight[0]
    bias_sum = output_bias[0, 0].astype(jnp.float32) + output_bias[0, 1].astype(jnp.float32)
    gathered_pieces = tensor_pieces(jnp.concatenate([tokens, cotangent], axis=0))
    gathered_rows = jnp.concatenate(gathered_pieces, axis=1)
    input_rows = gathered_rows[: tokens.shape[0]]
    output_grads = gathered_rows[tokens.shape[0] :]
    tick_rows = tokens.shape[0] // NMB
    sub_blocks = tick_rows // MB
    segment_all, place_all = positions(lengths, MB)
    cos_all, sin_all = rotary(place_all)
    segment_all = segment_all.reshape(NMB, sub_blocks, MB)
    cos_all = cos_all.reshape(NMB, tick_rows, cos_all.shape[-1])
    sin_all = sin_all.reshape(NMB, tick_rows, sin_all.shape[-1])

    def pick(early_val, late_val):
        return jax.tree.map(
            lambda upper_val, lower_val: jnp.where(leading, upper_val, lower_val),
            early_val,
            late_val,
        )

    received = jnp.zeros((tick_rows, model_width), jnp.bfloat16)
    tick_outputs = []
    tick_stored = []
    for section_tick in range(NMB + 1):
        early_block = min(section_tick, NMB - 1)
        late_block = max(section_tick - 1, 0)
        block_rows = jnp.where(
            leading, input_rows[early_block * tick_rows : (early_block + 1) * tick_rows], received
        )
        segment, cosv, sinv = pick(
            (segment_all[early_block], cos_all[early_block], sin_all[early_block]),
            (segment_all[late_block], cos_all[late_block], sin_all[late_block]),
        )
        inputs = block_rows.astype(jnp.float32)
        row_mean = jnp.mean(inputs, axis=1, keepdims=True)
        centred = inputs - row_mean
        forward_inv_scale = lax.rsqrt(jnp.mean(centred * centred, axis=1, keepdims=True) + EPSILON)
        forward_normed = centred * forward_inv_scale
        forward_h_attn = (forward_normed * ln_gains[0] + ln_shifts[0]).astype(jnp.bfloat16)
        forward_h_mlp = (forward_normed * ln_gains[1] + ln_shifts[1]).astype(jnp.bfloat16)
        joined_proj = (
            jnp.dot(forward_h_attn, joined_mat, preferred_element_type=jnp.float32) + joined_add
        )
        forward_block_len = block_rows.shape[0]
        forward_queries = rotate(
            joined_proj[:, :local_width].reshape(forward_block_len, local_heads, HD), cosv, sinv
        ).astype(jnp.bfloat16)
        forward_keys_rot = rotate(
            joined_proj[:, local_width : 2 * local_width].reshape(
                forward_block_len, local_heads, HD
            ),
            cosv,
            sinv,
        ).astype(jnp.bfloat16)
        forward_values = (
            joined_proj[:, 2 * local_width :]
            .reshape(forward_block_len, local_heads, HD)
            .astype(jnp.bfloat16)
        )
        blocked = (sub_blocks, MB, local_heads, HD)
        forward_scores = (
            jnp.einsum(
                "bqhd,bkhd->bhqk",
                forward_queries.reshape(blocked),
                forward_keys_rot.reshape(blocked),
                preferred_element_type=jnp.float32,
            )
            * score_scale
        )
        forward_scores = jnp.where(allowed_keys(segment)[:, None], forward_scores, MASKED)
        row_top = jnp.max(forward_scores, axis=3, keepdims=True)
        exponent = jnp.exp(forward_scores - row_top)
        row_total = jnp.sum(exponent, axis=3, keepdims=True)
        forward_log_total = row_top + jnp.log(row_total)
        weights_low = (exponent / row_total).astype(jnp.bfloat16)
        forward_context = jnp.einsum(
            "bhqk,bkhd->bqhd",
            weights_low,
            forward_values.reshape(blocked),
            preferred_element_type=jnp.float32,
        )
        forward_context = forward_context.reshape(forward_block_len, local_width).astype(
            jnp.bfloat16
        )
        forward_up_proj = (
            jnp.dot(forward_h_mlp, up_mat, preferred_element_type=jnp.float32) + up_add
        )
        forward_activated = exact_gelu(forward_up_proj).astype(jnp.bfloat16)
        partial_value = jnp.dot(forward_context, dense_mat, preferred_element_type=jnp.float32)
        partial_value = partial_value + jnp.dot(
            forward_activated, down_mat, preferred_element_type=jnp.float32
        )
        branches = tensor_scatter_sum(partial_value.astype(jnp.bfloat16))
        column_start = lax.axis_index("tensor") * quarter
        own_inputs = lax.dynamic_slice_in_dim(inputs, column_start, quarter, 1)
        own_bias = lax.dynamic_slice_in_dim(bias_sum, column_start, quarter, 0)
        result = own_inputs + branches + own_bias
        forward_stored = (
            forward_normed,
            forward_inv_scale,
            forward_h_attn,
            forward_h_mlp,
            forward_queries,
            forward_keys_rot,
            forward_values,
            forward_log_total,
            forward_context,
            forward_up_proj,
            forward_activated,
        )
        result, stored = (result, forward_stored)
        result_low = result.astype(jnp.bfloat16)
        tick_outputs.append(result_low)
        tick_stored.append((stored, segment, cosv, sinv))
        if section_tick < NMB:
            received = cross_gather(result_low, 0)
    section_rows = jnp.concatenate(
        [jnp.where(leading, tick_outputs[block], tick_outputs[block + 1]) for block in range(NMB)],
        axis=0,
    )
    section_out = section_rows[None]
    returned = jnp.zeros((tick_rows, model_width), jnp.bfloat16)
    tick_grads = []
    totals = None
    for section_tick in range(NMB + 1):
        own_block = min(section_tick, NMB - 1)
        late_tick = max(section_tick - 1, 0)
        upper_tick = min(section_tick + 1, NMB)
        from_output = output_grads[own_block * tick_rows : (own_block + 1) * tick_rows]
        if section_tick == NMB:
            from_output = jnp.zeros_like(from_output)
        grad_rows = jnp.where(leading, returned, from_output)
        stored, segment, cosv, sinv = pick(tick_stored[late_tick], tick_stored[upper_tick])
        (
            normed,
            inv_scale,
            h_attn,
            h_mlp,
            queries,
            keys_rot,
            values,
            log_total,
            context,
            up_proj,
            activated,
        ) = stored
        block_len = grad_rows.shape[0]
        grad_wide = grad_rows.astype(jnp.float32)
        column_sum = jnp.sum(grad_wide, axis=0)
        backward_grad_dense = contract_rows(context, grad_rows)
        backward_grad_down = contract_rows(activated, grad_rows)
        d_context = contract_cols(grad_rows, dense_mat).astype(jnp.bfloat16)
        d_act = contract_cols(grad_rows, down_mat)
        unused, slope_back = jax.vjp(exact_gelu, up_proj)
        d_up = slope_back(d_act)[0].astype(jnp.bfloat16)
        grad_up_add = jnp.sum(d_up.astype(jnp.float32), axis=0)
        backward_grad_up = contract_rows(h_mlp, d_up)
        d_hmlp = contract_cols(d_up, up_mat)
        blocked = (sub_blocks, MB, local_heads, HD)
        queries_b = queries.reshape(blocked)
        keys_b = keys_rot.reshape(blocked)
        scores = (
            jnp.einsum("bqhd,bkhd->bhqk", queries_b, keys_b, preferred_element_type=jnp.float32)
            * score_scale
        )
        scores = jnp.where(allowed_keys(segment)[:, None], scores, MASKED)
        weights_soft = jnp.exp(scores - log_total)
        d_context3 = d_context.reshape(blocked)
        d_values = jnp.einsum(
            "bhqk,bqhd->bkhd",
            weights_soft.astype(jnp.bfloat16),
            d_context3,
            preferred_element_type=jnp.float32,
        ).astype(jnp.bfloat16)
        d_weights = jnp.einsum(
            "bqhd,bkhd->bhqk", d_context3, values.reshape(blocked), preferred_element_type=jnp.float32
        )
        row_delta = jnp.sum(weights_soft * d_weights, axis=3, keepdims=True)
        d_scores = (weights_soft * (d_weights - row_delta)).astype(jnp.bfloat16)
        heads_shape = (block_len, local_heads, HD)
        d_queries = (
            jnp.einsum("bhqk,bkhd->bqhd", d_scores, keys_b, preferred_element_type=jnp.float32)
            * score_scale
        ).reshape(heads_shape)
        d_keys = (
            jnp.einsum("bhqk,bqhd->bkhd", d_scores, queries_b, preferred_element_type=jnp.float32)
            * score_scale
        ).reshape(heads_shape)
        d_queries = (
            rotate_back(d_queries, cosv, sinv).reshape(block_len, local_width).astype(jnp.bfloat16)
        )
        d_keys = (
            rotate_back(d_keys, cosv, sinv).reshape(block_len, local_width).astype(jnp.bfloat16)
        )
        d_joined = jnp.concatenate(
            [d_queries, d_keys, d_values.reshape(block_len, local_width)], axis=1
        )
        grad_joined_add = jnp.sum(d_joined.astype(jnp.float32), axis=0)
        backward_grad_joined = contract_rows(d_joined, h_attn)
        d_hattn = contract_cols(d_joined, joined_mat)
        grad_gains = jnp.concatenate(
            [jnp.sum(d_hattn * normed, axis=0), jnp.sum(d_hmlp * normed, axis=0)]
        )
        grad_shifts = jnp.concatenate([jnp.sum(d_hattn, axis=0), jnp.sum(d_hmlp, axis=0)])
        d_norm = tensor_scatter_sum(
            (d_hattn * ln_gains[0] + d_hmlp * ln_gains[1]).astype(jnp.bfloat16)
        )
        column_start = lax.axis_index("tensor") * quarter
        own_normed = lax.dynamic_slice_in_dim(normed, column_start, quarter, 1)
        own_grad = lax.dynamic_slice_in_dim(grad_wide, column_start, quarter, 1)
        row_stats = tensor_sum(
            jnp.concatenate(
                [
                    jnp.sum(d_norm, axis=1, keepdims=True),
                    jnp.sum(d_norm * own_normed, axis=1, keepdims=True),
                ],
                axis=1,
            )
        ) / model_width
        grad_input = own_grad + inv_scale * (
            d_norm - row_stats[:, 0:1] - own_normed * row_stats[:, 1:2]
        )
        small_terms = jnp.concatenate(
            [grad_gains, grad_shifts, column_sum, column_sum, grad_joined_add, grad_up_add]
        )
        terms = (
            backward_grad_joined[None],
            backward_grad_dense[None],
            backward_grad_up[None],
            backward_grad_down[None],
            small_terms[None],
        )
        grad_input, terms = (grad_input, terms)
        grad_low = grad_input.astype(jnp.bfloat16)
        tick_grads.append(grad_low)
        if totals is None:
            totals = terms
        else:
            totals = jax.tree.map(lambda older, newer: older + newer, totals, terms)
        if section_tick < NMB:
            returned = cross_gather(grad_low, 1)
    small_rows = totals[4][0]
    small_pad = (-small_rows.shape[0]) % model_width
    small_rows = jnp.pad(small_rows, (0, small_pad)).reshape(-1, model_width)
    pieces = (totals[0][0], totals[1][0], totals[2][0], totals[3][0], small_rows)
    slab = jnp.concatenate([piece.astype(jnp.bfloat16) for piece in pieces], axis=0)
    slab = lax.psum(slab, "dp").astype(jnp.float32)
    summed = []
    offset = 0
    for piece in pieces:
        summed.append(slab[offset : offset + piece.shape[0]])
        offset = offset + piece.shape[0]
    grad_rows_all = jnp.concatenate(
        [jnp.where(leading, tick_grads[block + 1], tick_grads[block]) for block in range(NMB)],
        axis=0,
    )
    input_grad = grad_rows_all[None]
    grad_joined = summed[0].T.reshape(1, model_width, 3, local_width)
    grad_dense = summed[1][None]
    grad_up = summed[2][None]
    grad_down = summed[3][None]
    small_sum = summed[4].reshape(-1)
    ln_sum = tensor_sum(small_sum[: 4 * model_width])
    grad_ln_gain = ln_sum[: 2 * model_width].reshape(1, 2, model_width)
    grad_ln_bias = ln_sum[2 * model_width :].reshape(1, 2, model_width)
    offset = 4 * model_width
    grad_output_bias = small_sum[offset : offset + 2 * model_width].reshape(1, 2, model_width)
    offset = offset + 2 * model_width
    grad_joined_bias = small_sum[offset : offset + 3 * local_width].reshape(1, 3, local_width)
    offset = offset + 3 * local_width
    grad_up_bias = small_sum[offset : offset + hidden_local].reshape(1, hidden_local)
    return (
        section_out,
        input_grad,
        grad_ln_gain,
        grad_ln_bias,
        grad_joined,
        grad_joined_bias,
        grad_dense,
        grad_up,
        grad_up_bias,
        grad_down,
        grad_output_bias,
    )


def solution(mesh):
    placed = (
        P("dp", "tensor"),
        P("dp", None),
        P("pipe", None, None),
        P("pipe", None, None),
        P("pipe", None, None, "tensor"),
        P("pipe", None, "tensor"),
        P("pipe", "tensor", None),
        P("pipe", None, "tensor"),
        P("pipe", "tensor"),
        P("pipe", "tensor", None),
        P("pipe", None, None),
        P("dp", "tensor"),
    )
    return jax.shard_map(
        per_device,
        mesh=mesh,
        in_specs=placed,
        out_specs=(
            P("pipe", "dp", "tensor"),
            P("pipe", "dp", "tensor"),
            P("pipe", None, None),
            P("pipe", None, None),
            P("pipe", None, None, "tensor"),
            P("pipe", None, "tensor"),
            P("pipe", "tensor", None),
            P("pipe", None, "tensor"),
            P("pipe", "tensor"),
            P("pipe", "tensor", None),
            P("pipe", None, None),
        ),
        check_vma=False,
    )
```

```python
import jax
import jax.numpy as jnp
from jax import lax
from jax.sharding import PartitionSpec as P

HD = 64
ROT = 16
MB = 128
NMB = 4


EPSILON = 1e-05
MASKED = -1e30


def passed_along(x, axis, by):
    peers = lax.axis_size(axis)
    pairs = [(i, i + by) for i in range(peers) if 0 <= i + by < peers]
    return lax.ppermute(x, axis, pairs)


def tensor_pieces(x):
    peers = lax.axis_size("tensor")
    me = lax.axis_index("tensor")
    parts = [x]
    for shift in range(1, peers):
        pairs = [(i, (i + shift) % peers) for i in range(peers)]
        parts.append(lax.ppermute(x, "tensor", pairs))
    ordered = []
    for owner in range(peers):
        slot = (me - owner) % peers
        chosen = parts[peers - 1]
        for k in range(peers - 2, -1, -1):
            chosen = jnp.where(slot == k, parts[k], chosen)
        ordered.append(chosen)
    return ordered


def tensor_sum(x):
    pieces = tensor_pieces(x)
    total = pieces[0].astype(jnp.float32)
    for piece in pieces[1:]:
        total = total + piece.astype(jnp.float32)
    return total

def ordered_by_owner(parts, me, peers):
    ordered = []
    for owner in range(peers):
        slot = (me - owner) % peers
        chosen = parts[peers - 1]
        for k in range(peers - 2, -1, -1):
            chosen = jnp.where(slot == k, parts[k], chosen)
        ordered.append(chosen)
    return ordered


def tensor_scatter_sum(x):
    peers = lax.axis_size("tensor")
    me = lax.axis_index("tensor")
    width = x.shape[1] // peers

    def piece_for(owner):
        return lax.dynamic_slice_in_dim(x, owner * width, width, 1)

    parts = [piece_for(me)]
    for shift in range(1, peers):
        pairs = [(i, (i + shift) % peers) for i in range(peers)]
        parts.append(lax.ppermute(piece_for((me + shift) % peers), "tensor", pairs))
    ordered = ordered_by_owner(parts, me, peers)
    total = ordered[0].astype(jnp.float32)
    for piece in ordered[1:]:
        total = total + piece.astype(jnp.float32)
    return total


def cross_gather(x, source_stage):
    peers = lax.axis_size("tensor")
    me = lax.axis_index("tensor")
    target_stage = 1 - source_stage
    parts = []
    for shift in range(peers):
        pairs = [
            (source_stage * peers + i, target_stage * peers + (i + shift) % peers)
            for i in range(peers)
        ]
        parts.append(lax.ppermute(x, ("pipe", "tensor"), pairs))
    return jnp.concatenate(ordered_by_owner(parts, me, peers), axis=1)


def as_sent(x):
    return jax.tree.map(lambda a: a.astype(jnp.bfloat16) if a.dtype == jnp.float32 else a, x)


def positions(lengths, block_rows):
    seq_count = lengths.shape[1]
    counter = jnp.arange(seq_count, dtype=jnp.int32)
    lower_tri = (counter[:, None] >= counter[None, :]).astype(jnp.int32)
    seg_ends = jnp.sum(lengths[:, None, :] * lower_tri[None, :, :], axis=2)
    starts = seg_ends - lengths
    row_index = jnp.arange(block_rows, dtype=jnp.int32)
    segment = jnp.sum((row_index[None, :, None] >= seg_ends[:, None, :]).astype(jnp.int32), axis=2)
    member = (segment[:, :, None] == counter[None, None, :]).astype(jnp.int32)
    place = row_index[None, :] - jnp.sum(member * starts[:, None, :], axis=2)
    return (segment, place)


def rotary(place):
    half_rot = ROT // 2
    inv_freq = jnp.power(10000.0, -2.0 * jnp.arange(half_rot, dtype=jnp.float32) / ROT)
    angles = place.astype(jnp.float32)[..., None] * inv_freq
    return (jnp.cos(angles), jnp.sin(angles))


def rotate(heads_in, cosv, sinv):
    half_rot = ROT // 2
    first_half = heads_in[..., :half_rot]
    second_half = heads_in[..., half_rot:ROT]
    cos_rows = cosv[:, None, :]
    sin_rows = sinv[:, None, :]
    return jnp.concatenate(
        [
            first_half * cos_rows - second_half * sin_rows,
            second_half * cos_rows + first_half * sin_rows,
            heads_in[..., ROT:],
        ],
        axis=-1,
    )


def rotate_back(heads_in, cosv, sinv):
    half_rot = ROT // 2
    first_half = heads_in[..., :half_rot]
    second_half = heads_in[..., half_rot:ROT]
    cos_rows = cosv[:, None, :]
    sin_rows = sinv[:, None, :]
    return jnp.concatenate(
        [
            first_half * cos_rows + second_half * sin_rows,
            second_half * cos_rows - first_half * sin_rows,
            heads_in[..., ROT:],
        ],
        axis=-1,
    )


def exact_gelu(values):
    return jax.nn.gelu(values, approximate=False)


def allowed_keys(segment):
    row_index = jnp.arange(segment.shape[-1], dtype=jnp.int32)
    same = segment[..., :, None] == segment[..., None, :]
    return same & (row_index[None, :] <= row_index[:, None])


def contract_rows(left, right):
    return lax.dot_general(
        left, right, (((0,), (0,)), ((), ())), preferred_element_type=jnp.float32
    )


def contract_cols(left, right):
    return lax.dot_general(
        left, right, (((1,), (1,)), ((), ())), preferred_element_type=jnp.float32
    )


def per_device(
    tokens,
    lengths,
    ln_gain,
    ln_bias,
    joined_weight,
    joined_bias,
    dense_weight,
    up_weight,
    up_bias,
    down_weight,
    output_bias,
    cotangent,
):
    leading = lax.axis_index("pipe") == 0
    model_width = joined_weight.shape[1]
    local_width = joined_weight.shape[3]
    local_heads = local_width // HD
    hidden_local = up_weight.shape[2]
    quarter = tokens.shape[1]
    score_scale = HD ** (-0.5)
    ln_gains = ln_gain[0].astype(jnp.float32)
    ln_shifts = ln_bias[0].astype(jnp.float32)
    joined_mat = joined_weight[0].reshape(model_width, 3 * local_width)
    joined_add = joined_bias[0].astype(jnp.float32).reshape(3 * local_width)
    dense_mat = dense_weight[0]
    up_mat = up_weight[0]
    up_add = up_bias[0].astype(jnp.float32)
    down_mat = down_weight[0]
    bias_sum = output_bias[0, 0].astype(jnp.float32) + output_bias[0, 1].astype(jnp.float32)
    gathered_pieces = tensor_pieces(jnp.concatenate([tokens, cotangent], axis=0))
    gathered_rows = jnp.concatenate(gathered_pieces, axis=1)
    input_rows = gathered_rows[: tokens.shape[0]]
    output_grads = gathered_rows[tokens.shape[0] :]
    tick_rows = tokens.shape[0] // NMB
    sub_blocks = tick_rows // MB
    segment_all, place_all = positions(lengths, MB)
    cos_all, sin_all = rotary(place_all)
    segment_all = segment_all.reshape(NMB, sub_blocks, MB)
    cos_all = cos_all.reshape(NMB, tick_rows, cos_all.shape[-1])
    sin_all = sin_all.reshape(NMB, tick_rows, sin_all.shape[-1])

    def pick(early_val, late_val):
        return jax.tree.map(
            lambda upper_val, lower_val: jnp.where(leading, upper_val, lower_val),
            early_val,
            late_val,
        )

    received = jnp.zeros((tick_rows, model_width), jnp.bfloat16)
    tick_outputs = []
    tick_stored = []
    for section_tick in range(NMB + 1):
        early_block = min(section_tick, NMB - 1)
        late_block = max(section_tick - 1, 0)
        block_rows = jnp.where(
            leading, input_rows[early_block * tick_rows : (early_block + 1) * tick_rows], received
        )
        segment, cosv, sinv = pick(
            (segment_all[early_block], cos_all[early_block], sin_all[early_block]),
            (segment_all[late_block], cos_all[late_block], sin_all[late_block]),
        )
        inputs = block_rows.astype(jnp.float32)
        row_mean = jnp.mean(inputs, axis=1, keepdims=True)
        centred = inputs - row_mean
        forward_inv_scale = lax.rsqrt(jnp.mean(centred * centred, axis=1, keepdims=True) + EPSILON)
        forward_normed = centred * forward_inv_scale
        forward_h_attn = (forward_normed * ln_gains[0] + ln_shifts[0]).astype(jnp.bfloat16)
        forward_h_mlp = (forward_normed * ln_gains[1] + ln_shifts[1]).astype(jnp.bfloat16)
        joined_proj = (
            jnp.dot(forward_h_attn, joined_mat, preferred_element_type=jnp.float32) + joined_add
        )
        forward_block_len = block_rows.shape[0]
        forward_queries = rotate(
            joined_proj[:, :local_width].reshape(forward_block_len, local_heads, HD), cosv, sinv
        ).astype(jnp.bfloat16)
        forward_keys_rot = rotate(
            joined_proj[:, local_width : 2 * local_width].reshape(
                forward_block_len, local_heads, HD
            ),
            cosv,
            sinv,
        ).astype(jnp.bfloat16)
        forward_values = (
            joined_proj[:, 2 * local_width :]
            .reshape(forward_block_len, local_heads, HD)
            .astype(jnp.bfloat16)
        )
        blocked = (sub_blocks, MB, local_heads, HD)
        forward_scores = (
            jnp.einsum(
                "bqhd,bkhd->bhqk",
                forward_queries.reshape(blocked),
                forward_keys_rot.reshape(blocked),
                preferred_element_type=jnp.float32,
            )
            * score_scale
        )
        forward_scores = jnp.where(allowed_keys(segment)[:, None], forward_scores, MASKED)
        row_top = jnp.max(forward_scores, axis=3, keepdims=True)
        exponent = jnp.exp(forward_scores - row_top)
        row_total = jnp.sum(exponent, axis=3, keepdims=True)
        forward_log_total = row_top + jnp.log(row_total)
        weights_low = (exponent / row_total).astype(jnp.bfloat16)
        forward_context = jnp.einsum(
            "bhqk,bkhd->bqhd",
            weights_low,
            forward_values.reshape(blocked),
            preferred_element_type=jnp.float32,
        )
        forward_context = forward_context.reshape(forward_block_len, local_width).astype(
            jnp.bfloat16
        )
        forward_up_proj = (
            jnp.dot(forward_h_mlp, up_mat, preferred_element_type=jnp.float32) + up_add
        )
        forward_activated = exact_gelu(forward_up_proj).astype(jnp.bfloat16)
        partial_value = jnp.dot(forward_context, dense_mat, preferred_element_type=jnp.float32)
        partial_value = partial_value + jnp.dot(
            forward_activated, down_mat, preferred_element_type=jnp.float32
        )
        branches = tensor_scatter_sum(partial_value.astype(jnp.bfloat16))
        column_start = lax.axis_index("tensor") * quarter
        own_inputs = lax.dynamic_slice_in_dim(inputs, column_start, quarter, 1)
        own_bias = lax.dynamic_slice_in_dim(bias_sum, column_start, quarter, 0)
        result = own_inputs + branches + own_bias
        forward_stored = (
            forward_normed,
            forward_inv_scale,
            forward_h_attn,
            forward_h_mlp,
            forward_queries,
            forward_keys_rot,
            forward_values,
            forward_log_total,
            forward_context,
            forward_up_proj,
            forward_activated,
        )
        result, stored = (result, forward_stored)
        result_low = result.astype(jnp.bfloat16)
        tick_outputs.append(result_low)
        tick_stored.append((stored, segment, cosv, sinv))
        if section_tick < NMB:
            received = cross_gather(result_low, 0)
    section_rows = jnp.concatenate(
        [jnp.where(leading, tick_outputs[block], tick_outputs[block + 1]) for block in range(NMB)],
        axis=0,
    )
    section_out = section_rows[None]
    returned = jnp.zeros((tick_rows, model_width), jnp.bfloat16)
    tick_grads = []
    totals = None
    for section_tick in range(NMB + 1):
        own_block = min(section_tick, NMB - 1)
        late_tick = max(section_tick - 1, 0)
        upper_tick = min(section_tick + 1, NMB)
        from_output = output_grads[own_block * tick_rows : (own_block + 1) * tick_rows]
        if section_tick == NMB:
            from_output = jnp.zeros_like(from_output)
        grad_rows = jnp.where(leading, returned, from_output)
        stored, segment, cosv, sinv = pick(tick_stored[late_tick], tick_stored[upper_tick])
        (
            normed,
            inv_scale,
            h_attn,
            h_mlp,
            queries,
            keys_rot,
            values,
            log_total,
            context,
            up_proj,
            activated,
        ) = stored
        block_len = grad_rows.shape[0]
        grad_wide = grad_rows.astype(jnp.float32)
        column_sum = jnp.sum(grad_wide, axis=0)
        backward_grad_dense = contract_rows(context, grad_rows)
        backward_grad_down = contract_rows(activated, grad_rows)
        d_context = contract_cols(grad_rows, dense_mat).astype(jnp.bfloat16)
        d_act = contract_cols(grad_rows, down_mat)
        unused, slope_back = jax.vjp(exact_gelu, up_proj)
        d_up = slope_back(d_act)[0].astype(jnp.bfloat16)
        grad_up_add = jnp.sum(d_up.astype(jnp.float32), axis=0)
        backward_grad_up = contract_rows(h_mlp, d_up)
        d_hmlp = contract_cols(d_up, up_mat)
        blocked = (sub_blocks, MB, local_heads, HD)
        queries_b = queries.reshape(blocked)
        keys_b = keys_rot.reshape(blocked)
        scores = (
            jnp.einsum("bqhd,bkhd->bhqk", queries_b, keys_b, preferred_element_type=jnp.float32)
            * score_scale
        )
        scores = jnp.where(allowed_keys(segment)[:, None], scores, MASKED)
        weights_soft = jnp.exp(scores - log_total)
        d_context3 = d_context.reshape(blocked)
        d_values = jnp.einsum(
            "bhqk,bqhd->bkhd",
            weights_soft.astype(jnp.bfloat16),
            d_context3,
            preferred_element_type=jnp.float32,
        ).astype(jnp.bfloat16)
        d_weights = jnp.einsum(
            "bqhd,bkhd->bhqk", d_context3, values.reshape(blocked), preferred_element_type=jnp.float32
        )
        row_delta = jnp.sum(weights_soft * d_weights, axis=3, keepdims=True)
        d_scores = (weights_soft * (d_weights - row_delta)).astype(jnp.bfloat16)
        heads_shape = (block_len, local_heads, HD)
        d_queries = (
            jnp.einsum("bhqk,bkhd->bqhd", d_scores, keys_b, preferred_element_type=jnp.float32)
            * score_scale
        ).reshape(heads_shape)
        d_keys = (
            jnp.einsum("bhqk,bqhd->bkhd", d_scores, queries_b, preferred_element_type=jnp.float32)
            * score_scale
        ).reshape(heads_shape)
        d_queries = (
            rotate_back(d_queries, cosv, sinv).reshape(block_len, local_width).astype(jnp.bfloat16)
        )
        d_keys = (
            rotate_back(d_keys, cosv, sinv).reshape(block_len, local_width).astype(jnp.bfloat16)
        )
        d_joined = jnp.concatenate(
            [d_queries, d_keys, d_values.reshape(block_len, local_width)], axis=1
        )
        grad_joined_add = jnp.sum(d_joined.astype(jnp.float32), axis=0)
        backward_grad_joined = contract_rows(d_joined, h_attn)
        d_hattn = contract_cols(d_joined, joined_mat)
        grad_gains = jnp.concatenate(
            [jnp.sum(d_hattn * normed, axis=0), jnp.sum(d_hmlp * normed, axis=0)]
        )
        grad_shifts = jnp.concatenate([jnp.sum(d_hattn, axis=0), jnp.sum(d_hmlp, axis=0)])
        d_norm = tensor_scatter_sum(
            (d_hattn * ln_gains[0] + d_hmlp * ln_gains[1]).astype(jnp.bfloat16)
        )
        column_start = lax.axis_index("tensor") * quarter
        own_normed = lax.dynamic_slice_in_dim(normed, column_start, quarter, 1)
        own_grad = lax.dynamic_slice_in_dim(grad_wide, column_start, quarter, 1)
        row_stats = tensor_sum(
            jnp.concatenate(
                [
                    jnp.sum(d_norm, axis=1, keepdims=True),
                    jnp.sum(d_norm * own_normed, axis=1, keepdims=True),
                ],
                axis=1,
            )
        ) / model_width
        grad_input = own_grad + inv_scale * (
            d_norm - row_stats[:, 0:1] - own_normed * row_stats[:, 1:2]
        )
        small_terms = jnp.concatenate(
            [grad_gains, grad_shifts, column_sum, column_sum, grad_joined_add, grad_up_add]
        )
        terms = (
            backward_grad_joined[None],
            backward_grad_dense[None],
            backward_grad_up[None],
            backward_grad_down[None],
            small_terms[None],
        )
        grad_input, terms = (grad_input, terms)
        grad_low = grad_input.astype(jnp.bfloat16)
        tick_grads.append(grad_low)
        if totals is None:
            totals = terms
        else:
            totals = jax.tree.map(lambda older, newer: older + newer, totals, terms)
        if section_tick < NMB:
            returned = cross_gather(grad_low, 1)
    small_rows = totals[4][0]
    small_pad = (-small_rows.shape[0]) % model_width
    small_rows = jnp.pad(small_rows, (0, small_pad)).reshape(-1, model_width)
    pieces = (totals[0][0], totals[1][0], totals[2][0], totals[3][0], small_rows)
    slab = jnp.concatenate([piece.astype(jnp.bfloat16) for piece in pieces], axis=0)
    slab = lax.psum(slab, "dp").astype(jnp.float32)
    summed = []
    offset = 0
    for piece in pieces:
        summed.append(slab[offset : offset + piece.shape[0]])
        offset = offset + piece.shape[0]
    grad_rows_all = jnp.concatenate(
        [jnp.where(leading, tick_grads[block + 1], tick_grads[block]) for block in range(NMB)],
        axis=0,
    )
    input_grad = grad_rows_all[None]
    grad_joined = summed[0].T.reshape(1, model_width, 3, local_width)
    grad_dense = summed[1][None]
    grad_up = summed[2][None]
    grad_down = summed[3][None]
    small_sum = summed[4].reshape(-1)
    ln_sum = tensor_sum(small_sum[: 4 * model_width])
    grad_ln_gain = ln_sum[: 2 * model_width].reshape(1, 2, model_width)
    grad_ln_bias = ln_sum[2 * model_width :].reshape(1, 2, model_width)
    offset = 4 * model_width
    grad_output_bias = small_sum[offset : offset + 2 * model_width].reshape(1, 2, model_width)
    offset = offset + 2 * model_width
    grad_joined_bias = small_sum[offset : offset + 3 * local_width].reshape(1, 3, local_width)
    offset = offset + 3 * local_width
    grad_up_bias = small_sum[offset : offset + hidden_local].reshape(1, hidden_local)
    return (
        section_out,
        input_grad,
        grad_ln_gain,
        grad_ln_bias,
        grad_joined,
        grad_joined_bias,
        grad_dense,
        grad_up,
        grad_up_bias,
        grad_down,
        grad_output_bias,
    )


def solution(mesh):
    placed = (
        P("dp", "tensor"),
        P("dp", None),
        P("pipe", None, None),
        P("pipe", None, None),
        P("pipe", None, None, "tensor"),
        P("pipe", None, "tensor"),
        P("pipe", "tensor", None),
        P("pipe", None, "tensor"),
        P("pipe", "tensor"),
        P("pipe", "tensor", None),
        P("pipe", None, None),
        P("dp", "tensor"),
    )
    return jax.shard_map(
        per_device,
        mesh=mesh,
        in_specs=placed,
        out_specs=(
            P("pipe", "dp", "tensor"),
            P("pipe", "dp", "tensor"),
            P("pipe", None, None),
            P("pipe", None, None),
            P("pipe", None, None, "tensor"),
            P("pipe", None, "tensor"),
            P("pipe", "tensor", None),
            P("pipe", None, "tensor"),
            P("pipe", "tensor"),
            P("pipe", "tensor", None),
            P("pipe", None, None),
        ),
        check_vma=False,
    )
```

```python
import jax
import jax.numpy as jnp
from jax import lax
from jax.sharding import PartitionSpec as P

HD = 64
ROT = 16
MB = 128
NMB = 2


EPSILON = 1e-05
MASKED = -1e30


def passed_along(x, axis, by):
    peers = lax.axis_size(axis)
    pairs = [(i, i + by) for i in range(peers) if 0 <= i + by < peers]
    return lax.ppermute(x, axis, pairs)


def tensor_pieces(x):
    peers = lax.axis_size("tensor")
    me = lax.axis_index("tensor")
    parts = [x]
    for shift in range(1, peers):
        pairs = [(i, (i + shift) % peers) for i in range(peers)]
        parts.append(lax.ppermute(x, "tensor", pairs))
    ordered = []
    for owner in range(peers):
        slot = (me - owner) % peers
        chosen = parts[peers - 1]
        for k in range(peers - 2, -1, -1):
            chosen = jnp.where(slot == k, parts[k], chosen)
        ordered.append(chosen)
    return ordered


def tensor_sum(x):
    pieces = tensor_pieces(x)
    total = pieces[0].astype(jnp.float32)
    for piece in pieces[1:]:
        total = total + piece.astype(jnp.float32)
    return total

def ordered_by_owner(parts, me, peers):
    ordered = []
    for owner in range(peers):
        slot = (me - owner) % peers
        chosen = parts[peers - 1]
        for k in range(peers - 2, -1, -1):
            chosen = jnp.where(slot == k, parts[k], chosen)
        ordered.append(chosen)
    return ordered


def tensor_scatter_sum(x):
    peers = lax.axis_size("tensor")
    me = lax.axis_index("tensor")
    width = x.shape[1] // peers

    def piece_for(owner):
        return lax.dynamic_slice_in_dim(x, owner * width, width, 1)

    parts = [piece_for(me)]
    for shift in range(1, peers):
        pairs = [(i, (i + shift) % peers) for i in range(peers)]
        parts.append(lax.ppermute(piece_for((me + shift) % peers), "tensor", pairs))
    ordered = ordered_by_owner(parts, me, peers)
    total = ordered[0].astype(jnp.float32)
    for piece in ordered[1:]:
        total = total + piece.astype(jnp.float32)
    return total


def cross_gather(x, source_stage):
    peers = lax.axis_size("tensor")
    me = lax.axis_index("tensor")
    target_stage = 1 - source_stage
    parts = []
    for shift in range(peers):
        pairs = [
            (source_stage * peers + i, target_stage * peers + (i + shift) % peers)
            for i in range(peers)
        ]
        parts.append(lax.ppermute(x, ("pipe", "tensor"), pairs))
    return jnp.concatenate(ordered_by_owner(parts, me, peers), axis=1)


def as_sent(x):
    return jax.tree.map(lambda a: a.astype(jnp.bfloat16) if a.dtype == jnp.float32 else a, x)


def positions(lengths, block_rows):
    seq_count = lengths.shape[1]
    counter = jnp.arange(seq_count, dtype=jnp.int32)
    lower_tri = (counter[:, None] >= counter[None, :]).astype(jnp.int32)
    seg_ends = jnp.sum(lengths[:, None, :] * lower_tri[None, :, :], axis=2)
    starts = seg_ends - lengths
    row_index = jnp.arange(block_rows, dtype=jnp.int32)
    segment = jnp.sum((row_index[None, :, None] >= seg_ends[:, None, :]).astype(jnp.int32), axis=2)
    member = (segment[:, :, None] == counter[None, None, :]).astype(jnp.int32)
    place = row_index[None, :] - jnp.sum(member * starts[:, None, :], axis=2)
    return (segment, place)


def rotary(place):
    half_rot = ROT // 2
    inv_freq = jnp.power(10000.0, -2.0 * jnp.arange(half_rot, dtype=jnp.float32) / ROT)
    angles = place.astype(jnp.float32)[..., None] * inv_freq
    return (jnp.cos(angles), jnp.sin(angles))


def rotate(heads_in, cosv, sinv):
    half_rot = ROT // 2
    first_half = heads_in[..., :half_rot]
    second_half = heads_in[..., half_rot:ROT]
    cos_rows = cosv[:, None, :]
    sin_rows = sinv[:, None, :]
    return jnp.concatenate(
        [
            first_half * cos_rows - second_half * sin_rows,
            second_half * cos_rows + first_half * sin_rows,
            heads_in[..., ROT:],
        ],
        axis=-1,
    )


def rotate_back(heads_in, cosv, sinv):
    half_rot = ROT // 2
    first_half = heads_in[..., :half_rot]
    second_half = heads_in[..., half_rot:ROT]
    cos_rows = cosv[:, None, :]
    sin_rows = sinv[:, None, :]
    return jnp.concatenate(
        [
            first_half * cos_rows + second_half * sin_rows,
            second_half * cos_rows - first_half * sin_rows,
            heads_in[..., ROT:],
        ],
        axis=-1,
    )


def exact_gelu(values):
    return jax.nn.gelu(values, approximate=False)


def allowed_keys(segment):
    row_index = jnp.arange(segment.shape[-1], dtype=jnp.int32)
    same = segment[..., :, None] == segment[..., None, :]
    return same & (row_index[None, :] <= row_index[:, None])


def contract_rows(left, right):
    return lax.dot_general(
        left, right, (((0,), (0,)), ((), ())), preferred_element_type=jnp.float32
    )


def contract_cols(left, right):
    return lax.dot_general(
        left, right, (((1,), (1,)), ((), ())), preferred_element_type=jnp.float32
    )


def per_device(
    tokens,
    lengths,
    ln_gain,
    ln_bias,
    joined_weight,
    joined_bias,
    dense_weight,
    up_weight,
    up_bias,
    down_weight,
    output_bias,
    cotangent,
):
    leading = lax.axis_index("pipe") == 0
    model_width = joined_weight.shape[1]
    local_width = joined_weight.shape[3]
    local_heads = local_width // HD
    hidden_local = up_weight.shape[2]
    quarter = tokens.shape[1]
    score_scale = HD ** (-0.5)
    ln_gains = ln_gain[0].astype(jnp.float32)
    ln_shifts = ln_bias[0].astype(jnp.float32)
    joined_mat = joined_weight[0].reshape(model_width, 3 * local_width)
    joined_add = joined_bias[0].astype(jnp.float32).reshape(3 * local_width)
    dense_mat = dense_weight[0]
    up_mat = up_weight[0]
    up_add = up_bias[0].astype(jnp.float32)
    down_mat = down_weight[0]
    bias_sum = output_bias[0, 0].astype(jnp.float32) + output_bias[0, 1].astype(jnp.float32)
    input_rows = jnp.concatenate(tensor_pieces(tokens), axis=1)
    output_grads = jnp.concatenate(tensor_pieces(cotangent), axis=1)
    tick_rows = tokens.shape[0] // NMB
    sub_blocks = tick_rows // MB
    segment_all, place_all = positions(lengths, MB)
    cos_all, sin_all = rotary(place_all)
    segment_all = segment_all.reshape(NMB, sub_blocks, MB)
    cos_all = cos_all.reshape(NMB, tick_rows, cos_all.shape[-1])
    sin_all = sin_all.reshape(NMB, tick_rows, sin_all.shape[-1])

    def pick(early_val, late_val):
        return jax.tree.map(
            lambda upper_val, lower_val: jnp.where(leading, upper_val, lower_val),
            early_val,
            late_val,
        )

    received = jnp.zeros((tick_rows, model_width), jnp.bfloat16)
    tick_outputs = []
    tick_stored = []
    for section_tick in range(NMB + 1):
        early_block = min(section_tick, NMB - 1)
        late_block = max(section_tick - 1, 0)
        block_rows = jnp.where(
            leading, input_rows[early_block * tick_rows : (early_block + 1) * tick_rows], received
        )
        segment, cosv, sinv = pick(
            (segment_all[early_block], cos_all[early_block], sin_all[early_block]),
            (segment_all[late_block], cos_all[late_block], sin_all[late_block]),
        )
        inputs = block_rows.astype(jnp.float32)
        row_mean = jnp.mean(inputs, axis=1, keepdims=True)
        centred = inputs - row_mean
        forward_inv_scale = lax.rsqrt(jnp.mean(centred * centred, axis=1, keepdims=True) + EPSILON)
        forward_normed = centred * forward_inv_scale
        forward_h_attn = (forward_normed * ln_gains[0] + ln_shifts[0]).astype(jnp.bfloat16)
        forward_h_mlp = (forward_normed * ln_gains[1] + ln_shifts[1]).astype(jnp.bfloat16)
        joined_proj = (
            jnp.dot(forward_h_attn, joined_mat, preferred_element_type=jnp.float32) + joined_add
        )
        forward_block_len = block_rows.shape[0]
        forward_queries = rotate(
            joined_proj[:, :local_width].reshape(forward_block_len, local_heads, HD), cosv, sinv
        ).astype(jnp.bfloat16)
        forward_keys_rot = rotate(
            joined_proj[:, local_width : 2 * local_width].reshape(
                forward_block_len, local_heads, HD
            ),
            cosv,
            sinv,
        ).astype(jnp.bfloat16)
        forward_values = (
            joined_proj[:, 2 * local_width :]
            .reshape(forward_block_len, local_heads, HD)
            .astype(jnp.bfloat16)
        )
        blocked = (sub_blocks, MB, local_heads, HD)
        forward_scores = (
            jnp.einsum(
                "bqhd,bkhd->bhqk",
                forward_queries.reshape(blocked),
                forward_keys_rot.reshape(blocked),
                preferred_element_type=jnp.float32,
            )
            * score_scale
        )
        forward_scores = jnp.where(allowed_keys(segment)[:, None], forward_scores, MASKED)
        row_top = jnp.max(forward_scores, axis=3, keepdims=True)
        exponent = jnp.exp(forward_scores - row_top)
        row_total = jnp.sum(exponent, axis=3, keepdims=True)
        forward_log_total = row_top + jnp.log(row_total)
        weights_low = (exponent / row_total).astype(jnp.bfloat16)
        forward_context = jnp.einsum(
            "bhqk,bkhd->bqhd",
            weights_low,
            forward_values.reshape(blocked),
            preferred_element_type=jnp.float32,
        )
        forward_context = forward_context.reshape(forward_block_len, local_width).astype(
            jnp.bfloat16
        )
        forward_up_proj = (
            jnp.dot(forward_h_mlp, up_mat, preferred_element_type=jnp.float32) + up_add
        )
        forward_activated = exact_gelu(forward_up_proj).astype(jnp.bfloat16)
        partial_value = jnp.dot(forward_context, dense_mat, preferred_element_type=jnp.float32)
        partial_value = partial_value + jnp.dot(
            forward_activated, down_mat, preferred_element_type=jnp.float32
        )
        branches = tensor_scatter_sum(partial_value.astype(jnp.bfloat16))
        column_start = lax.axis_index("tensor") * quarter
        own_inputs = lax.dynamic_slice_in_dim(inputs, column_start, quarter, 1)
        own_bias = lax.dynamic_slice_in_dim(bias_sum, column_start, quarter, 0)
        result = own_inputs + branches + own_bias
        forward_stored = (
            forward_normed,
            forward_inv_scale,
            forward_h_attn,
            forward_h_mlp,
            forward_queries,
            forward_keys_rot,
            forward_values,
            forward_log_total,
            forward_context,
            forward_up_proj,
            forward_activated,
        )
        result, stored = (result, forward_stored)
        result_low = result.astype(jnp.bfloat16)
        tick_outputs.append(result_low)
        tick_stored.append((stored, segment, cosv, sinv))
        if section_tick < NMB:
            received = cross_gather(result_low, 0)
    section_rows = jnp.concatenate(
        [jnp.where(leading, tick_outputs[block], tick_outputs[block + 1]) for block in range(NMB)],
        axis=0,
    )
    section_out = section_rows[None]
    returned = jnp.zeros((tick_rows, model_width), jnp.bfloat16)
    tick_grads = []
    totals = None
    for section_tick in range(NMB + 1):
        own_block = min(section_tick, NMB - 1)
        late_tick = max(section_tick - 1, 0)
        upper_tick = min(section_tick + 1, NMB)
        from_output = output_grads[own_block * tick_rows : (own_block + 1) * tick_rows]
        if section_tick == NMB:
            from_output = jnp.zeros_like(from_output)
        grad_rows = jnp.where(leading, returned, from_output)
        stored, segment, cosv, sinv = pick(tick_stored[late_tick], tick_stored[upper_tick])
        (
            normed,
            inv_scale,
            h_attn,
            h_mlp,
            queries,
            keys_rot,
            values,
            log_total,
            context,
            up_proj,
            activated,
        ) = stored
        block_len = grad_rows.shape[0]
        grad_wide = grad_rows.astype(jnp.float32)
        column_sum = jnp.sum(grad_wide, axis=0)
        backward_grad_dense = contract_rows(context, grad_rows)
        backward_grad_down = contract_rows(activated, grad_rows)
        d_context = contract_cols(grad_rows, dense_mat).astype(jnp.bfloat16)
        d_act = contract_cols(grad_rows, down_mat)
        unused, slope_back = jax.vjp(exact_gelu, up_proj)
        d_up = slope_back(d_act)[0].astype(jnp.bfloat16)
        grad_up_add = jnp.sum(d_up.astype(jnp.float32), axis=0)
        backward_grad_up = contract_rows(h_mlp, d_up)
        d_hmlp = contract_cols(d_up, up_mat)
        blocked = (sub_blocks, MB, local_heads, HD)
        queries_b = queries.reshape(blocked)
        keys_b = keys_rot.reshape(blocked)
        scores = (
            jnp.einsum("bqhd,bkhd->bhqk", queries_b, keys_b, preferred_element_type=jnp.float32)
            * score_scale
        )
        scores = jnp.where(allowed_keys(segment)[:, None], scores, MASKED)
        weights_soft = jnp.exp(scores - log_total)
        d_context3 = d_context.reshape(blocked)
        d_values = jnp.einsum(
            "bhqk,bqhd->bkhd",
            weights_soft.astype(jnp.bfloat16),
            d_context3,
            preferred_element_type=jnp.float32,
        ).astype(jnp.bfloat16)
        d_weights = jnp.einsum(
            "bqhd,bkhd->bhqk", d_context3, values.reshape(blocked), preferred_element_type=jnp.float32
        )
        row_delta = jnp.sum(weights_soft * d_weights, axis=3, keepdims=True)
        d_scores = (weights_soft * (d_weights - row_delta)).astype(jnp.bfloat16)
        heads_shape = (block_len, local_heads, HD)
        d_queries = (
            jnp.einsum("bhqk,bkhd->bqhd", d_scores, keys_b, preferred_element_type=jnp.float32)
            * score_scale
        ).reshape(heads_shape)
        d_keys = (
            jnp.einsum("bhqk,bqhd->bkhd", d_scores, queries_b, preferred_element_type=jnp.float32)
            * score_scale
        ).reshape(heads_shape)
        d_queries = (
            rotate_back(d_queries, cosv, sinv).reshape(block_len, local_width).astype(jnp.bfloat16)
        )
        d_keys = (
            rotate_back(d_keys, cosv, sinv).reshape(block_len, local_width).astype(jnp.bfloat16)
        )
        d_joined = jnp.concatenate(
            [d_queries, d_keys, d_values.reshape(block_len, local_width)], axis=1
        )
        grad_joined_add = jnp.sum(d_joined.astype(jnp.float32), axis=0)
        backward_grad_joined = contract_rows(d_joined, h_attn)
        d_hattn = contract_cols(d_joined, joined_mat)
        grad_gains = jnp.concatenate(
            [jnp.sum(d_hattn * normed, axis=0), jnp.sum(d_hmlp * normed, axis=0)]
        )
        grad_shifts = jnp.concatenate([jnp.sum(d_hattn, axis=0), jnp.sum(d_hmlp, axis=0)])
        d_norm = tensor_scatter_sum(
            (d_hattn * ln_gains[0] + d_hmlp * ln_gains[1]).astype(jnp.bfloat16)
        )
        column_start = lax.axis_index("tensor") * quarter
        own_normed = lax.dynamic_slice_in_dim(normed, column_start, quarter, 1)
        own_grad = lax.dynamic_slice_in_dim(grad_wide, column_start, quarter, 1)
        row_stats = tensor_sum(
            jnp.concatenate(
                [
                    jnp.sum(d_norm, axis=1, keepdims=True),
                    jnp.sum(d_norm * own_normed, axis=1, keepdims=True),
                ],
                axis=1,
            )
        ) / model_width
        grad_input = own_grad + inv_scale * (
            d_norm - row_stats[:, 0:1] - own_normed * row_stats[:, 1:2]
        )
        small_terms = jnp.concatenate(
            [grad_gains, grad_shifts, column_sum, column_sum, grad_joined_add, grad_up_add]
        )
        terms = (
            backward_grad_joined[None],
            backward_grad_dense[None],
            backward_grad_up[None],
            backward_grad_down[None],
            small_terms[None],
        )
        grad_input, terms = (grad_input, terms)
        grad_low = grad_input.astype(jnp.bfloat16)
        tick_grads.append(grad_low)
        if totals is None:
            totals = terms
        else:
            totals = jax.tree.map(lambda older, newer: older + newer, totals, terms)
        if section_tick < NMB:
            returned = cross_gather(grad_low, 1)
    small_rows = totals[4][0]
    small_pad = (-small_rows.shape[0]) % model_width
    small_rows = jnp.pad(small_rows, (0, small_pad)).reshape(-1, model_width)
    pieces = (totals[0][0], totals[1][0], totals[2][0], totals[3][0], small_rows)
    slab = jnp.concatenate([piece.astype(jnp.bfloat16) for piece in pieces], axis=0)
    slab = lax.psum(slab, "dp").astype(jnp.float32)
    summed = []
    offset = 0
    for piece in pieces:
        summed.append(slab[offset : offset + piece.shape[0]])
        offset = offset + piece.shape[0]
    grad_rows_all = jnp.concatenate(
        [jnp.where(leading, tick_grads[block + 1], tick_grads[block]) for block in range(NMB)],
        axis=0,
    )
    input_grad = grad_rows_all[None]
    grad_joined = summed[0].T.reshape(1, model_width, 3, local_width)
    grad_dense = summed[1][None]
    grad_up = summed[2][None]
    grad_down = summed[3][None]
    small_sum = summed[4].reshape(-1)
    ln_sum = tensor_sum(small_sum[: 4 * model_width])
    grad_ln_gain = ln_sum[: 2 * model_width].reshape(1, 2, model_width)
    grad_ln_bias = ln_sum[2 * model_width :].reshape(1, 2, model_width)
    offset = 4 * model_width
    grad_output_bias = small_sum[offset : offset + 2 * model_width].reshape(1, 2, model_width)
    offset = offset + 2 * model_width
    grad_joined_bias = small_sum[offset : offset + 3 * local_width].reshape(1, 3, local_width)
    offset = offset + 3 * local_width
    grad_up_bias = small_sum[offset : offset + hidden_local].reshape(1, hidden_local)
    return (
        section_out,
        input_grad,
        grad_ln_gain,
        grad_ln_bias,
        grad_joined,
        grad_joined_bias,
        grad_dense,
        grad_up,
        grad_up_bias,
        grad_down,
        grad_output_bias,
    )


def solution(mesh):
    placed = (
        P("dp", "tensor"),
        P("dp", None),
        P("pipe", None, None),
        P("pipe", None, None),
        P("pipe", None, None, "tensor"),
        P("pipe", None, "tensor"),
        P("pipe", "tensor", None),
        P("pipe", None, "tensor"),
        P("pipe", "tensor"),
        P("pipe", "tensor", None),
        P("pipe", None, None),
        P("dp", "tensor"),
    )
    return jax.shard_map(
        per_device,
        mesh=mesh,
        in_specs=placed,
        out_specs=(
            P("pipe", "dp", "tensor"),
            P("pipe", "dp", "tensor"),
            P("pipe", None, None),
            P("pipe", None, None),
            P("pipe", None, None, "tensor"),
            P("pipe", None, "tensor"),
            P("pipe", "tensor", None),
            P("pipe", None, "tensor"),
            P("pipe", "tensor"),
            P("pipe", "tensor", None),
            P("pipe", None, None),
        ),
        check_vma=False,
    )
```

```python
import jax
import jax.numpy as jnp
from jax import lax
from jax.sharding import PartitionSpec as P

HD = 64
ROT = 16
MB = 128
NMB = 2


EPSILON = 1e-05
MASKED = -1e30


def passed_along(x, axis, by):
    peers = lax.axis_size(axis)
    pairs = [(i, i + by) for i in range(peers) if 0 <= i + by < peers]
    return lax.ppermute(x, axis, pairs)


def tensor_pieces(x):
    peers = lax.axis_size("tensor")
    me = lax.axis_index("tensor")
    parts = [x]
    for shift in range(1, peers):
        pairs = [(i, (i + shift) % peers) for i in range(peers)]
        parts.append(lax.ppermute(x, "tensor", pairs))
    ordered = []
    for owner in range(peers):
        slot = (me - owner) % peers
        chosen = parts[peers - 1]
        for k in range(peers - 2, -1, -1):
            chosen = jnp.where(slot == k, parts[k], chosen)
        ordered.append(chosen)
    return ordered


def tensor_sum(x):
    pieces = tensor_pieces(x)
    total = pieces[0].astype(jnp.float32)
    for piece in pieces[1:]:
        total = total + piece.astype(jnp.float32)
    return total

def ordered_by_owner(parts, me, peers):
    ordered = []
    for owner in range(peers):
        slot = (me - owner) % peers
        chosen = parts[peers - 1]
        for k in range(peers - 2, -1, -1):
            chosen = jnp.where(slot == k, parts[k], chosen)
        ordered.append(chosen)
    return ordered


def tensor_scatter_sum(x):
    peers = lax.axis_size("tensor")
    me = lax.axis_index("tensor")
    width = x.shape[1] // peers

    def piece_for(owner):
        return lax.dynamic_slice_in_dim(x, owner * width, width, 1)

    parts = [piece_for(me)]
    for shift in range(1, peers):
        pairs = [(i, (i + shift) % peers) for i in range(peers)]
        parts.append(lax.ppermute(piece_for((me + shift) % peers), "tensor", pairs))
    ordered = ordered_by_owner(parts, me, peers)
    total = ordered[0].astype(jnp.float32)
    for piece in ordered[1:]:
        total = total + piece.astype(jnp.float32)
    return total


def cross_gather(x, source_stage):
    peers = lax.axis_size("tensor")
    me = lax.axis_index("tensor")
    target_stage = 1 - source_stage
    parts = []
    for shift in range(peers):
        pairs = [
            (source_stage * peers + i, target_stage * peers + (i + shift) % peers)
            for i in range(peers)
        ]
        parts.append(lax.ppermute(x, ("pipe", "tensor"), pairs))
    return jnp.concatenate(ordered_by_owner(parts, me, peers), axis=1)


def as_sent(x):
    return jax.tree.map(lambda a: a.astype(jnp.bfloat16) if a.dtype == jnp.float32 else a, x)


def positions(lengths, block_rows):
    seq_count = lengths.shape[1]
    counter = jnp.arange(seq_count, dtype=jnp.int32)
    lower_tri = (counter[:, None] >= counter[None, :]).astype(jnp.int32)
    seg_ends = jnp.sum(lengths[:, None, :] * lower_tri[None, :, :], axis=2)
    starts = seg_ends - lengths
    row_index = jnp.arange(block_rows, dtype=jnp.int32)
    segment = jnp.sum((row_index[None, :, None] >= seg_ends[:, None, :]).astype(jnp.int32), axis=2)
    member = (segment[:, :, None] == counter[None, None, :]).astype(jnp.int32)
    place = row_index[None, :] - jnp.sum(member * starts[:, None, :], axis=2)
    return (segment, place)


def rotary(place):
    half_rot = ROT // 2
    inv_freq = jnp.power(10000.0, -2.0 * jnp.arange(half_rot, dtype=jnp.float32) / ROT)
    angles = place.astype(jnp.float32)[..., None] * inv_freq
    return (jnp.cos(angles), jnp.sin(angles))


def rotate(heads_in, cosv, sinv):
    half_rot = ROT // 2
    first_half = heads_in[..., :half_rot]
    second_half = heads_in[..., half_rot:ROT]
    cos_rows = cosv[:, None, :]
    sin_rows = sinv[:, None, :]
    return jnp.concatenate(
        [
            first_half * cos_rows - second_half * sin_rows,
            second_half * cos_rows + first_half * sin_rows,
            heads_in[..., ROT:],
        ],
        axis=-1,
    )


def rotate_back(heads_in, cosv, sinv):
    half_rot = ROT // 2
    first_half = heads_in[..., :half_rot]
    second_half = heads_in[..., half_rot:ROT]
    cos_rows = cosv[:, None, :]
    sin_rows = sinv[:, None, :]
    return jnp.concatenate(
        [
            first_half * cos_rows + second_half * sin_rows,
            second_half * cos_rows - first_half * sin_rows,
            heads_in[..., ROT:],
        ],
        axis=-1,
    )


def exact_gelu(values):
    return jax.nn.gelu(values, approximate=False)


def allowed_keys(segment):
    row_index = jnp.arange(segment.shape[-1], dtype=jnp.int32)
    same = segment[..., :, None] == segment[..., None, :]
    return same & (row_index[None, :] <= row_index[:, None])


def contract_rows(left, right):
    return lax.dot_general(
        left, right, (((0,), (0,)), ((), ())), preferred_element_type=jnp.float32
    )


def contract_cols(left, right):
    return lax.dot_general(
        left, right, (((1,), (1,)), ((), ())), preferred_element_type=jnp.float32
    )


def per_device(
    tokens,
    lengths,
    ln_gain,
    ln_bias,
    joined_weight,
    joined_bias,
    dense_weight,
    up_weight,
    up_bias,
    down_weight,
    output_bias,
    cotangent,
):
    leading = lax.axis_index("pipe") == 0
    model_width = joined_weight.shape[1]
    local_width = joined_weight.shape[3]
    local_heads = local_width // HD
    hidden_local = up_weight.shape[2]
    quarter = tokens.shape[1]
    score_scale = HD ** (-0.5)
    ln_gains = ln_gain[0].astype(jnp.float32)
    ln_shifts = ln_bias[0].astype(jnp.float32)
    joined_mat = joined_weight[0].reshape(model_width, 3 * local_width)
    joined_add = joined_bias[0].astype(jnp.float32).reshape(3 * local_width)
    dense_mat = dense_weight[0]
    up_mat = up_weight[0]
    up_add = up_bias[0].astype(jnp.float32)
    down_mat = down_weight[0]
    bias_sum = output_bias[0, 0].astype(jnp.float32) + output_bias[0, 1].astype(jnp.float32)
    gathered_pieces = tensor_pieces(jnp.concatenate([tokens, cotangent], axis=0))
    gathered_rows = jnp.concatenate(gathered_pieces, axis=1)
    input_rows = gathered_rows[: tokens.shape[0]]
    output_grads = gathered_rows[tokens.shape[0] :]
    tick_rows = tokens.shape[0] // NMB
    sub_blocks = tick_rows // MB
    segment_all, place_all = positions(lengths, MB)
    cos_all, sin_all = rotary(place_all)
    segment_all = segment_all.reshape(NMB, sub_blocks, MB)
    cos_all = cos_all.reshape(NMB, tick_rows, cos_all.shape[-1])
    sin_all = sin_all.reshape(NMB, tick_rows, sin_all.shape[-1])

    def pick(early_val, late_val):
        return jax.tree.map(
            lambda upper_val, lower_val: jnp.where(leading, upper_val, lower_val),
            early_val,
            late_val,
        )

    received = jnp.zeros((tick_rows, model_width), jnp.bfloat16)
    tick_outputs = []
    tick_stored = []
    for section_tick in range(NMB + 1):
        early_block = min(section_tick, NMB - 1)
        late_block = max(section_tick - 1, 0)
        block_rows = jnp.where(
            leading, input_rows[early_block * tick_rows : (early_block + 1) * tick_rows], received
        )
        segment, cosv, sinv = pick(
            (segment_all[early_block], cos_all[early_block], sin_all[early_block]),
            (segment_all[late_block], cos_all[late_block], sin_all[late_block]),
        )
        inputs = block_rows.astype(jnp.float32)
        row_mean = jnp.mean(inputs, axis=1, keepdims=True)
        centred = inputs - row_mean
        forward_inv_scale = lax.rsqrt(jnp.mean(centred * centred, axis=1, keepdims=True) + EPSILON)
        forward_normed = centred * forward_inv_scale
        forward_h_attn = (forward_normed * ln_gains[0] + ln_shifts[0]).astype(jnp.bfloat16)
        forward_h_mlp = (forward_normed * ln_gains[1] + ln_shifts[1]).astype(jnp.bfloat16)
        joined_proj = (
            jnp.dot(forward_h_attn, joined_mat, preferred_element_type=jnp.float32) + joined_add
        )
        forward_block_len = block_rows.shape[0]
        forward_queries = rotate(
            joined_proj[:, :local_width].reshape(forward_block_len, local_heads, HD), cosv, sinv
        ).astype(jnp.bfloat16)
        forward_keys_rot = rotate(
            joined_proj[:, local_width : 2 * local_width].reshape(
                forward_block_len, local_heads, HD
            ),
            cosv,
            sinv,
        ).astype(jnp.bfloat16)
        forward_values = (
            joined_proj[:, 2 * local_width :]
            .reshape(forward_block_len, local_heads, HD)
            .astype(jnp.bfloat16)
        )
        blocked = (sub_blocks, MB, local_heads, HD)
        forward_scores = (
            jnp.einsum(
                "bqhd,bkhd->bhqk",
                forward_queries.reshape(blocked),
                forward_keys_rot.reshape(blocked),
                preferred_element_type=jnp.float32,
            )
            * score_scale
        )
        forward_scores = jnp.where(allowed_keys(segment)[:, None], forward_scores, MASKED)
        row_top = jnp.max(forward_scores, axis=3, keepdims=True)
        exponent = jnp.exp(forward_scores - row_top)
        row_total = jnp.sum(exponent, axis=3, keepdims=True)
        forward_log_total = row_top + jnp.log(row_total)
        weights_low = (exponent / row_total).astype(jnp.bfloat16)
        forward_context = jnp.einsum(
            "bhqk,bkhd->bqhd",
            weights_low,
            forward_values.reshape(blocked),
            preferred_element_type=jnp.float32,
        )
        forward_context = forward_context.reshape(forward_block_len, local_width).astype(
            jnp.bfloat16
        )
        forward_up_proj = (
            jnp.dot(forward_h_mlp, up_mat, preferred_element_type=jnp.float32) + up_add
        )
        forward_activated = exact_gelu(forward_up_proj).astype(jnp.bfloat16)
        partial_value = jnp.dot(forward_context, dense_mat, preferred_element_type=jnp.float32)
        partial_value = partial_value + jnp.dot(
            forward_activated, down_mat, preferred_element_type=jnp.float32
        )
        branches = tensor_scatter_sum(partial_value.astype(jnp.bfloat16))
        column_start = lax.axis_index("tensor") * quarter
        own_inputs = lax.dynamic_slice_in_dim(inputs, column_start, quarter, 1)
        own_bias = lax.dynamic_slice_in_dim(bias_sum, column_start, quarter, 0)
        result = own_inputs + branches + own_bias
        forward_stored = (
            forward_normed,
            forward_inv_scale,
            forward_h_attn,
            forward_h_mlp,
            forward_queries,
            forward_keys_rot,
            forward_values,
            forward_log_total,
            forward_context,
            forward_up_proj,
            forward_activated,
        )
        result, stored = (result, forward_stored)
        result_low = result.astype(jnp.bfloat16)
        tick_outputs.append(result_low)
        tick_stored.append((stored, segment, cosv, sinv))
        if section_tick < NMB:
            received = cross_gather(result_low, 0)
    section_rows = jnp.concatenate(
        [jnp.where(leading, tick_outputs[block], tick_outputs[block + 1]) for block in range(NMB)],
        axis=0,
    )
    section_out = section_rows[None]
    returned = jnp.zeros((tick_rows, model_width), jnp.bfloat16)
    tick_grads = []
    totals = None
    for section_tick in range(NMB + 1):
        own_block = min(section_tick, NMB - 1)
        late_tick = max(section_tick - 1, 0)
        upper_tick = min(section_tick + 1, NMB)
        from_output = output_grads[own_block * tick_rows : (own_block + 1) * tick_rows]
        if section_tick == NMB:
            from_output = jnp.zeros_like(from_output)
        grad_rows = jnp.where(leading, returned, from_output)
        stored, segment, cosv, sinv = pick(tick_stored[late_tick], tick_stored[upper_tick])
        (
            normed,
            inv_scale,
            h_attn,
            h_mlp,
            queries,
            keys_rot,
            values,
            log_total,
            context,
            up_proj,
            activated,
        ) = stored
        block_len = grad_rows.shape[0]
        grad_wide = grad_rows.astype(jnp.float32)
        column_sum = jnp.sum(grad_wide, axis=0)
        backward_grad_dense = contract_rows(context, grad_rows)
        backward_grad_down = contract_rows(activated, grad_rows)
        d_context = contract_cols(grad_rows, dense_mat).astype(jnp.bfloat16)
        d_act = contract_cols(grad_rows, down_mat)
        unused, slope_back = jax.vjp(exact_gelu, up_proj)
        d_up = slope_back(d_act)[0].astype(jnp.bfloat16)
        grad_up_add = jnp.sum(d_up.astype(jnp.float32), axis=0)
        backward_grad_up = contract_rows(h_mlp, d_up)
        d_hmlp = contract_cols(d_up, up_mat)
        blocked = (sub_blocks, MB, local_heads, HD)
        queries_b = queries.reshape(blocked)
        keys_b = keys_rot.reshape(blocked)
        scores = (
            jnp.einsum("bqhd,bkhd->bhqk", queries_b, keys_b, preferred_element_type=jnp.float32)
            * score_scale
        )
        scores = jnp.where(allowed_keys(segment)[:, None], scores, MASKED)
        weights_soft = jnp.exp(scores - log_total)
        d_context3 = d_context.reshape(blocked)
        d_values = jnp.einsum(
            "bhqk,bqhd->bkhd",
            weights_soft.astype(jnp.bfloat16),
            d_context3,
            preferred_element_type=jnp.float32,
        ).astype(jnp.bfloat16)
        d_weights = jnp.einsum(
            "bqhd,bkhd->bhqk", d_context3, values.reshape(blocked), preferred_element_type=jnp.float32
        )
        row_delta = jnp.sum(weights_soft * d_weights, axis=3, keepdims=True)
        d_scores = (weights_soft * (d_weights - row_delta)).astype(jnp.bfloat16)
        heads_shape = (block_len, local_heads, HD)
        d_queries = (
            jnp.einsum("bhqk,bkhd->bqhd", d_scores, keys_b, preferred_element_type=jnp.float32)
            * score_scale
        ).reshape(heads_shape)
        d_keys = (
            jnp.einsum("bhqk,bqhd->bkhd", d_scores, queries_b, preferred_element_type=jnp.float32)
            * score_scale
        ).reshape(heads_shape)
        d_queries = (
            rotate_back(d_queries, cosv, sinv).reshape(block_len, local_width).astype(jnp.bfloat16)
        )
        d_keys = (
            rotate_back(d_keys, cosv, sinv).reshape(block_len, local_width).astype(jnp.bfloat16)
        )
        d_joined = jnp.concatenate(
            [d_queries, d_keys, d_values.reshape(block_len, local_width)], axis=1
        )
        grad_joined_add = jnp.sum(d_joined.astype(jnp.float32), axis=0)
        backward_grad_joined = contract_rows(d_joined, h_attn)
        d_hattn = contract_cols(d_joined, joined_mat)
        grad_gains = jnp.concatenate(
            [jnp.sum(d_hattn * normed, axis=0), jnp.sum(d_hmlp * normed, axis=0)]
        )
        grad_shifts = jnp.concatenate([jnp.sum(d_hattn, axis=0), jnp.sum(d_hmlp, axis=0)])
        d_norm = tensor_scatter_sum(
            (d_hattn * ln_gains[0] + d_hmlp * ln_gains[1]).astype(jnp.bfloat16)
        )
        column_start = lax.axis_index("tensor") * quarter
        own_normed = lax.dynamic_slice_in_dim(normed, column_start, quarter, 1)
        own_grad = lax.dynamic_slice_in_dim(grad_wide, column_start, quarter, 1)
        row_stats = tensor_sum(
            jnp.concatenate(
                [
                    jnp.sum(d_norm, axis=1, keepdims=True),
                    jnp.sum(d_norm * own_normed, axis=1, keepdims=True),
                ],
                axis=1,
            )
        ) / model_width
        grad_input = own_grad + inv_scale * (
            d_norm - row_stats[:, 0:1] - own_normed * row_stats[:, 1:2]
        )
        small_terms = jnp.concatenate(
            [grad_gains, grad_shifts, column_sum, column_sum, grad_joined_add, grad_up_add]
        )
        terms = (
            backward_grad_joined[None],
            backward_grad_dense[None],
            backward_grad_up[None],
            backward_grad_down[None],
            small_terms[None],
        )
        grad_input, terms = (grad_input, terms)
        grad_low = grad_input.astype(jnp.bfloat16)
        tick_grads.append(grad_low)
        if totals is None:
            totals = terms
        else:
            totals = jax.tree.map(lambda older, newer: older + newer, totals, terms)
        if section_tick < NMB:
            returned = cross_gather(grad_low, 1)
    small_rows = totals[4][0]
    small_pad = (-small_rows.shape[0]) % model_width
    small_rows = jnp.pad(small_rows, (0, small_pad)).reshape(-1, model_width)
    early = jnp.concatenate(
        [totals[1][0], totals[2][0], totals[3][0]], axis=0
    ).astype(jnp.bfloat16)
    early = lax.psum(early, "dp").astype(jnp.float32)
    late = jnp.concatenate([totals[0][0], small_rows], axis=0).astype(jnp.bfloat16)
    late = late + (early[0:1, 0:1] * 0).astype(jnp.bfloat16)
    late = lax.psum(late, "dp").astype(jnp.float32)
    dense_rows = totals[1].shape[1]
    up_rows = totals[2].shape[1]
    joined_rows = totals[0].shape[1]
    summed = [
        late[:joined_rows],
        early[:dense_rows],
        early[dense_rows : dense_rows + up_rows],
        early[dense_rows + up_rows :],
        late[joined_rows:],
    ]
    grad_rows_all = jnp.concatenate(
        [jnp.where(leading, tick_grads[block + 1], tick_grads[block]) for block in range(NMB)],
        axis=0,
    )
    input_grad = grad_rows_all[None]
    grad_joined = summed[0].T.reshape(1, model_width, 3, local_width)
    grad_dense = summed[1][None]
    grad_up = summed[2][None]
    grad_down = summed[3][None]
    small_sum = summed[4].reshape(-1)
    ln_sum = tensor_sum(small_sum[: 4 * model_width])
    grad_ln_gain = ln_sum[: 2 * model_width].reshape(1, 2, model_width)
    grad_ln_bias = ln_sum[2 * model_width :].reshape(1, 2, model_width)
    offset = 4 * model_width
    grad_output_bias = small_sum[offset : offset + 2 * model_width].reshape(1, 2, model_width)
    offset = offset + 2 * model_width
    grad_joined_bias = small_sum[offset : offset + 3 * local_width].reshape(1, 3, local_width)
    offset = offset + 3 * local_width
    grad_up_bias = small_sum[offset : offset + hidden_local].reshape(1, hidden_local)
    return (
        section_out,
        input_grad,
        grad_ln_gain,
        grad_ln_bias,
        grad_joined,
        grad_joined_bias,
        grad_dense,
        grad_up,
        grad_up_bias,
        grad_down,
        grad_output_bias,
    )


def solution(mesh):
    placed = (
        P("dp", "tensor"),
        P("dp", None),
        P("pipe", None, None),
        P("pipe", None, None),
        P("pipe", None, None, "tensor"),
        P("pipe", None, "tensor"),
        P("pipe", "tensor", None),
        P("pipe", None, "tensor"),
        P("pipe", "tensor"),
        P("pipe", "tensor", None),
        P("pipe", None, None),
        P("dp", "tensor"),
    )
    return jax.shard_map(
        per_device,
        mesh=mesh,
        in_specs=placed,
        out_specs=(
            P("pipe", "dp", "tensor"),
            P("pipe", "dp", "tensor"),
            P("pipe", None, None),
            P("pipe", None, None),
            P("pipe", None, None, "tensor"),
            P("pipe", None, "tensor"),
            P("pipe", "tensor", None),
            P("pipe", None, "tensor"),
            P("pipe", "tensor"),
            P("pipe", "tensor", None),
            P("pipe", None, None),
        ),
        check_vma=False,
    )
```

```python
import jax
import jax.numpy as jnp
from jax import lax
from jax.sharding import PartitionSpec as P

HD = 64
ROT = 16
MB = 128
NMB = 2


EPSILON = 1e-05
MASKED = -1e30


def passed_along(x, axis, by):
    peers = lax.axis_size(axis)
    pairs = [(i, i + by) for i in range(peers) if 0 <= i + by < peers]
    return lax.ppermute(x, axis, pairs)


def tensor_pieces(x):
    peers = lax.axis_size("tensor")
    me = lax.axis_index("tensor")
    parts = [x]
    for shift in range(1, peers):
        pairs = [(i, (i + shift) % peers) for i in range(peers)]
        parts.append(lax.ppermute(x, "tensor", pairs))
    ordered = []
    for owner in range(peers):
        slot = (me - owner) % peers
        chosen = parts[peers - 1]
        for k in range(peers - 2, -1, -1):
            chosen = jnp.where(slot == k, parts[k], chosen)
        ordered.append(chosen)
    return ordered


def tensor_sum(x):
    pieces = tensor_pieces(x)
    total = pieces[0].astype(jnp.float32)
    for piece in pieces[1:]:
        total = total + piece.astype(jnp.float32)
    return total

def ordered_by_owner(parts, me, peers):
    ordered = []
    for owner in range(peers):
        slot = (me - owner) % peers
        chosen = parts[peers - 1]
        for k in range(peers - 2, -1, -1):
            chosen = jnp.where(slot == k, parts[k], chosen)
        ordered.append(chosen)
    return ordered


def tensor_scatter_sum(x):
    peers = lax.axis_size("tensor")
    me = lax.axis_index("tensor")
    width = x.shape[1] // peers

    def piece_for(owner):
        return lax.dynamic_slice_in_dim(x, owner * width, width, 1)

    parts = [piece_for(me)]
    for shift in range(1, peers):
        pairs = [(i, (i + shift) % peers) for i in range(peers)]
        parts.append(lax.ppermute(piece_for((me + shift) % peers), "tensor", pairs))
    ordered = ordered_by_owner(parts, me, peers)
    total = ordered[0].astype(jnp.float32)
    for piece in ordered[1:]:
        total = total + piece.astype(jnp.float32)
    return total


def cross_gather(x, source_stage):
    peers = lax.axis_size("tensor")
    me = lax.axis_index("tensor")
    target_stage = 1 - source_stage
    parts = []
    for shift in range(peers):
        pairs = [
            (source_stage * peers + i, target_stage * peers + (i + shift) % peers)
            for i in range(peers)
        ]
        parts.append(lax.ppermute(x, ("pipe", "tensor"), pairs))
    return jnp.concatenate(ordered_by_owner(parts, me, peers), axis=1)


def as_sent(x):
    return jax.tree.map(lambda a: a.astype(jnp.bfloat16) if a.dtype == jnp.float32 else a, x)


def positions(lengths, block_rows):
    seq_count = lengths.shape[1]
    counter = jnp.arange(seq_count, dtype=jnp.int32)
    lower_tri = (counter[:, None] >= counter[None, :]).astype(jnp.int32)
    seg_ends = jnp.sum(lengths[:, None, :] * lower_tri[None, :, :], axis=2)
    starts = seg_ends - lengths
    row_index = jnp.arange(block_rows, dtype=jnp.int32)
    segment = jnp.sum((row_index[None, :, None] >= seg_ends[:, None, :]).astype(jnp.int32), axis=2)
    member = (segment[:, :, None] == counter[None, None, :]).astype(jnp.int32)
    place = row_index[None, :] - jnp.sum(member * starts[:, None, :], axis=2)
    return (segment, place)


def rotary(place):
    half_rot = ROT // 2
    inv_freq = jnp.power(10000.0, -2.0 * jnp.arange(half_rot, dtype=jnp.float32) / ROT)
    angles = place.astype(jnp.float32)[..., None] * inv_freq
    return (jnp.cos(angles), jnp.sin(angles))


def rotate(heads_in, cosv, sinv):
    half_rot = ROT // 2
    first_half = heads_in[..., :half_rot]
    second_half = heads_in[..., half_rot:ROT]
    cos_rows = cosv[:, None, :]
    sin_rows = sinv[:, None, :]
    return jnp.concatenate(
        [
            first_half * cos_rows - second_half * sin_rows,
            second_half * cos_rows + first_half * sin_rows,
            heads_in[..., ROT:],
        ],
        axis=-1,
    )


def rotate_back(heads_in, cosv, sinv):
    half_rot = ROT // 2
    first_half = heads_in[..., :half_rot]
    second_half = heads_in[..., half_rot:ROT]
    cos_rows = cosv[:, None, :]
    sin_rows = sinv[:, None, :]
    return jnp.concatenate(
        [
            first_half * cos_rows + second_half * sin_rows,
            second_half * cos_rows - first_half * sin_rows,
            heads_in[..., ROT:],
        ],
        axis=-1,
    )


def exact_gelu(values):
    return jax.nn.gelu(values, approximate=False)


def allowed_keys(segment):
    row_index = jnp.arange(segment.shape[-1], dtype=jnp.int32)
    same = segment[..., :, None] == segment[..., None, :]
    return same & (row_index[None, :] <= row_index[:, None])


def contract_rows(left, right):
    return lax.dot_general(
        left, right, (((0,), (0,)), ((), ())), preferred_element_type=jnp.float32
    )


def contract_cols(left, right):
    return lax.dot_general(
        left, right, (((1,), (1,)), ((), ())), preferred_element_type=jnp.float32
    )


def per_device(
    tokens,
    lengths,
    ln_gain,
    ln_bias,
    joined_weight,
    joined_bias,
    dense_weight,
    up_weight,
    up_bias,
    down_weight,
    output_bias,
    cotangent,
):
    leading = lax.axis_index("pipe") == 0
    model_width = joined_weight.shape[1]
    local_width = joined_weight.shape[3]
    local_heads = local_width // HD
    hidden_local = up_weight.shape[2]
    quarter = tokens.shape[1]
    score_scale = HD ** (-0.5)
    ln_gains = ln_gain[0].astype(jnp.float32)
    ln_shifts = ln_bias[0].astype(jnp.float32)
    joined_mat = joined_weight[0].reshape(model_width, 3 * local_width)
    joined_add = joined_bias[0].astype(jnp.float32).reshape(3 * local_width)
    dense_mat = dense_weight[0]
    up_mat = up_weight[0]
    up_add = up_bias[0].astype(jnp.float32)
    down_mat = down_weight[0]
    bias_sum = output_bias[0, 0].astype(jnp.float32) + output_bias[0, 1].astype(jnp.float32)
    gathered_pieces = tensor_pieces(jnp.concatenate([tokens, cotangent], axis=0))
    gathered_rows = jnp.concatenate(gathered_pieces, axis=1)
    input_rows = gathered_rows[: tokens.shape[0]]
    output_grads = gathered_rows[tokens.shape[0] :]
    tick_rows = tokens.shape[0] // NMB
    sub_blocks = tick_rows // MB
    segment_all, place_all = positions(lengths, MB)
    cos_all, sin_all = rotary(place_all)
    segment_all = segment_all.reshape(NMB, sub_blocks, MB)
    cos_all = cos_all.reshape(NMB, tick_rows, cos_all.shape[-1])
    sin_all = sin_all.reshape(NMB, tick_rows, sin_all.shape[-1])

    def pick(early_val, late_val):
        return jax.tree.map(
            lambda upper_val, lower_val: jnp.where(leading, upper_val, lower_val),
            early_val,
            late_val,
        )

    received = jnp.zeros((tick_rows, model_width), jnp.bfloat16)
    tick_outputs = []
    tick_stored = []
    for section_tick in range(NMB + 1):
        early_block = min(section_tick, NMB - 1)
        late_block = max(section_tick - 1, 0)
        block_rows = jnp.where(
            leading, input_rows[early_block * tick_rows : (early_block + 1) * tick_rows], received
        )
        segment, cosv, sinv = pick(
            (segment_all[early_block], cos_all[early_block], sin_all[early_block]),
            (segment_all[late_block], cos_all[late_block], sin_all[late_block]),
        )
        inputs = block_rows.astype(jnp.float32)
        row_mean = jnp.mean(inputs, axis=1, keepdims=True)
        centred = inputs - row_mean
        forward_inv_scale = lax.rsqrt(jnp.mean(centred * centred, axis=1, keepdims=True) + EPSILON)
        forward_normed = centred * forward_inv_scale
        forward_h_attn = (forward_normed * ln_gains[0] + ln_shifts[0]).astype(jnp.bfloat16)
        forward_h_mlp = (forward_normed * ln_gains[1] + ln_shifts[1]).astype(jnp.bfloat16)
        joined_proj = (
            jnp.dot(forward_h_attn, joined_mat, preferred_element_type=jnp.float32) + joined_add
        )
        forward_block_len = block_rows.shape[0]
        forward_queries = rotate(
            joined_proj[:, :local_width].reshape(forward_block_len, local_heads, HD), cosv, sinv
        ).astype(jnp.bfloat16)
        forward_keys_rot = rotate(
            joined_proj[:, local_width : 2 * local_width].reshape(
                forward_block_len, local_heads, HD
            ),
            cosv,
            sinv,
        ).astype(jnp.bfloat16)
        forward_values = (
            joined_proj[:, 2 * local_width :]
            .reshape(forward_block_len, local_heads, HD)
            .astype(jnp.bfloat16)
        )
        blocked = (sub_blocks, MB, local_heads, HD)
        forward_scores = (
            jnp.einsum(
                "bqhd,bkhd->bhqk",
                forward_queries.reshape(blocked),
                forward_keys_rot.reshape(blocked),
                preferred_element_type=jnp.float32,
            )
            * score_scale
        )
        forward_scores = jnp.where(allowed_keys(segment)[:, None], forward_scores, MASKED)
        row_top = jnp.max(forward_scores, axis=3, keepdims=True)
        exponent = jnp.exp(forward_scores - row_top)
        row_total = jnp.sum(exponent, axis=3, keepdims=True)
        forward_log_total = row_top + jnp.log(row_total)
        weights_low = (exponent / row_total).astype(jnp.bfloat16)
        forward_context = jnp.einsum(
            "bhqk,bkhd->bqhd",
            weights_low,
            forward_values.reshape(blocked),
            preferred_element_type=jnp.float32,
        )
        forward_context = forward_context.reshape(forward_block_len, local_width).astype(
            jnp.bfloat16
        )
        forward_up_proj = (
            jnp.dot(forward_h_mlp, up_mat, preferred_element_type=jnp.float32) + up_add
        )
        forward_activated = exact_gelu(forward_up_proj).astype(jnp.bfloat16)
        partial_value = jnp.dot(forward_context, dense_mat, preferred_element_type=jnp.float32)
        partial_value = partial_value + jnp.dot(
            forward_activated, down_mat, preferred_element_type=jnp.float32
        )
        branches = tensor_scatter_sum(partial_value.astype(jnp.bfloat16))
        column_start = lax.axis_index("tensor") * quarter
        own_inputs = lax.dynamic_slice_in_dim(inputs, column_start, quarter, 1)
        own_bias = lax.dynamic_slice_in_dim(bias_sum, column_start, quarter, 0)
        result = own_inputs + branches + own_bias
        forward_stored = (
            forward_normed,
            forward_inv_scale,
            forward_h_attn,
            forward_h_mlp,
            forward_queries,
            forward_keys_rot,
            forward_values,
            forward_log_total,
            forward_context,
            forward_up_proj,
            forward_activated,
        )
        result, stored = (result, forward_stored)
        result_low = result.astype(jnp.bfloat16)
        tick_outputs.append(result_low)
        tick_stored.append((stored, segment, cosv, sinv))
        if section_tick < NMB:
            received = cross_gather(result_low, 0)
    section_rows = jnp.concatenate(
        [jnp.where(leading, tick_outputs[block], tick_outputs[block + 1]) for block in range(NMB)],
        axis=0,
    )
    section_out = section_rows[None]
    returned = jnp.zeros((tick_rows, model_width), jnp.bfloat16)
    tick_grads = []
    totals = None
    for section_tick in range(NMB + 1):
        own_block = min(section_tick, NMB - 1)
        late_tick = max(section_tick - 1, 0)
        upper_tick = min(section_tick + 1, NMB)
        from_output = output_grads[own_block * tick_rows : (own_block + 1) * tick_rows]
        if section_tick == NMB:
            from_output = jnp.zeros_like(from_output)
        grad_rows = jnp.where(leading, returned, from_output)
        stored, segment, cosv, sinv = pick(tick_stored[late_tick], tick_stored[upper_tick])
        (
            normed,
            inv_scale,
            h_attn,
            h_mlp,
            queries,
            keys_rot,
            values,
            log_total,
            context,
            up_proj,
            activated,
        ) = stored
        block_len = grad_rows.shape[0]
        grad_wide = grad_rows.astype(jnp.float32)
        column_sum = jnp.sum(grad_wide, axis=0)
        backward_grad_dense = contract_rows(context, grad_rows)
        backward_grad_down = contract_rows(activated, grad_rows)
        d_context = contract_cols(grad_rows, dense_mat).astype(jnp.bfloat16)
        d_act = contract_cols(grad_rows, down_mat)
        unused, slope_back = jax.vjp(exact_gelu, up_proj)
        d_up = slope_back(d_act)[0].astype(jnp.bfloat16)
        grad_up_add = jnp.sum(d_up.astype(jnp.float32), axis=0)
        backward_grad_up = contract_rows(h_mlp, d_up)
        d_hmlp = contract_cols(d_up, up_mat)
        blocked = (sub_blocks, MB, local_heads, HD)
        queries_b = queries.reshape(blocked)
        keys_b = keys_rot.reshape(blocked)
        scores = (
            jnp.einsum("bqhd,bkhd->bhqk", queries_b, keys_b, preferred_element_type=jnp.float32)
            * score_scale
        )
        scores = jnp.where(allowed_keys(segment)[:, None], scores, MASKED)
        weights_soft = jnp.exp(scores - log_total)
        d_context3 = d_context.reshape(blocked)
        d_values = jnp.einsum(
            "bhqk,bqhd->bkhd",
            weights_soft.astype(jnp.bfloat16),
            d_context3,
            preferred_element_type=jnp.float32,
        ).astype(jnp.bfloat16)
        d_weights = jnp.einsum(
            "bqhd,bkhd->bhqk", d_context3, values.reshape(blocked), preferred_element_type=jnp.float32
        )
        row_delta = jnp.sum(weights_soft * d_weights, axis=3, keepdims=True)
        d_scores = (weights_soft * (d_weights - row_delta)).astype(jnp.bfloat16)
        heads_shape = (block_len, local_heads, HD)
        d_queries = (
            jnp.einsum("bhqk,bkhd->bqhd", d_scores, keys_b, preferred_element_type=jnp.float32)
            * score_scale
        ).reshape(heads_shape)
        d_keys = (
            jnp.einsum("bhqk,bqhd->bkhd", d_scores, queries_b, preferred_element_type=jnp.float32)
            * score_scale
        ).reshape(heads_shape)
        d_queries = (
            rotate_back(d_queries, cosv, sinv).reshape(block_len, local_width).astype(jnp.bfloat16)
        )
        d_keys = (
            rotate_back(d_keys, cosv, sinv).reshape(block_len, local_width).astype(jnp.bfloat16)
        )
        d_joined = jnp.concatenate(
            [d_queries, d_keys, d_values.reshape(block_len, local_width)], axis=1
        )
        grad_joined_add = jnp.sum(d_joined.astype(jnp.float32), axis=0)
        backward_grad_joined = contract_rows(d_joined, h_attn)
        d_hattn = contract_cols(d_joined, joined_mat)
        grad_gains = jnp.concatenate(
            [jnp.sum(d_hattn * normed, axis=0), jnp.sum(d_hmlp * normed, axis=0)]
        )
        grad_shifts = jnp.concatenate([jnp.sum(d_hattn, axis=0), jnp.sum(d_hmlp, axis=0)])
        d_norm_part = d_hattn * ln_gains[0] + d_hmlp * ln_gains[1]
        row_stats = tensor_sum(
            jnp.concatenate(
                [
                    jnp.sum(d_norm_part, axis=1, keepdims=True),
                    jnp.sum(d_norm_part * normed, axis=1, keepdims=True),
                ],
                axis=1,
            )
        ) / model_width
        d_norm = tensor_scatter_sum(d_norm_part.astype(jnp.bfloat16))
        column_start = lax.axis_index("tensor") * quarter
        own_normed = lax.dynamic_slice_in_dim(normed, column_start, quarter, 1)
        own_grad = lax.dynamic_slice_in_dim(grad_wide, column_start, quarter, 1)
        grad_input = own_grad + inv_scale * (
            d_norm - row_stats[:, 0:1] - own_normed * row_stats[:, 1:2]
        )
        small_terms = jnp.concatenate(
            [grad_gains, grad_shifts, column_sum, column_sum, grad_joined_add, grad_up_add]
        )
        terms = (
            backward_grad_joined[None],
            backward_grad_dense[None],
            backward_grad_up[None],
            backward_grad_down[None],
            small_terms[None],
        )
        grad_input, terms = (grad_input, terms)
        grad_low = grad_input.astype(jnp.bfloat16)
        tick_grads.append(grad_low)
        if totals is None:
            totals = terms
        else:
            totals = jax.tree.map(lambda older, newer: older + newer, totals, terms)
        if section_tick < NMB:
            returned = cross_gather(grad_low, 1)
    small_rows = totals[4][0]
    small_pad = (-small_rows.shape[0]) % model_width
    small_rows = jnp.pad(small_rows, (0, small_pad)).reshape(-1, model_width)
    pieces = (totals[0][0], totals[1][0], totals[2][0], totals[3][0], small_rows)
    slab = jnp.concatenate([piece.astype(jnp.bfloat16) for piece in pieces], axis=0)
    slab = lax.psum(slab, "dp").astype(jnp.float32)
    summed = []
    offset = 0
    for piece in pieces:
        summed.append(slab[offset : offset + piece.shape[0]])
        offset = offset + piece.shape[0]
    grad_rows_all = jnp.concatenate(
        [jnp.where(leading, tick_grads[block + 1], tick_grads[block]) for block in range(NMB)],
        axis=0,
    )
    input_grad = grad_rows_all[None]
    grad_joined = summed[0].T.reshape(1, model_width, 3, local_width)
    grad_dense = summed[1][None]
    grad_up = summed[2][None]
    grad_down = summed[3][None]
    small_sum = summed[4].reshape(-1)
    ln_sum = tensor_sum(small_sum[: 4 * model_width])
    grad_ln_gain = ln_sum[: 2 * model_width].reshape(1, 2, model_width)
    grad_ln_bias = ln_sum[2 * model_width :].reshape(1, 2, model_width)
    offset = 4 * model_width
    grad_output_bias = small_sum[offset : offset + 2 * model_width].reshape(1, 2, model_width)
    offset = offset + 2 * model_width
    grad_joined_bias = small_sum[offset : offset + 3 * local_width].reshape(1, 3, local_width)
    offset = offset + 3 * local_width
    grad_up_bias = small_sum[offset : offset + hidden_local].reshape(1, hidden_local)
    return (
        section_out,
        input_grad,
        grad_ln_gain,
        grad_ln_bias,
        grad_joined,
        grad_joined_bias,
        grad_dense,
        grad_up,
        grad_up_bias,
        grad_down,
        grad_output_bias,
    )


def solution(mesh):
    placed = (
        P("dp", "tensor"),
        P("dp", None),
        P("pipe", None, None),
        P("pipe", None, None),
        P("pipe", None, None, "tensor"),
        P("pipe", None, "tensor"),
        P("pipe", "tensor", None),
        P("pipe", None, "tensor"),
        P("pipe", "tensor"),
        P("pipe", "tensor", None),
        P("pipe", None, None),
        P("dp", "tensor"),
    )
    return jax.shard_map(
        per_device,
        mesh=mesh,
        in_specs=placed,
        out_specs=(
            P("pipe", "dp", "tensor"),
            P("pipe", "dp", "tensor"),
            P("pipe", None, None),
            P("pipe", None, None),
            P("pipe", None, None, "tensor"),
            P("pipe", None, "tensor"),
            P("pipe", "tensor", None),
            P("pipe", None, "tensor"),
            P("pipe", "tensor"),
            P("pipe", "tensor", None),
            P("pipe", None, None),
        ),
        check_vma=False,
    )
```

```python
import jax
import jax.numpy as jnp
from jax import lax
from jax.sharding import PartitionSpec as P

HD = 64
ROT = 16
MB = 128
NMB = 2


EPSILON = 1e-05
MASKED = -1e30


def passed_along(x, axis, by):
    peers = lax.axis_size(axis)
    pairs = [(i, i + by) for i in range(peers) if 0 <= i + by < peers]
    return lax.ppermute(x, axis, pairs)


def tensor_pieces(x):
    peers = lax.axis_size("tensor")
    me = lax.axis_index("tensor")
    parts = [x]
    for shift in range(1, peers):
        pairs = [(i, (i + shift) % peers) for i in range(peers)]
        parts.append(lax.ppermute(x, "tensor", pairs))
    ordered = []
    for owner in range(peers):
        slot = (me - owner) % peers
        chosen = parts[peers - 1]
        for k in range(peers - 2, -1, -1):
            chosen = jnp.where(slot == k, parts[k], chosen)
        ordered.append(chosen)
    return ordered


def tensor_sum(x):
    pieces = tensor_pieces(x)
    total = pieces[0].astype(jnp.float32)
    for piece in pieces[1:]:
        total = total + piece.astype(jnp.float32)
    return total

def ordered_by_owner(parts, me, peers):
    ordered = []
    for owner in range(peers):
        slot = (me - owner) % peers
        chosen = parts[peers - 1]
        for k in range(peers - 2, -1, -1):
            chosen = jnp.where(slot == k, parts[k], chosen)
        ordered.append(chosen)
    return ordered


def tensor_scatter_sum(x):
    peers = lax.axis_size("tensor")
    me = lax.axis_index("tensor")
    width = x.shape[1] // peers

    def piece_for(owner):
        return lax.dynamic_slice_in_dim(x, owner * width, width, 1)

    parts = [piece_for(me)]
    for shift in range(1, peers):
        pairs = [(i, (i + shift) % peers) for i in range(peers)]
        parts.append(lax.ppermute(piece_for((me + shift) % peers), "tensor", pairs))
    ordered = ordered_by_owner(parts, me, peers)
    total = ordered[0].astype(jnp.float32)
    for piece in ordered[1:]:
        total = total + piece.astype(jnp.float32)
    return total


def cross_gather(x, source_stage):
    peers = lax.axis_size("tensor")
    me = lax.axis_index("tensor")
    target_stage = 1 - source_stage
    parts = []
    for shift in range(peers):
        pairs = [
            (source_stage * peers + i, target_stage * peers + (i + shift) % peers)
            for i in range(peers)
        ]
        parts.append(lax.ppermute(x, ("pipe", "tensor"), pairs))
    return jnp.concatenate(ordered_by_owner(parts, me, peers), axis=1)


def as_sent(x):
    return jax.tree.map(lambda a: a.astype(jnp.bfloat16) if a.dtype == jnp.float32 else a, x)


def positions(lengths, block_rows):
    seq_count = lengths.shape[1]
    counter = jnp.arange(seq_count, dtype=jnp.int32)
    lower_tri = (counter[:, None] >= counter[None, :]).astype(jnp.int32)
    seg_ends = jnp.sum(lengths[:, None, :] * lower_tri[None, :, :], axis=2)
    starts = seg_ends - lengths
    row_index = jnp.arange(block_rows, dtype=jnp.int32)
    segment = jnp.sum((row_index[None, :, None] >= seg_ends[:, None, :]).astype(jnp.int32), axis=2)
    member = (segment[:, :, None] == counter[None, None, :]).astype(jnp.int32)
    place = row_index[None, :] - jnp.sum(member * starts[:, None, :], axis=2)
    return (segment, place)


def rotary(place):
    half_rot = ROT // 2
    inv_freq = jnp.power(10000.0, -2.0 * jnp.arange(half_rot, dtype=jnp.float32) / ROT)
    angles = place.astype(jnp.float32)[..., None] * inv_freq
    return (jnp.cos(angles), jnp.sin(angles))


def rotate(heads_in, cosv, sinv):
    half_rot = ROT // 2
    first_half = heads_in[..., :half_rot]
    second_half = heads_in[..., half_rot:ROT]
    cos_rows = cosv[:, None, :]
    sin_rows = sinv[:, None, :]
    return jnp.concatenate(
        [
            first_half * cos_rows - second_half * sin_rows,
            second_half * cos_rows + first_half * sin_rows,
            heads_in[..., ROT:],
        ],
        axis=-1,
    )


def rotate_back(heads_in, cosv, sinv):
    half_rot = ROT // 2
    first_half = heads_in[..., :half_rot]
    second_half = heads_in[..., half_rot:ROT]
    cos_rows = cosv[:, None, :]
    sin_rows = sinv[:, None, :]
    return jnp.concatenate(
        [
            first_half * cos_rows + second_half * sin_rows,
            second_half * cos_rows - first_half * sin_rows,
            heads_in[..., ROT:],
        ],
        axis=-1,
    )


def exact_gelu(values):
    return jax.nn.gelu(values, approximate=False)


def allowed_keys(segment):
    row_index = jnp.arange(segment.shape[-1], dtype=jnp.int32)
    same = segment[..., :, None] == segment[..., None, :]
    return same & (row_index[None, :] <= row_index[:, None])


def contract_rows(left, right):
    return lax.dot_general(
        left, right, (((0,), (0,)), ((), ())), preferred_element_type=jnp.float32
    )


def contract_cols(left, right):
    return lax.dot_general(
        left, right, (((1,), (1,)), ((), ())), preferred_element_type=jnp.float32
    )


def per_device(
    tokens,
    lengths,
    ln_gain,
    ln_bias,
    joined_weight,
    joined_bias,
    dense_weight,
    up_weight,
    up_bias,
    down_weight,
    output_bias,
    cotangent,
):
    leading = lax.axis_index("pipe") == 0
    model_width = joined_weight.shape[1]
    local_width = joined_weight.shape[3]
    local_heads = local_width // HD
    hidden_local = up_weight.shape[2]
    quarter = tokens.shape[1]
    score_scale = HD ** (-0.5)
    ln_gains = ln_gain[0].astype(jnp.float32)
    ln_shifts = ln_bias[0].astype(jnp.float32)
    joined_mat = joined_weight[0].reshape(model_width, 3 * local_width)
    joined_add = joined_bias[0].astype(jnp.float32).reshape(3 * local_width)
    dense_mat = dense_weight[0]
    up_mat = up_weight[0]
    up_add = up_bias[0].astype(jnp.float32)
    down_mat = down_weight[0]
    bias_sum = output_bias[0, 0].astype(jnp.float32) + output_bias[0, 1].astype(jnp.float32)
    gathered_pieces = tensor_pieces(jnp.concatenate([tokens, cotangent], axis=0))
    gathered_rows = jnp.concatenate(gathered_pieces, axis=1)
    input_rows = gathered_rows[: tokens.shape[0]]
    output_grads = gathered_rows[tokens.shape[0] :]
    tick_rows = tokens.shape[0] // NMB
    sub_blocks = tick_rows // MB
    segment_all, place_all = positions(lengths, MB)
    cos_all, sin_all = rotary(place_all)
    segment_all = segment_all.reshape(NMB, sub_blocks, MB)
    cos_all = cos_all.reshape(NMB, tick_rows, cos_all.shape[-1])
    sin_all = sin_all.reshape(NMB, tick_rows, sin_all.shape[-1])

    def pick(early_val, late_val):
        return jax.tree.map(
            lambda upper_val, lower_val: jnp.where(leading, upper_val, lower_val),
            early_val,
            late_val,
        )

    received = jnp.zeros((tick_rows, model_width), jnp.bfloat16)
    tick_outputs = []
    tick_stored = []
    for section_tick in range(NMB + 1):
        early_block = min(section_tick, NMB - 1)
        late_block = max(section_tick - 1, 0)
        block_rows = jnp.where(
            leading, input_rows[early_block * tick_rows : (early_block + 1) * tick_rows], received
        )
        segment, cosv, sinv = pick(
            (segment_all[early_block], cos_all[early_block], sin_all[early_block]),
            (segment_all[late_block], cos_all[late_block], sin_all[late_block]),
        )
        inputs = block_rows.astype(jnp.float32)
        row_mean = jnp.mean(inputs, axis=1, keepdims=True)
        centred = inputs - row_mean
        forward_inv_scale = lax.rsqrt(jnp.mean(centred * centred, axis=1, keepdims=True) + EPSILON)
        forward_normed = centred * forward_inv_scale
        forward_h_attn = (forward_normed * ln_gains[0] + ln_shifts[0]).astype(jnp.bfloat16)
        forward_h_mlp = (forward_normed * ln_gains[1] + ln_shifts[1]).astype(jnp.bfloat16)
        joined_proj = (
            jnp.dot(forward_h_attn, joined_mat, preferred_element_type=jnp.float32) + joined_add
        )
        forward_block_len = block_rows.shape[0]
        forward_queries = rotate(
            joined_proj[:, :local_width].reshape(forward_block_len, local_heads, HD), cosv, sinv
        ).astype(jnp.bfloat16)
        forward_keys_rot = rotate(
            joined_proj[:, local_width : 2 * local_width].reshape(
                forward_block_len, local_heads, HD
            ),
            cosv,
            sinv,
        ).astype(jnp.bfloat16)
        forward_values = (
            joined_proj[:, 2 * local_width :]
            .reshape(forward_block_len, local_heads, HD)
            .astype(jnp.bfloat16)
        )
        blocked = (sub_blocks, MB, local_heads, HD)
        forward_scores = (
            jnp.einsum(
                "bqhd,bkhd->bhqk",
                forward_queries.reshape(blocked),
                forward_keys_rot.reshape(blocked),
                preferred_element_type=jnp.float32,
            )
            * score_scale
        )
        forward_scores = jnp.where(allowed_keys(segment)[:, None], forward_scores, MASKED)
        row_top = jnp.max(forward_scores, axis=3, keepdims=True)
        exponent = jnp.exp(forward_scores - row_top)
        row_total = jnp.sum(exponent, axis=3, keepdims=True)
        forward_log_total = row_top + jnp.log(row_total)
        weights_low = (exponent / row_total).astype(jnp.bfloat16)
        forward_context = jnp.einsum(
            "bhqk,bkhd->bqhd",
            weights_low,
            forward_values.reshape(blocked),
            preferred_element_type=jnp.float32,
        )
        forward_context = forward_context.reshape(forward_block_len, local_width).astype(
            jnp.bfloat16
        )
        forward_up_proj = (
            jnp.dot(forward_h_mlp, up_mat, preferred_element_type=jnp.float32) + up_add
        )
        forward_activated = exact_gelu(forward_up_proj).astype(jnp.bfloat16)
        partial_value = jnp.dot(forward_context, dense_mat, preferred_element_type=jnp.float32)
        partial_value = partial_value + jnp.dot(
            forward_activated, down_mat, preferred_element_type=jnp.float32
        )
        branches = tensor_scatter_sum(partial_value.astype(jnp.bfloat16))
        column_start = lax.axis_index("tensor") * quarter
        own_inputs = lax.dynamic_slice_in_dim(inputs, column_start, quarter, 1)
        own_bias = lax.dynamic_slice_in_dim(bias_sum, column_start, quarter, 0)
        result = own_inputs + branches + own_bias
        forward_stored = (
            forward_normed,
            forward_inv_scale,
            forward_h_attn,
            forward_h_mlp,
            forward_queries,
            forward_keys_rot,
            forward_values,
            forward_log_total,
            forward_context,
            forward_up_proj,
            forward_activated,
        )
        result, stored = (result, forward_stored)
        result_low = result.astype(jnp.bfloat16)
        tick_outputs.append(result_low)
        tick_stored.append((stored, segment, cosv, sinv))
        if section_tick < NMB:
            received = cross_gather(result_low, 0)
    section_rows = jnp.concatenate(
        [jnp.where(leading, tick_outputs[block], tick_outputs[block + 1]) for block in range(NMB)],
        axis=0,
    )
    section_out = section_rows[None]
    returned = jnp.zeros((tick_rows, model_width), jnp.bfloat16)
    tick_grads = []
    totals = None
    for section_tick in range(NMB + 1):
        own_block = min(section_tick, NMB - 1)
        late_tick = max(section_tick - 1, 0)
        upper_tick = min(section_tick + 1, NMB)
        from_output = output_grads[own_block * tick_rows : (own_block + 1) * tick_rows]
        if section_tick == NMB:
            from_output = jnp.zeros_like(from_output)
        grad_rows = jnp.where(leading, returned, from_output)
        stored, segment, cosv, sinv = pick(tick_stored[late_tick], tick_stored[upper_tick])
        (
            normed,
            inv_scale,
            h_attn,
            h_mlp,
            queries,
            keys_rot,
            values,
            log_total,
            context,
            up_proj,
            activated,
        ) = stored
        block_len = grad_rows.shape[0]
        grad_wide = grad_rows.astype(jnp.float32)
        column_sum = jnp.sum(grad_wide, axis=0)
        backward_grad_dense = contract_rows(context, grad_rows)
        backward_grad_down = contract_rows(activated, grad_rows)
        d_context = contract_cols(grad_rows, dense_mat).astype(jnp.bfloat16)
        d_act = contract_cols(grad_rows, down_mat)
        unused, slope_back = jax.vjp(exact_gelu, up_proj)
        d_up = slope_back(d_act)[0].astype(jnp.bfloat16)
        grad_up_add = jnp.sum(d_up.astype(jnp.float32), axis=0)
        backward_grad_up = contract_rows(h_mlp, d_up)
        d_hmlp = contract_cols(d_up, up_mat)
        blocked = (sub_blocks, MB, local_heads, HD)
        queries_b = queries.reshape(blocked)
        keys_b = keys_rot.reshape(blocked)
        scores = (
            jnp.einsum("bqhd,bkhd->bhqk", queries_b, keys_b, preferred_element_type=jnp.float32)
            * score_scale
        )
        scores = jnp.where(allowed_keys(segment)[:, None], scores, MASKED)
        weights_soft = jnp.exp(scores - log_total)
        d_context3 = d_context.reshape(blocked)
        d_values = jnp.einsum(
            "bhqk,bqhd->bkhd",
            weights_soft.astype(jnp.bfloat16),
            d_context3,
            preferred_element_type=jnp.float32,
        ).astype(jnp.bfloat16)
        d_weights = jnp.einsum(
            "bqhd,bkhd->bhqk", d_context3, values.reshape(blocked), preferred_element_type=jnp.float32
        )
        row_delta = jnp.sum(weights_soft * d_weights, axis=3, keepdims=True)
        d_scores = (weights_soft * (d_weights - row_delta)).astype(jnp.bfloat16)
        heads_shape = (block_len, local_heads, HD)
        d_queries = (
            jnp.einsum("bhqk,bkhd->bqhd", d_scores, keys_b, preferred_element_type=jnp.float32)
            * score_scale
        ).reshape(heads_shape)
        d_keys = (
            jnp.einsum("bhqk,bqhd->bkhd", d_scores, queries_b, preferred_element_type=jnp.float32)
            * score_scale
        ).reshape(heads_shape)
        d_queries = (
            rotate_back(d_queries, cosv, sinv).reshape(block_len, local_width).astype(jnp.bfloat16)
        )
        d_keys = (
            rotate_back(d_keys, cosv, sinv).reshape(block_len, local_width).astype(jnp.bfloat16)
        )
        d_joined = jnp.concatenate(
            [d_queries, d_keys, d_values.reshape(block_len, local_width)], axis=1
        )
        grad_joined_add = jnp.sum(d_joined.astype(jnp.float32), axis=0)
        backward_grad_joined = contract_rows(d_joined, h_attn)
        d_hattn = contract_cols(d_joined, joined_mat)
        grad_gains = jnp.concatenate(
            [jnp.sum(d_hattn * normed, axis=0), jnp.sum(d_hmlp * normed, axis=0)]
        )
        grad_shifts = jnp.concatenate([jnp.sum(d_hattn, axis=0), jnp.sum(d_hmlp, axis=0)])
        d_norm = tensor_scatter_sum(
            (d_hattn * ln_gains[0] + d_hmlp * ln_gains[1]).astype(jnp.bfloat16)
        )
        column_start = lax.axis_index("tensor") * quarter
        own_normed = lax.dynamic_slice_in_dim(normed, column_start, quarter, 1)
        own_grad = lax.dynamic_slice_in_dim(grad_wide, column_start, quarter, 1)
        row_stats = tensor_sum(
            jnp.concatenate(
                [
                    jnp.sum(d_norm, axis=1, keepdims=True),
                    jnp.sum(d_norm * own_normed, axis=1, keepdims=True),
                ],
                axis=1,
            )
        ) / model_width
        grad_input = own_grad + inv_scale * (
            d_norm - row_stats[:, 0:1] - own_normed * row_stats[:, 1:2]
        )
        small_terms = jnp.concatenate(
            [grad_gains, grad_shifts, column_sum, column_sum, grad_joined_add, grad_up_add]
        )
        terms = (
            backward_grad_joined[None],
            backward_grad_dense[None],
            backward_grad_up[None],
            backward_grad_down[None],
            small_terms[None],
        )
        grad_input, terms = (grad_input, terms)
        grad_low = grad_input.astype(jnp.bfloat16)
        tick_grads.append(grad_low)
        if totals is None:
            totals = terms
        else:
            totals = jax.tree.map(lambda older, newer: older + newer, totals, terms)
        if section_tick < NMB:
            returned = cross_gather(grad_low, 1)
    small_rows = totals[4][0]
    small_pad = (-small_rows.shape[0]) % model_width
    small_rows = jnp.pad(small_rows, (0, small_pad)).reshape(-1, model_width)
    pieces = (totals[0][0], totals[1][0], totals[2][0], totals[3][0], small_rows)
    slab = jnp.concatenate([piece.astype(jnp.bfloat16) for piece in pieces], axis=0)
    slab = lax.psum(slab, "dp")
    summed = []
    offset = 0
    for piece in pieces:
        summed.append(slab[offset : offset + piece.shape[0]].astype(jnp.float32))
        offset = offset + piece.shape[0]
    grad_rows_all = jnp.concatenate(
        [jnp.where(leading, tick_grads[block + 1], tick_grads[block]) for block in range(NMB)],
        axis=0,
    )
    input_grad = grad_rows_all[None]
    grad_joined = summed[0].T.reshape(1, model_width, 3, local_width)
    grad_dense = summed[1][None]
    grad_up = summed[2][None]
    grad_down = summed[3][None]
    small_sum = summed[4].reshape(-1)
    ln_sum = tensor_sum(small_sum[: 4 * model_width])
    grad_ln_gain = ln_sum[: 2 * model_width].reshape(1, 2, model_width)
    grad_ln_bias = ln_sum[2 * model_width :].reshape(1, 2, model_width)
    offset = 4 * model_width
    grad_output_bias = small_sum[offset : offset + 2 * model_width].reshape(1, 2, model_width)
    offset = offset + 2 * model_width
    grad_joined_bias = small_sum[offset : offset + 3 * local_width].reshape(1, 3, local_width)
    offset = offset + 3 * local_width
    grad_up_bias = small_sum[offset : offset + hidden_local].reshape(1, hidden_local)
    return (
        section_out,
        input_grad,
        grad_ln_gain,
        grad_ln_bias,
        grad_joined,
        grad_joined_bias,
        grad_dense,
        grad_up,
        grad_up_bias,
        grad_down,
        grad_output_bias,
    )


def solution(mesh):
    placed = (
        P("dp", "tensor"),
        P("dp", None),
        P("pipe", None, None),
        P("pipe", None, None),
        P("pipe", None, None, "tensor"),
        P("pipe", None, "tensor"),
        P("pipe", "tensor", None),
        P("pipe", None, "tensor"),
        P("pipe", "tensor"),
        P("pipe", "tensor", None),
        P("pipe", None, None),
        P("dp", "tensor"),
    )
    return jax.shard_map(
        per_device,
        mesh=mesh,
        in_specs=placed,
        out_specs=(
            P("pipe", "dp", "tensor"),
            P("pipe", "dp", "tensor"),
            P("pipe", None, None),
            P("pipe", None, None),
            P("pipe", None, None, "tensor"),
            P("pipe", None, "tensor"),
            P("pipe", "tensor", None),
            P("pipe", None, "tensor"),
            P("pipe", "tensor"),
            P("pipe", "tensor", None),
            P("pipe", None, None),
        ),
        check_vma=False,
    )
```
